32 devices in a mesh: dp: 8 (over y, x, core), seq: 4 (over z).
Axes of the slice: x: 2, y: 2, z: 4, core: 2. Of those that a mesh axis runs over, the one named last changes fastest.
Arguments:
- tokens: bfloat16 [32, 1024, 768], P('dp', 'seq'), may hold values from -6 to 6
- segment_ids: int32 [32, 1024], P('dp', 'seq'), may hold values from 0 to 1024, as said below
- valid_mask: int32 [32, 1024], P('dp', 'seq'), may hold values from 0 to 1, as said below
- cotangent: bfloat16 [32, 1024, 768], P('dp', 'seq'), may hold values from -6 to 6
- gain_one: bfloat16 [768], P(('dp', 'seq')), may hold values from 0.5 to 1.5
- gain_two: bfloat16 [768], P(('dp', 'seq')), may hold values from 0.5 to 1.5
- bias_table: bfloat16 [384], P(('dp', 'seq')), may hold values from -4 to 4
- qkv_weight: bfloat16 [768, 2304], P(('dp', 'seq')), may hold values from -0.109375 to 0.109375
- out_weight: bfloat16 [768, 768], P(('dp', 'seq')), may hold values from -1.75 to 1.75
- in_weight: bfloat16 [768, 3072], P(('dp', 'seq')), may hold values from -0.21875 to 0.21875
- back_weight: bfloat16 [3072, 768], P(('dp', 'seq')), may hold values from -0.109375 to 0.109375
Outputs:
- output: bfloat16 [32, 1024, 768], P('dp', 'seq')
- grad_input: bfloat16 [32, 1024, 768], P('dp', 'seq')
- grad_gain_one: float32 [768], P(('dp', 'seq'))
- grad_gain_two: float32 [768], P(('dp', 'seq'))
- grad_bias_table: float32 [384], P(('dp', 'seq'))
- grad_qkv_weight: float32 [768, 2304], P(('dp', 'seq'))
- grad_out_weight: float32 [768, 768], P(('dp', 'seq'))
- grad_in_weight: float32 [768, 3072], P(('dp', 'seq'))
- grad_back_weight: float32 [3072, 768], P(('dp', 'seq'))
The draws below stay inside these ranges and needn't reach their ends.
Inputs may be any that keep to these rules, and one draw needn't show every extreme that they name: `segment_ids`: ids never fall along a sequence; a run of equal ids is one document; every sequence ends in 1 to 256 padding positions, which carry the id 1024. `valid_mask`: 1 exactly where segment_ids is not 1024.
All inputs are finite; a program needn't handle non-finite values.
Results may differ from the reference program's by a relative error of at most 0.019.
Values may be sent and summed in bfloat16 or wider, within the bound.
A program may use at most 320 MiB of HBM per device.

```python
from functools import partial
import jax
import jax.numpy as jnp
from jax import lax

D = 768
HEADS = 12
HD = 64
FF = 3072
BUCKETS = 32
LEN = 1024
SEQS = 32


def layout(key):
    key_exponent = jax.random.fold_in(key, 11)
    key_extra = jax.random.fold_in(key, 12)
    key_padding = jax.random.fold_in(key, 13)
    doc_count = LEN // 4 + 1
    exponent = jax.random.randint(key_exponent, (SEQS, doc_count), 2, 11)
    base_len = jnp.left_shift(jnp.ones_like(exponent), exponent)
    extra_len = jax.random.randint(key_extra, (SEQS, doc_count), 0, 1 << 30) % base_len
    doc_ends = jnp.cumsum(base_len + extra_len, axis=1).astype(jnp.int32)
    places = jnp.arange(LEN, dtype=jnp.int32)
    seg_ids = jax.vmap(partial(jnp.searchsorted, side='right'), in_axes=(0, None))(doc_ends, places).astype(jnp.int32)
    pad_len = jax.random.randint(key_padding, (SEQS, 1), 1, LEN // 4 + 1)
    valid_rows = (places[None, :] < LEN - pad_len).astype(jnp.int32)
    seg_ids = jnp.where(valid_rows == 1, seg_ids, LEN).astype(jnp.int32)
    return (seg_ids, valid_rows)


def draw_segment_ids(key, part):
    return layout(key)[0]


def draw_valid_mask(key, part):
    return layout(key)[1]


def level_of(rng, dims, split, least, largest):
    loudness, own = 1.0, jax.random.fold_in(rng, 6)
    for dim, parts in split:
        steps = jnp.exp(jax.random.uniform(jax.random.fold_in(own, dim), (parts,), jnp.float32, least / len(split), largest / len(split)))
        loudness = loudness * jnp.repeat(steps, dims[dim] // parts).reshape([-1 if axis == dim else 1 for axis in range(len(dims))])
    return loudness


def scatter_about(key, shape, deviation, bound, cuts=(), kind=jnp.bfloat16):
    gain = level_of(key, shape, cuts, -0.22, 0.18) if cuts else 1.0
    array = jax.random.normal(key, shape, jnp.float32) * deviation * gain
    return jnp.minimum(jnp.maximum(array, -bound), bound).astype(kind)


def setup_inputs(seed: int = 0) -> dict:
    keys = jax.random.split(jax.random.key(seed), 12)
    tokens = scatter_about(keys[0], (SEQS, LEN, D), 1.0, 6.0, ((0, 8), (1, 4)))
    segment_ids = draw_segment_ids(jax.random.fold_in(keys[11], 71), 0)
    valid_mask = draw_valid_mask(jax.random.fold_in(keys[11], 71), 0)
    cotangent = scatter_about(keys[3], (SEQS, LEN, D), 1.0, 6.0, ((0, 8), (1, 4)))
    gain_one = jnp.clip(1.0 + 0.1 * jax.random.normal(keys[4], (D,), jnp.float32), 0.5, 1.5).astype(jnp.bfloat16)
    gain_two = jnp.clip(1.0 + 0.1 * jax.random.normal(keys[5], (D,), jnp.float32), 0.5, 1.5).astype(jnp.bfloat16)
    bias_table = scatter_about(keys[6], (BUCKETS * HEADS,), 1.0, 4.0, ((0, 32),))
    qkv_weight = scatter_about(keys[7], (D, 3 * D), (4 * D) ** -0.5, 0.109375, ((0, 32),))
    out_weight = scatter_about(keys[8], (D, D), (D // 64) ** -0.5, 1.75, ((0, 32),))
    in_weight = scatter_about(keys[9], (D, FF), D ** -0.5, 0.21875, ((0, 32),))
    back_weight = scatter_about(keys[10], (FF, D), FF ** -0.5, 0.109375, ((0, 32),))
    return dict(tokens=tokens, segment_ids=segment_ids, valid_mask=valid_mask, cotangent=cotangent, gain_one=gain_one, gain_two=gain_two, bias_table=bias_table, qkv_weight=qkv_weight, out_weight=out_weight, in_weight=in_weight, back_weight=back_weight)


EPS = 1e-06
NEGATIVE = -1e+30
TOP_PRECISION = lax.Precision.HIGHEST
bucket_limits = (12, 16, 23, 32, 46, 64, 91)

@jax.custom_vjp
def low(v):
    return lax.optimization_barrier(v.astype(jnp.bfloat16)).astype(jnp.float32)

@jax.custom_vjp
def low_back(v):
    return v

def low_keep(v):
    return (low(v), None)

def low_pass(kept, grad):
    return (grad,)

def back_keep(v):
    return (v, None)

def back_low(kept, grad):
    return (low(grad),)
low.defvjp(low_keep, low_pass)
low_back.defvjp(back_keep, back_low)

def bucket_of(relative):
    distance = jnp.abs(relative).astype(jnp.int32)
    counted = jnp.zeros(distance.shape, jnp.int32)
    for threshold in bucket_limits:
        counted = counted + (distance >= threshold).astype(jnp.int32)
    inside = jnp.where(distance < 8, distance, counted + 8).astype(jnp.int32)
    return (inside + 16 * (relative > 0).astype(jnp.int32)).astype(jnp.int32)

def rms_norm(values, gain_vec):
    return values * lax.rsqrt(lax.optimization_barrier(jnp.mean(values * values, axis=-1, keepdims=True)) + EPS) * gain_vec

def layer(inputs, seg_block, single_hot_vector, param_set):
    gain_first, gain_second, bias_matrix, qkv_full, out_full, in_full, back_full = param_set
    group_len = inputs.shape[0]
    normed = low(rms_norm(inputs, gain_first))
    projected = low_back(low(jnp.einsum('gtd,de->gte', normed, qkv_full, precision=TOP_PRECISION)))
    queries = projected[..., :D].reshape(group_len, LEN, HEADS, HD)
    keys_all = projected[..., D:2 * D].reshape(group_len, LEN, HEADS, HD)
    values_all = projected[..., 2 * D:].reshape(group_len, LEN, HEADS, HD)
    complete_bias = jnp.einsum('dto,dl->lto', single_hot_vector, bias_matrix, precision=TOP_PRECISION)
    scores = low_back(jnp.einsum('gqhd,gkhd->ghqk', queries, keys_all, precision=TOP_PRECISION) + complete_bias[None])
    allowed = (seg_block[:, :, None] == seg_block[:, None, :])[:, None]
    masked = jnp.where(allowed, scores, jnp.full(scores.shape, NEGATIVE, scores.dtype))
    row_peak = lax.optimization_barrier(jnp.max(masked, axis=-1, keepdims=True))
    shifted = jnp.exp(masked - row_peak)
    softmax_probabilities = shifted / lax.optimization_barrier(jnp.sum(shifted, axis=-1, keepdims=True))
    attn_mixed = jnp.einsum('ghqk,gkhd->gqhd', low(softmax_probabilities), values_all, precision=TOP_PRECISION)
    attn_mixed = low_back(low(attn_mixed.reshape(group_len, LEN, D)))
    middle = inputs + low_back(jnp.einsum('gtd,de->gte', attn_mixed, out_full, precision=TOP_PRECISION))
    second = low(rms_norm(middle, gain_second))
    pre = low_back(jnp.einsum('gtd,df->gtf', second, in_full, precision=TOP_PRECISION))
    hidden = low(jax.nn.gelu(pre, approximate=True))
    return middle + low_back(jnp.einsum('gtf,fd->gtd', hidden, back_full, precision=TOP_PRECISION))

def reference(tokens, segment_ids, valid_mask, cotangent, gain_one, gain_two, bias_table, qkv_weight, out_weight, in_weight, back_weight):
    places = jnp.arange(LEN, dtype=jnp.int32)
    buckets = bucket_of(places[None, :] - places[:, None])
    single_hot_vector = (buckets[None] == jnp.arange(BUCKETS, dtype=jnp.int32)[:, None, None]).astype(jnp.float32)
    param_set = (gain_one.astype(jnp.float32), gain_two.astype(jnp.float32), bias_table.astype(jnp.float32).reshape(BUCKETS, HEADS), qkv_weight.astype(jnp.float32), out_weight.astype(jnp.float32), in_weight.astype(jnp.float32), back_weight.astype(jnp.float32))
    group_count = SEQS // 4
    inputs_all = tokens.astype(jnp.float32).reshape(group_count, 4, LEN, D)
    seg_all = segment_ids.astype(jnp.int32).reshape(group_count, 4, LEN)
    cot_all = (cotangent.astype(jnp.float32) * valid_mask.astype(jnp.float32)[..., None]).reshape(group_count, 4, LEN, D)

    def one_group(totals, group_items):
        block_x, block_seg, block_cot = group_items

        def forward(inputs, params_in):
            return layer(inputs, block_seg, single_hot_vector, params_in)
        result, pullback = jax.vjp(forward, block_x, param_set)
        grad_x, grad_params = pullback(block_cot)
        totals = tuple((total + piece.astype(jnp.float32) for total, piece in zip(totals, grad_params)))
        return (totals, (result.astype(jnp.bfloat16), grad_x.astype(jnp.bfloat16)))
    zero_grads = tuple((jnp.zeros(item.shape, jnp.float32) for item in param_set))
    totals, (outputs, grad_rows) = lax.scan(one_group, zero_grads, (inputs_all, seg_all, cot_all))
    grad_first, grad_second, grad_grid, grad_qkv, grad_out, grad_in, grad_back = totals
    return (outputs.reshape(SEQS, LEN, D), grad_rows.reshape(SEQS, LEN, D), grad_first, grad_second, grad_grid.reshape(BUCKETS * HEADS), grad_qkv, grad_out, grad_in, grad_back)
```

```python
import functools

import jax
import jax.numpy as jnp
from jax import lax
from jax.experimental import pallas as pl
from jax.experimental.pallas import tpu as pltpu
from jax.sharding import PartitionSpec as P

HEADS = 12
HD = 64
BUCKETS = 32


EPS = 1e-06
NEGATIVE = -1e30
bucket_limits = (12, 16, 23, 32, 46, 64, 91)


def bucket_of(relative):
    distance = jnp.abs(relative)
    counted = jnp.zeros_like(distance)
    for threshold in bucket_limits:
        counted = counted + (distance >= threshold).astype(jnp.int32)
    inside = jnp.where(distance < 8, distance, 8 + counted)
    return inside + 16 * (relative > 0).astype(jnp.int32)


def rms_scale(values):
    return lax.rsqrt(jnp.mean(values * values, axis=-1, keepdims=True) + EPS)


def smooth_gate(values):
    return jax.nn.gelu(values, approximate=True)


def norm_backward(values, scale_inv, gain_vec, grad_normed):
    weighted = grad_normed * gain_vec
    grad_gain = jnp.sum(grad_normed * values * scale_inv, axis=0)
    cubed = scale_inv * scale_inv * scale_inv
    grad_values = scale_inv * weighted - values * cubed * jnp.mean(
        weighted * values, axis=-1, keepdims=True
    )
    return (grad_values, grad_gain)


def group_scores(query_part, key_part, seg_query, seg_key, complete_bias):
    scores = (
        jnp.einsum("gqhd,gkhd->ghqk", query_part, key_part, preferred_element_type=jnp.float32)
        + complete_bias[None]
    )
    allowed = (seg_query[:, :, None] == seg_key[:, None, :])[:, None]
    return jnp.where(allowed, scores, NEGATIVE)


def query_backward(items, complete_bias):
    query_part, key_part, value_part, seg_query, seg_key, log_total, grad_part = items
    scores = group_scores(query_part, key_part, seg_query, seg_key, complete_bias)
    softmax_probabilities = jnp.exp(scores - log_total)
    grad_probs = jnp.einsum(
        "gqhd,gkhd->ghqk", grad_part, value_part, preferred_element_type=jnp.float32
    )
    row_inner = jnp.sum(softmax_probabilities * grad_probs, axis=-1, keepdims=True)
    grad_scores = (softmax_probabilities * (grad_probs - row_inner)).astype(jnp.bfloat16)
    grad_query = jnp.einsum(
        "ghqk,gkhd->gqhd", grad_scores, key_part, preferred_element_type=jnp.float32
    ).astype(jnp.bfloat16)
    return (softmax_probabilities, grad_scores, grad_query, row_inner)


def general_shards(
    tokens,
    segment_ids,
    valid_mask,
    cotangent,
    gain_one,
    gain_two,
    bias_table,
    qkv_weight,
    out_weight,
    in_weight,
    back_weight,
):
    gathered = (
        lax.all_gather(gain_one, ("dp", "seq"), axis=0, tiled=True),
        lax.all_gather(gain_two, ("dp", "seq"), axis=0, tiled=True),
        lax.all_gather(bias_table, ("dp", "seq"), axis=0, tiled=True),
        lax.all_gather(qkv_weight, ("dp", "seq"), axis=0, tiled=True),
        lax.all_gather(out_weight, ("dp", "seq"), axis=0, tiled=True),
        lax.all_gather(in_weight, ("dp", "seq"), axis=0, tiled=True),
        lax.all_gather(back_weight, ("dp", "seq"), axis=0, tiled=True),
    )
    gain_first, gain_second, table_flat, qkv_full, out_full, in_full, back_full = gathered
    seq_count, block_len, model_width = tokens.shape
    seq_len = block_len * lax.axis_size("seq")
    row_count = seq_count * block_len
    group_size = seq_count
    while group_size % 2 == 0 and group_size // 2 * block_len >= 512:
        group_size = group_size // 2
    group_count = seq_count // group_size
    flat_x = tokens.reshape(row_count, model_width).astype(jnp.float32)
    first_scale = rms_scale(flat_x)
    first_gain = gain_first.astype(jnp.float32)
    first_normed = (flat_x * first_scale * first_gain).astype(jnp.bfloat16)
    projected = jnp.dot(first_normed, qkv_full, preferred_element_type=jnp.float32).astype(
        jnp.bfloat16
    )
    queries = projected[:, :model_width].reshape(group_count, group_size, block_len, HEADS, HD)
    local_keys = projected[:, model_width : 2 * model_width].reshape(
        seq_count, block_len, model_width
    )
    local_values = projected[:, 2 * model_width :].reshape(seq_count, block_len, model_width)
    all_keys, all_values, all_segments = (
        lax.all_gather(local_keys, "seq", axis=1, tiled=True),
        lax.all_gather(local_values, "seq", axis=1, tiled=True),
        lax.all_gather(segment_ids, "seq", axis=1, tiled=True),
    )
    key_groups = all_keys.reshape(group_count, group_size, seq_len, HEADS, HD)
    value_groups = all_values.reshape(group_count, group_size, seq_len, HEADS, HD)
    segkey_groups = all_segments.reshape(group_count, group_size, seq_len)
    segquery_groups = segment_ids.reshape(group_count, group_size, block_len)
    offset = lax.axis_index("seq") * block_len
    query_places = offset + jnp.arange(block_len, dtype=jnp.int32)
    key_places = jnp.arange(seq_len, dtype=jnp.int32)
    buckets = bucket_of(key_places[None, :] - query_places[:, None])
    single_hot_vector = (
        buckets[None] == jnp.arange(BUCKETS, dtype=jnp.int32)[:, None, None]
    ).astype(jnp.bfloat16)
    bias_matrix = table_flat.reshape(BUCKETS, HEADS)
    complete_bias = jnp.einsum(
        "dto,dl->lto", single_hot_vector, bias_matrix, preferred_element_type=jnp.float32
    )

    def attend(group_items):
        query_part, key_part, value_part, seg_query, seg_key = group_items
        scores = group_scores(query_part, key_part, seg_query, seg_key, complete_bias)
        row_peak = jnp.max(scores, axis=-1, keepdims=True)
        shifted = jnp.exp(scores - row_peak)
        row_total = jnp.sum(shifted, axis=-1, keepdims=True)
        softmax_probabilities = (shifted / row_total).astype(jnp.bfloat16)
        attn_part = jnp.einsum(
            "ghqk,gkhd->gqhd", softmax_probabilities, value_part, preferred_element_type=jnp.float32
        )
        return (attn_part.astype(jnp.bfloat16), row_peak + jnp.log(row_total))

    attn_mixed, log_totals = lax.map(
        attend, (queries, key_groups, value_groups, segquery_groups, segkey_groups)
    )
    mixed_flat = attn_mixed.reshape(row_count, model_width)
    middle = flat_x + jnp.dot(mixed_flat, out_full, preferred_element_type=jnp.float32)
    second_scale = rms_scale(middle)
    second_gain = gain_second.astype(jnp.float32)
    second_normed = (middle * second_scale * second_gain).astype(jnp.bfloat16)
    hidden_pre = jnp.dot(second_normed, in_full, preferred_element_type=jnp.float32)
    hidden_float, gate_pullback = jax.vjp(smooth_gate, hidden_pre)
    hidden = hidden_float.astype(jnp.bfloat16)
    result = middle + jnp.dot(hidden, back_full, preferred_element_type=jnp.float32)
    output = result.astype(jnp.bfloat16).reshape(seq_count, block_len, model_width)
    grad_result = cotangent.reshape(row_count, model_width).astype(
        jnp.float32
    ) * valid_mask.reshape(row_count, 1).astype(jnp.float32)
    grad_branch = grad_result.astype(jnp.bfloat16)
    grad_back = jnp.einsum("tf,td->fd", hidden, grad_branch, preferred_element_type=jnp.float32)
    grad_hidden = jnp.einsum(
        "td,fd->tf", grad_branch, back_full, preferred_element_type=jnp.float32
    )
    grad_pre = gate_pullback(grad_hidden)[0].astype(jnp.bfloat16)
    grad_in = jnp.einsum("td,tf->df", second_normed, grad_pre, preferred_element_type=jnp.float32)
    grad_second_normed = jnp.einsum(
        "tf,df->td", grad_pre, in_full, preferred_element_type=jnp.float32
    )
    grad_middle_norm, grad_gain_second = norm_backward(
        middle, second_scale, second_gain, grad_second_normed
    )
    grad_middle = grad_result + grad_middle_norm
    grad_attn = grad_middle.astype(jnp.bfloat16)
    grad_out = jnp.einsum("td,te->de", mixed_flat, grad_attn, preferred_element_type=jnp.float32)
    grad_mixed = jnp.einsum(
        "te,de->td", grad_attn, out_full, preferred_element_type=jnp.float32
    ).astype(jnp.bfloat16)
    grad_mixed_groups = grad_mixed.reshape(group_count, group_size, block_len, HEADS, HD)
    backward_entries = (
        queries,
        key_groups,
        value_groups,
        segquery_groups,
        segkey_groups,
        log_totals,
        grad_mixed_groups,
    )
    bias_zero = jnp.zeros((HEADS, block_len, seq_len), jnp.float32)

    def full_backward(bias_total_sum, group_items):
        softmax_probabilities, grad_scores, grad_query, row_inner = query_backward(
            group_items, complete_bias
        )
        query_part = group_items[0]
        grad_part = group_items[6]
        key_gradient = jnp.einsum(
            "ghqk,gqhd->gkhd", grad_scores, query_part, preferred_element_type=jnp.float32
        )
        grad_value = jnp.einsum(
            "ghqk,gqhd->gkhd",
            softmax_probabilities.astype(jnp.bfloat16),
            grad_part,
            preferred_element_type=jnp.float32,
        )
        bias_total_sum = bias_total_sum + jnp.sum(grad_scores.astype(jnp.float32), axis=0)
        return (bias_total_sum, (grad_query, key_gradient, grad_value))

    bias_total_sum, (grad_queries, grad_keys, grad_values) = lax.scan(
        full_backward, bias_zero, backward_entries
    )
    key_terms = grad_keys.reshape(seq_count, seq_len, model_width)
    value_terms = grad_values.reshape(seq_count, seq_len, model_width)
    key_sum, value_sum = (
        lax.psum_scatter(
            key_terms.astype(jnp.bfloat16), "seq", scatter_dimension=1, tiled=True
        ).astype(jnp.float32),
        lax.psum_scatter(
            value_terms.astype(jnp.bfloat16), "seq", scatter_dimension=1, tiled=True
        ).astype(jnp.float32),
    )
    key_low = key_sum.astype(jnp.bfloat16)
    value_low = value_sum.astype(jnp.bfloat16)
    grad_projected = jnp.concatenate(
        [
            grad_queries.reshape(row_count, model_width),
            key_low.reshape(row_count, model_width),
            value_low.reshape(row_count, model_width),
        ],
        axis=1,
    )
    grad_qkv = jnp.einsum(
        "td,te->de", first_normed, grad_projected, preferred_element_type=jnp.float32
    )
    grad_first_normed = jnp.einsum(
        "te,de->td", grad_projected, qkv_full, preferred_element_type=jnp.float32
    )
    grad_x_norm, grad_gain_first = norm_backward(flat_x, first_scale, first_gain, grad_first_normed)
    grad_tokens = (
        (grad_middle + grad_x_norm).astype(jnp.bfloat16).reshape(seq_count, block_len, model_width)
    )
    grad_table = jnp.einsum(
        "fuy,suy->fs",
        single_hot_vector.astype(jnp.float32),
        bias_total_sum,
        precision=lax.Precision.HIGHEST,
    ).reshape(BUCKETS * HEADS)
    owned = (
        lax.psum_scatter(grad_gain_first, ("dp", "seq"), scatter_dimension=0, tiled=True),
        lax.psum_scatter(grad_gain_second, ("dp", "seq"), scatter_dimension=0, tiled=True),
        lax.psum_scatter(grad_table, ("dp", "seq"), scatter_dimension=0, tiled=True),
        lax.psum_scatter(grad_qkv, ("dp", "seq"), scatter_dimension=0, tiled=True),
        lax.psum_scatter(grad_out, ("dp", "seq"), scatter_dimension=0, tiled=True),
        lax.psum_scatter(grad_in, ("dp", "seq"), scatter_dimension=0, tiled=True),
        lax.psum_scatter(grad_back, ("dp", "seq"), scatter_dimension=0, tiled=True),
    )
    owned_gain_one, owned_gain_two, owned_table, owned_qkv, owned_out, owned_in, owned_back = owned
    return (
        output,
        grad_tokens,
        owned_gain_one,
        owned_gain_two,
        owned_table,
        owned_qkv,
        owned_out,
        owned_in,
        owned_back,
    )


MESH = pl.DeviceIdType.MESH

def flip(i, bit):
    return i + bit - 2 * bit * ((i // bit) % 2)

def gather_kernel(items, *refs):
    n_arr = 5
    tok, seg = refs[0], refs[1]
    shards = refs[2:2 + n_arr]
    xf, sf = refs[2 + n_arr], refs[3 + n_arr]
    full = refs[4 + n_arr:4 + 2 * n_arr]
    loc_sem, t_send, t_recv, s_send, s_recv, z_send, z_recv, h_send, h_recv = refs[4 + 2 * n_arr:]
    dp, z = lax.axis_index("dp"), lax.axis_index("seq")
    n_z = 4
    peers = [(dp, lax.rem(z + s, n_z)) for s in range(1, n_z)] + [(flip(dp, b), z) for b in (1, 2, 4)]
    barrier = pltpu.get_barrier_semaphore()
    for p in peers:
        pl.semaphore_signal(barrier, inc=1, device_id=p, device_id_type=MESH)
    pl.semaphore_wait(barrier, len(peers))

    def block(it, d, zz):
        return full[items[it][0]].at[d * n_z + zz]

    def own(it):
        return shards[items[it][0]]

    n_it = len(items)
    def z_copy(it, way, step):
        src_z = z - step if way == 0 else z + step
        src = own(it) if step == 0 else block(it, dp, src_z)
        return pltpu.make_async_remote_copy(
            src_ref=src, dst_ref=block(it, dp, src_z), send_sem=z_send.at[it, way, step],
            recv_sem=z_recv.at[it, way, step], device_id=(dp, z + 1 if way == 0 else z - 1), device_id_type=MESH)

    def z_wait(it, way, step):
        src_z = z - 1 - step if way == 0 else z + 1 + step
        blk = block(it, dp, src_z)
        pltpu.make_async_remote_copy(src_ref=blk, dst_ref=blk, send_sem=z_send.at[it, way, step],
            recv_sem=z_recv.at[it, way, step], device_id=(dp, z), device_id_type=MESH).wait_recv()

    def can_send(way, step):
        return (z >= step) & (z <= n_z - 2) if way == 0 else (z + step <= n_z - 1) & (z >= 1)

    def can_recv(way, step):
        return z >= step + 1 if way == 0 else z + 1 + step <= n_z - 1

    def z_start(it, step):
        for way in (0, 1):
            @pl.when(can_send(way, step))
            def _():
                z_copy(it, way, step).start()

    def z_recv_all(it, step):
        for way in (0, 1):
            @pl.when(can_recv(way, step))
            def _():
                z_wait(it, way, step)

    def hops(it):
        b1, b2 = items[it][1:]
        return [(0, b1), (0, b2), (b1, b2), (0, 1), (b1, 1), (b2, 1), (b1 + b2, 1)]

    def flips(d, mask):
        for b in (1, 2, 4):
            if mask & b:
                d = flip(d, b)
        return d

    def hop(it, slot, zz):
        mask, to = hops(it)[slot]
        blk = block(it, flips(dp, mask), zz)
        return pltpu.make_async_remote_copy(src_ref=blk, dst_ref=blk, send_sem=h_send.at[it, slot, zz],
            recv_sem=h_recv.at[it, slot, zz], device_id=(flip(dp, to), z), device_id_type=MESH)

    def hop_wait(it, slot, zz):
        mask, to = hops(it)[slot]
        blk = block(it, flips(dp, mask ^ to), zz)
        pltpu.make_async_remote_copy(src_ref=blk, dst_ref=blk, send_sem=h_send.at[it, slot, zz],
            recv_sem=h_recv.at[it, slot, zz], device_id=(dp, z), device_id_type=MESH).wait_recv()

    def own_hop(it, slot):
        to = hops(it)[slot][1]
        return pltpu.make_async_remote_copy(src_ref=own(it), dst_ref=block(it, dp, z), send_sem=h_send.at[it, slot, z],
            recv_sem=h_recv.at[it, slot, z], device_id=(flip(dp, to), z), device_id_type=MESH)

    def tok_copy(s):
        to = lax.rem(z + s, n_z)
        return [pltpu.make_async_remote_copy(src_ref=a.at[to], dst_ref=f.at[z], send_sem=ss.at[s - 1], recv_sem=rs.at[s - 1],
                device_id=(dp, to), device_id_type=MESH) for a, f, ss, rs in ((tok, xf, t_send, t_recv), (seg, sf, s_send, s_recv))]

    def tok_wait(s):
        frm = lax.rem(z + n_z - s, n_z)
        for f, ss, rs in ((xf, t_send, t_recv), (sf, s_send, s_recv)):
            pltpu.make_async_remote_copy(src_ref=f.at[frm], dst_ref=f.at[frm], send_sem=ss.at[s - 1], recv_sem=rs.at[s - 1],
                device_id=(dp, z), device_id_type=MESH).wait_recv()

    for it in range(n_it):
        z_start(it, 0)
        for slot in (0, 1, 3):
            own_hop(it, slot).start()
    locs = []
    for it in range(n_it):
        locs.append(pltpu.make_async_copy(own(it), block(it, dp, z), loc_sem.at[it]))
    locs.append(pltpu.make_async_copy(tok.at[z], xf.at[z], loc_sem.at[n_it]))
    locs.append(pltpu.make_async_copy(seg.at[z], sf.at[z], loc_sem.at[n_it + 1]))
    for c in locs:
        c.start()

    def forward(it, zz):
        hop_wait(it, 0, zz)
        hop(it, 2, zz).start()
        hop(it, 4, zz).start()
        hop_wait(it, 1, zz)
        hop(it, 5, zz).start()

    def arrivals(step):
        return [(can_recv(0, step), 0, z - 1 - step), (can_recv(1, step), 1, z + 1 + step)]

    for step in range(n_z):
        if step < n_z - 1:
            for it in range(n_it):
                for ok, way, zz in arrivals(step):
                    @pl.when(ok)
                    def _():
                        z_wait(it, way, step)
                        if step < n_z - 2:
                            @pl.when(can_send(way, step + 1))
                            def _():
                                z_copy(it, way, step + 1).start()
                        for slot in (0, 1, 3):
                            hop(it, slot, zz).start()
        if step == 1:
            for s in range(1, n_z):
                for c in tok_copy(s):
                    c.start()
        for it in range(n_it):
            if step == 0:
                forward(it, z)
            else:
                for ok, way, zz in arrivals(step - 1):
                    @pl.when(ok)
                    def _():
                        forward(it, zz)
    for zz in range(n_z):
        for it in range(n_it):
            hop_wait(it, 2, zz)
            hop(it, 6, zz).start()
    for s in range(1, n_z):
        tok_wait(s)
    for zz in range(n_z):
        for it in range(n_it):
            for slot in (3, 4, 5, 6):
                hop_wait(it, slot, zz)
    for c in locs:
        c.wait()
    for it in range(n_it):
        for step in range(n_z - 1):
            for way in (0, 1):
                @pl.when(can_send(way, step))
                def _():
                    z_copy(it, way, step).wait_send()
        for zz in range(n_z):
            for slot in range(7):
                hop(it, slot, zz).wait_send()
    for s in range(1, n_z):
        for c in tok_copy(s):
            c.wait_send()

def gather(tokens, seg, shards, items, collective_id=0):
    n_it = len(items)
    D = pltpu.SemaphoreType.DMA
    out_shape = [jax.ShapeDtypeStruct(tokens.shape, tokens.dtype), jax.ShapeDtypeStruct(seg.shape, seg.dtype)]
    out_shape += [jax.ShapeDtypeStruct((32, *s.shape), s.dtype) for s in shards]
    anyspec = pl.BlockSpec(memory_space=pltpu.HBM)
    return pl.pallas_call(
        functools.partial(gather_kernel, items),
        out_shape=out_shape,
        in_specs=[pl.BlockSpec(memory_space=pltpu.VMEM)] * (2 + len(shards)),
        out_specs=[anyspec] * len(out_shape),
        scratch_shapes=[D((n_it + 2,)), D((3,)), D((3,)), D((3,)), D((3,)), D((n_it, 2, 3)), D((n_it, 2, 3)), D((n_it, 7, 4)), D((n_it, 7, 4))],
        compiler_params=pltpu.CompilerParams(collective_id=collective_id, has_side_effects=True),
    )(tokens, seg, *shards)


LOG2E = 1.4426950408889634
BIG = -1e30
F32 = jnp.float32
BF = jnp.bfloat16

def extras(seg):
    L = seg.shape[0]
    nb = L.bit_length()
    nblk = L // 128
    lane = jnp.arange(128)[None, :] % 64
    row_blk = (jnp.arange(L) // 128)[:, None]
    b = lane - (nblk + 3)
    inb = (b >= 0) & (b < 2 * nb)
    bit = (seg[:, None] >> (jnp.clip(b, 0, 2 * nb - 1) // 2)) & 1
    flip = b % 2
    u = jnp.where(inb, (bit ^ flip), 0).astype(BF)
    w = jnp.where(inb & ((bit ^ flip) == 0), BIG, 0.0)
    onehot = (lane < nblk) & (lane == row_blk)
    ones = (lane >= nblk) & (lane < nblk + 3)
    exk = (w + (onehot | ones)).astype(BF)
    farl = ((lane < nblk) & (lane <= row_blk - 2)).astype(BF)
    farr = ((lane < nblk) & (lane >= row_blk + 2)).astype(BF)
    return u, exk, farl, farr

def strips(table):
    a = jnp.arange(128)[:, None]; c = jnp.arange(384)[None, :]
    bq = bucket_of(c - 128 - a)
    bk = bucket_of(a + 128 - c)
    def look(bk_):
        oh = (bk_[None] == jnp.arange(32)[:, None, None]).astype(BF)
        return jnp.einsum('bac,bh->hac', oh, table.astype(BF), preferred_element_type=F32)
    return look(bq), look(bk)

def fwd_kernel(nblk, bl_ref, q_ref, k_ref, v_ref, exq_ref, exk_ref, fl_ref, fr_ref, strip_ref, o_ref, qa_ref):
    L = q_ref.shape[0]
    hp = pl.program_id(0)
    lane = lax.broadcasted_iota(jnp.int32, (L, 128), 1)
    QB = 256
    outs = []
    for h in range(2):
        sel = (lane < 64) if h == 0 else (lane >= 64)
        bl = bl_ref[hp * 2 + h, 0].astype(BF); br = bl_ref[hp * 2 + h, 1].astype(BF)
        qa = jnp.where(sel, q_ref[...], exq_ref[...] + fl_ref[...] * bl + fr_ref[...] * br)
        ka = jnp.where(sel, k_ref[...], exk_ref[...])
        va = jnp.where(sel, v_ref[...], jnp.ones((L, 128), BF))
        lane_l = 64 * (1 - h)
        for blk in range(L // QB):
            r0 = blk * QB
            qb = qa[r0:r0 + QB]
            s = lax.dot_general(qb, ka, (((1,), (1,)), ((), ())), preferred_element_type=F32)
            rows = []
            for sub in range(QB // 128):
                I = blk * (QB // 128) + sub
                lo = max(I - 1, 0); hi = min(I + 1, nblk - 1)
                srow = s[sub * 128:(sub + 1) * 128]
                parts = []
                if lo > 0: parts.append(srow[:, :lo * 128])
                parts.append(srow[:, lo * 128:(hi + 1) * 128] + strip_ref[h, :, (lo - I + 1) * 128:(hi - I + 2) * 128])
                if hi < nblk - 1: parts.append(srow[:, (hi + 1) * 128:])
                rows.append(jnp.concatenate(parts, axis=1))
            s = jnp.concatenate(rows, axis=0)
            m = jnp.max(s, axis=1, keepdims=True)
            p = jnp.exp2((s - m) * LOG2E).astype(BF)
            o = jnp.dot(p, va, preferred_element_type=F32)
            l = o[:, lane_l:lane_l + 1]
            outs.append(o / l)
            lse = m + jnp.log(l)
            hi_ = (-lse).astype(BF); rest = -lse - hi_.astype(F32)
            mid = rest.astype(BF); low = (rest - mid.astype(F32)).astype(BF)
            base = 64 * (1 - h) + nblk
            ln = lane[:QB]
            qx = jnp.where(ln == base, hi_, jnp.where(ln == base + 1, mid, jnp.where(ln == base + 2, low, qb)))
            qa_ref[h, r0:r0 + QB, :] = qx
    n = L // QB
    for blk in range(n):
        o_ref[blk * QB:(blk + 1) * QB, :] = jnp.where(lane[:QB] < 64, outs[blk], outs[n + blk]).astype(BF)

def attn_fwd(qkv, ex, strip, far, interpret=False):
    L, W = qkv.shape
    D = W // 3
    H = D // HD
    npair = H // 2
    nblk = L // 128
    exq, exk, fl, fr = ex
    full = lambda: pl.BlockSpec((L, 128), lambda i: (0, 0))
    return pl.pallas_call(
        functools.partial(fwd_kernel, nblk),
        grid=(npair,),
        in_specs=[pl.BlockSpec(memory_space=pltpu.SMEM),
                  pl.BlockSpec((L, 128), lambda i: (0, i)),
                  pl.BlockSpec((L, 128), lambda i: (0, npair + i)),
                  pl.BlockSpec((L, 128), lambda i: (0, 2 * npair + i)),
                  full(), full(), full(), full(),
                  pl.BlockSpec((2, 128, 384), lambda i: (i, 0, 0))],
        out_specs=[pl.BlockSpec((L, 128), lambda i: (0, i)), pl.BlockSpec((2, L, 128), lambda i: (i, 0, 0))],
        out_shape=[jax.ShapeDtypeStruct((L, D), BF), jax.ShapeDtypeStruct((H, L, 128), BF)],
        compiler_params=pltpu.CompilerParams(vmem_limit_bytes=48 << 20),
        cost_estimate=pl.CostEstimate(flops=4 * L * L * D * 4, bytes_accessed=L * W * 4, transcendentals=L * L * H),
    )(far, qkv, qkv, qkv, exq, exk, fl, fr, strip)

def bwd_kernel(nblk, qa_ref, k_ref, v_ref, do_ref, o_ref, exk_ref, strip_ref,
               dq_ref, dk_ref, dv_ref, near_ref, far_ref):
    L = k_ref.shape[0]
    lane = lax.broadcasted_iota(jnp.int32, (L, 128), 1)
    KB = 256
    nsub = KB // 128
    prod = do_ref[...].astype(F32) * o_ref[...].astype(F32)
    dqs = []; dks = []; dvs = []
    for h in range(2):
        sel = (lane < 64) if h == 0 else (lane >= 64)
        other = 64 * (1 - h)
        qa = qa_ref[h]
        ka = jnp.where(sel, k_ref[...], exk_ref[...])
        va = jnp.where(sel, v_ref[...], ((lane >= other + nblk) & (lane < other + nblk + 3)).astype(BF))
        delta = -jnp.sum(jnp.where(sel, prod, 0.0), axis=1, keepdims=True)
        hi_ = delta.astype(BF); rest = delta - hi_.astype(F32)
        mid = rest.astype(BF); low = (rest - mid.astype(F32)).astype(BF)
        base = other + nblk
        doa = jnp.where(sel, do_ref[...], jnp.where(lane == base, hi_, jnp.where(lane == base + 1, mid, jnp.where(lane == base + 2, low, jnp.zeros((L, 128), BF)))))
        near = jnp.zeros((128, 384), F32)
        dqt = jnp.zeros((128, L), F32)
        for kb in range(L // KB):
            r0 = kb * KB
            kab = ka[r0:r0 + KB]
            s = lax.dot_general(kab, qa, (((1,), (1,)), ((), ())), preferred_element_type=F32)
            dp = lax.dot_general(va[r0:r0 + KB], doa, (((1,), (1,)), ((), ())), preferred_element_type=F32)
            prow = []; dsrow = []
            for sub in range(nsub):
                J = kb * nsub + sub
                lo = max(J - 1, 0); hi = min(J + 1, nblk - 1)
                srow = s[sub * 128:(sub + 1) * 128]
                parts = []
                if lo > 0: parts.append(srow[:, :lo * 128])
                parts.append(srow[:, lo * 128:(hi + 1) * 128] + strip_ref[h, :, (lo - J + 1) * 128:(hi - J + 2) * 128])
                if hi < nblk - 1: parts.append(srow[:, (hi + 1) * 128:])
                srow = jnp.concatenate(parts, axis=1)
                p = jnp.exp2(srow * LOG2E)
                ds = p * dp[sub * 128:(sub + 1) * 128]
                nr = ds[:, lo * 128:(hi + 1) * 128]
                if lo > J - 1: nr = jnp.concatenate([jnp.zeros((128, 128), F32), nr], axis=1)
                if hi < J + 1: nr = jnp.concatenate([nr, jnp.zeros((128, 128), F32)], axis=1)
                near = near + nr
                prow.append(p.astype(BF)); dsrow.append(ds.astype(BF))
            pb = jnp.concatenate(prow, axis=0); dsb = jnp.concatenate(dsrow, axis=0)
            dvs.append(jnp.dot(pb, doa, preferred_element_type=F32))
            dks.append(jnp.dot(dsb, qa, preferred_element_type=F32))
            dqt = dqt + lax.dot_general(kab, dsb, (((0,), (0,)), ((), ())), preferred_element_type=F32)
        near_ref[h] = near
        far_ref[h] = dqt[other:other + 8]
        dqs.append(dqt[64 * h:64 * h + 64])
    n = L // KB
    first = lane[:KB] < 64
    for kb in range(n):
        dk_ref[kb * KB:(kb + 1) * KB, :] = jnp.where(first, dks[kb], dks[n + kb]).astype(BF)
        dv_ref[kb * KB:(kb + 1) * KB, :] = jnp.where(first, dvs[kb], dvs[n + kb]).astype(BF)
    dq_ref[...] = jnp.concatenate(dqs, axis=0).T.astype(BF)

def attn_bwd(qa, qkv, do, o, exk, stripT):
    L, W = qkv.shape
    D = W // 3
    H = D // HD
    npair = H // 2
    nblk = L // 128
    col = lambda off: pl.BlockSpec((L, 128), lambda i: (0, off + i))
    return pl.pallas_call(
        functools.partial(bwd_kernel, nblk),
        grid=(npair,),
        in_specs=[pl.BlockSpec((2, L, 128), lambda i: (i, 0, 0)), col(npair), col(2 * npair), col(0), col(0),
                  pl.BlockSpec((L, 128), lambda i: (0, 0)), pl.BlockSpec((2, 128, 384), lambda i: (i, 0, 0))],
        out_specs=[col(0), col(0), col(0), pl.BlockSpec((2, 128, 384), lambda i: (i, 0, 0)), pl.BlockSpec((2, 8, L), lambda i: (i, 0, 0))],
        out_shape=[jax.ShapeDtypeStruct((L, D), BF)] * 3 + [jax.ShapeDtypeStruct((H, 128, 384), F32), jax.ShapeDtypeStruct((H, 8, L), F32)],
        compiler_params=pltpu.CompilerParams(vmem_limit_bytes=48 << 20),
        cost_estimate=pl.CostEstimate(flops=10 * L * L * D * 4, bytes_accessed=L * W * 6, transcendentals=L * L * H),
    )(qa, qkv, qkv, do, o, exk, stripT)


def fits(mesh):
    return mesh.shape["dp"] == 8 and mesh.shape["seq"] == 4


ITEMS = ((0, 4, 2), (4, 2, 4), (1, 2, 4), (2, 4, 2), (3, 2, 4))


def fast_shards(
    tokens,
    segment_ids,
    valid_mask,
    cotangent,
    gain_one,
    gain_two,
    bias_table,
    qkv_weight,
    out_weight,
    in_weight,
    back_weight,
):
    n_z = lax.axis_size("seq")
    seq_count, block_len, width = tokens.shape
    seq_len = n_z * block_len
    n_dev = n_z * lax.axis_size("dp")
    g_rows, t_rows = gain_one.shape[0], bias_table.shape[0]
    small = jnp.concatenate([gain_one, gain_two, bias_table])
    small = jnp.pad(small[None], ((0, 7), (0, 128 - small.shape[0])))
    grad_local = cotangent * valid_mask[..., None].astype(BF)
    x4, seg4, qkv_full, out_full, in_full, back_full, small_full = gather(
        tokens,
        segment_ids.reshape(seq_count, 1, block_len),
        (qkv_weight, out_weight, in_weight, back_weight, small),
        ITEMS,
    )
    qkv_full = qkv_full.reshape(width, 3 * width)
    out_full = out_full.reshape(width, width)
    in_full = in_full.reshape(width, -1)
    back_full = back_full.reshape(-1, width)
    small_full = small_full[:, 0]
    gain_first = small_full[:, :g_rows].reshape(1, width).astype(F32)
    gain_second = small_full[:, g_rows : 2 * g_rows].reshape(1, width).astype(F32)
    table = small_full[:, 2 * g_rows : 2 * g_rows + t_rows].reshape(BUCKETS, HEADS)
    grad_local, x4 = lax.optimization_barrier((grad_local, x4))
    g_low = lax.all_to_all(grad_local, "seq", 0, 1, tiled=True).reshape(seq_len, width)
    flat_x = x4.reshape(seq_len, width).astype(F32)
    seg = seg4.reshape(seq_len)
    exq, exk, far_left, far_right = extras(seg)
    strip, strip_t = strips(table.astype(F32))
    far = jnp.stack([table[BUCKETS // 2 - 1], table[BUCKETS - 1]], axis=1).astype(F32)
    first_scale = rms_scale(flat_x)
    first_normed = (flat_x * first_scale * gain_first).astype(BF)
    projected = jnp.dot(first_normed, qkv_full, preferred_element_type=F32).astype(BF)
    mixed, q_aug = attn_fwd(projected, (exq, exk, far_left, far_right), strip, far)
    middle = flat_x + jnp.dot(mixed, out_full, preferred_element_type=F32)
    second_scale = rms_scale(middle)
    second_normed = (middle * second_scale * gain_second).astype(BF)
    hidden_pre = jnp.dot(second_normed, in_full, preferred_element_type=F32)
    hidden_float, gate_pullback = jax.vjp(smooth_gate, hidden_pre)
    hidden = hidden_float.astype(BF)
    result = middle + jnp.dot(hidden, back_full, preferred_element_type=F32)
    output = lax.all_to_all(result.astype(BF).reshape(1, seq_len, width), "seq", 1, 0, tiled=True)
    grad_back = jnp.einsum("tf,td->fd", hidden, g_low, preferred_element_type=F32)
    grad_hidden = jnp.einsum("td,fd->tf", g_low, back_full, preferred_element_type=F32)
    grad_pre = gate_pullback(grad_hidden)[0].astype(BF)
    grad_in = jnp.einsum("td,tf->df", second_normed, grad_pre, preferred_element_type=F32)
    grad_second_normed = jnp.einsum("tf,df->td", grad_pre, in_full, preferred_element_type=F32)
    grad_middle_norm, grad_gain_second = norm_backward(
        middle, second_scale, gain_second, grad_second_normed
    )
    grad_middle = g_low.astype(F32) + grad_middle_norm
    grad_attn = grad_middle.astype(BF)
    grad_out = jnp.einsum("td,te->de", mixed, grad_attn, preferred_element_type=F32)
    grad_mixed = jnp.einsum("te,de->td", grad_attn, out_full, preferred_element_type=F32).astype(BF)
    dq, dk, dv, near, far_sums = attn_bwd(q_aug, projected, grad_mixed, mixed, exk, strip_t)
    grad_projected = jnp.concatenate([dq, dk, dv], axis=1)
    grad_qkv = jnp.einsum("td,te->de", first_normed, grad_projected, preferred_element_type=F32)
    grad_first_normed = jnp.einsum("te,de->td", grad_projected, qkv_full, preferred_element_type=F32)
    grad_x_norm, grad_gain_first = norm_backward(flat_x, first_scale, gain_first, grad_first_normed)
    grad_tokens = lax.all_to_all(
        (grad_middle + grad_x_norm).astype(BF).reshape(1, seq_len, width), "seq", 1, 0, tiled=True
    )
    near_bucket = bucket_of(jnp.arange(128)[:, None] + 128 - jnp.arange(384)[None, :])
    near_hot = (near_bucket[None] == jnp.arange(BUCKETS)[:, None, None]).astype(F32)
    grad_table = jnp.einsum("bac,hac->bh", near_hot, near, precision=lax.Precision.HIGHEST)
    query_block = jnp.arange(seq_len)[None, :] // 128
    key_block = jnp.arange(8)[:, None]
    left_sum = jnp.sum(jnp.where(key_block <= query_block - 2, far_sums, 0.0), axis=(1, 2))
    right_sum = jnp.sum(jnp.where(key_block >= query_block + 2, far_sums, 0.0), axis=(1, 2))
    grad_table = grad_table.at[BUCKETS // 2 - 1].add(left_sum).at[BUCKETS - 1].add(right_sum)
    axes = ("dp", "seq")
    small_grad = jnp.concatenate(
        [
            grad_gain_first.reshape(n_dev, g_rows),
            grad_gain_second.reshape(n_dev, g_rows),
            grad_table.reshape(n_dev, t_rows),
        ],
        axis=1,
    )
    small_own = lax.psum_scatter(small_grad, axes, scatter_dimension=0, tiled=True)[0]
    owned = [
        lax.psum_scatter(g.astype(BF), axes, scatter_dimension=0, tiled=True).astype(F32)
        for g in (grad_qkv, grad_out, grad_in, grad_back)
    ]
    return (
        output,
        grad_tokens,
        small_own[:g_rows],
        small_own[g_rows : 2 * g_rows],
        small_own[2 * g_rows :],
        *owned,
    )


def solution(mesh):
    in_specs = (
        P("dp", "seq", None),
        P("dp", "seq"),
        P("dp", "seq"),
        P("dp", "seq", None),
        P(("dp", "seq")),
        P(("dp", "seq")),
        P(("dp", "seq")),
        P(("dp", "seq"), None),
        P(("dp", "seq"), None),
        P(("dp", "seq"), None),
        P(("dp", "seq"), None),
    )
    out_specs = (
        P("dp", "seq", None),
        P("dp", "seq", None),
        P(("dp", "seq")),
        P(("dp", "seq")),
        P(("dp", "seq")),
        P(("dp", "seq"), None),
        P(("dp", "seq"), None),
        P(("dp", "seq"), None),
        P(("dp", "seq"), None),
    )
    return jax.shard_map(fast_shards if fits(mesh) else general_shards, mesh=mesh, in_specs=in_specs, out_specs=out_specs, check_vma=False)
```

```python
import functools

import jax
import jax.numpy as jnp
from jax import lax
from jax.experimental import pallas as pl
from jax.experimental.pallas import tpu as pltpu
from jax.sharding import PartitionSpec as P

HEADS = 12
HD = 64
BUCKETS = 32


EPS = 1e-06
NEGATIVE = -1e30
bucket_limits = (12, 16, 23, 32, 46, 64, 91)


def bucket_of(relative):
    distance = jnp.abs(relative)
    counted = jnp.zeros_like(distance)
    for threshold in bucket_limits:
        counted = counted + (distance >= threshold).astype(jnp.int32)
    inside = jnp.where(distance < 8, distance, 8 + counted)
    return inside + 16 * (relative > 0).astype(jnp.int32)


def rms_scale(values):
    return lax.rsqrt(jnp.mean(values * values, axis=-1, keepdims=True) + EPS)


def smooth_gate(values):
    return jax.nn.gelu(values, approximate=True)


def norm_backward(values, scale_inv, gain_vec, grad_normed):
    weighted = grad_normed * gain_vec
    grad_gain = jnp.sum(grad_normed * values * scale_inv, axis=0)
    cubed = scale_inv * scale_inv * scale_inv
    grad_values = scale_inv * weighted - values * cubed * jnp.mean(
        weighted * values, axis=-1, keepdims=True
    )
    return (grad_values, grad_gain)


def group_scores(query_part, key_part, seg_query, seg_key, complete_bias):
    scores = (
        jnp.einsum("gqhd,gkhd->ghqk", query_part, key_part, preferred_element_type=jnp.float32)
        + complete_bias[None]
    )
    allowed = (seg_query[:, :, None] == seg_key[:, None, :])[:, None]
    return jnp.where(allowed, scores, NEGATIVE)


def query_backward(items, complete_bias):
    query_part, key_part, value_part, seg_query, seg_key, log_total, grad_part = items
    scores = group_scores(query_part, key_part, seg_query, seg_key, complete_bias)
    softmax_probabilities = jnp.exp(scores - log_total)
    grad_probs = jnp.einsum(
        "gqhd,gkhd->ghqk", grad_part, value_part, preferred_element_type=jnp.float32
    )
    row_inner = jnp.sum(softmax_probabilities * grad_probs, axis=-1, keepdims=True)
    grad_scores = (softmax_probabilities * (grad_probs - row_inner)).astype(jnp.bfloat16)
    grad_query = jnp.einsum(
        "ghqk,gkhd->gqhd", grad_scores, key_part, preferred_element_type=jnp.float32
    ).astype(jnp.bfloat16)
    return (softmax_probabilities, grad_scores, grad_query, row_inner)


def general_shards(
    tokens,
    segment_ids,
    valid_mask,
    cotangent,
    gain_one,
    gain_two,
    bias_table,
    qkv_weight,
    out_weight,
    in_weight,
    back_weight,
):
    gathered = (
        lax.all_gather(gain_one, ("dp", "seq"), axis=0, tiled=True),
        lax.all_gather(gain_two, ("dp", "seq"), axis=0, tiled=True),
        lax.all_gather(bias_table, ("dp", "seq"), axis=0, tiled=True),
        lax.all_gather(qkv_weight, ("dp", "seq"), axis=0, tiled=True),
        lax.all_gather(out_weight, ("dp", "seq"), axis=0, tiled=True),
        lax.all_gather(in_weight, ("dp", "seq"), axis=0, tiled=True),
        lax.all_gather(back_weight, ("dp", "seq"), axis=0, tiled=True),
    )
    gain_first, gain_second, table_flat, qkv_full, out_full, in_full, back_full = gathered
    seq_count, block_len, model_width = tokens.shape
    seq_len = block_len * lax.axis_size("seq")
    row_count = seq_count * block_len
    group_size = seq_count
    while group_size % 2 == 0 and group_size // 2 * block_len >= 512:
        group_size = group_size // 2
    group_count = seq_count // group_size
    flat_x = tokens.reshape(row_count, model_width).astype(jnp.float32)
    first_scale = rms_scale(flat_x)
    first_gain = gain_first.astype(jnp.float32)
    first_normed = (flat_x * first_scale * first_gain).astype(jnp.bfloat16)
    projected = jnp.dot(first_normed, qkv_full, preferred_element_type=jnp.float32).astype(
        jnp.bfloat16
    )
    queries = projected[:, :model_width].reshape(group_count, group_size, block_len, HEADS, HD)
    local_keys = projected[:, model_width : 2 * model_width].reshape(
        seq_count, block_len, model_width
    )
    local_values = projected[:, 2 * model_width :].reshape(seq_count, block_len, model_width)
    all_keys, all_values, all_segments = (
        lax.all_gather(local_keys, "seq", axis=1, tiled=True),
        lax.all_gather(local_values, "seq", axis=1, tiled=True),
        lax.all_gather(segment_ids, "seq", axis=1, tiled=True),
    )
    key_groups = all_keys.reshape(group_count, group_size, seq_len, HEADS, HD)
    value_groups = all_values.reshape(group_count, group_size, seq_len, HEADS, HD)
    segkey_groups = all_segments.reshape(group_count, group_size, seq_len)
    segquery_groups = segment_ids.reshape(group_count, group_size, block_len)
    offset = lax.axis_index("seq") * block_len
    query_places = offset + jnp.arange(block_len, dtype=jnp.int32)
    key_places = jnp.arange(seq_len, dtype=jnp.int32)
    buckets = bucket_of(key_places[None, :] - query_places[:, None])
    single_hot_vector = (
        buckets[None] == jnp.arange(BUCKETS, dtype=jnp.int32)[:, None, None]
    ).astype(jnp.bfloat16)
    bias_matrix = table_flat.reshape(BUCKETS, HEADS)
    complete_bias = jnp.einsum(
        "dto,dl->lto", single_hot_vector, bias_matrix, preferred_element_type=jnp.float32
    )

    def attend(group_items):
        query_part, key_part, value_part, seg_query, seg_key = group_items
        scores = group_scores(query_part, key_part, seg_query, seg_key, complete_bias)
        row_peak = jnp.max(scores, axis=-1, keepdims=True)
        shifted = jnp.exp(scores - row_peak)
        row_total = jnp.sum(shifted, axis=-1, keepdims=True)
        softmax_probabilities = (shifted / row_total).astype(jnp.bfloat16)
        attn_part = jnp.einsum(
            "ghqk,gkhd->gqhd", softmax_probabilities, value_part, preferred_element_type=jnp.float32
        )
        return (attn_part.astype(jnp.bfloat16), row_peak + jnp.log(row_total))

    attn_mixed, log_totals = lax.map(
        attend, (queries, key_groups, value_groups, segquery_groups, segkey_groups)
    )
    mixed_flat = attn_mixed.reshape(row_count, model_width)
    middle = flat_x + jnp.dot(mixed_flat, out_full, preferred_element_type=jnp.float32)
    second_scale = rms_scale(middle)
    second_gain = gain_second.astype(jnp.float32)
    second_normed = (middle * second_scale * second_gain).astype(jnp.bfloat16)
    hidden_pre = jnp.dot(second_normed, in_full, preferred_element_type=jnp.float32)
    hidden_float, gate_pullback = jax.vjp(smooth_gate, hidden_pre)
    hidden = hidden_float.astype(jnp.bfloat16)
    result = middle + jnp.dot(hidden, back_full, preferred_element_type=jnp.float32)
    output = result.astype(jnp.bfloat16).reshape(seq_count, block_len, model_width)
    grad_result = cotangent.reshape(row_count, model_width).astype(
        jnp.float32
    ) * valid_mask.reshape(row_count, 1).astype(jnp.float32)
    grad_branch = grad_result.astype(jnp.bfloat16)
    grad_back = jnp.einsum("tf,td->fd", hidden, grad_branch, preferred_element_type=jnp.float32)
    grad_hidden = jnp.einsum(
        "td,fd->tf", grad_branch, back_full, preferred_element_type=jnp.float32
    )
    grad_pre = gate_pullback(grad_hidden)[0].astype(jnp.bfloat16)
    grad_in = jnp.einsum("td,tf->df", second_normed, grad_pre, preferred_element_type=jnp.float32)
    grad_second_normed = jnp.einsum(
        "tf,df->td", grad_pre, in_full, preferred_element_type=jnp.float32
    )
    grad_middle_norm, grad_gain_second = norm_backward(
        middle, second_scale, second_gain, grad_second_normed
    )
    grad_middle = grad_result + grad_middle_norm
    grad_attn = grad_middle.astype(jnp.bfloat16)
    grad_out = jnp.einsum("td,te->de", mixed_flat, grad_attn, preferred_element_type=jnp.float32)
    grad_mixed = jnp.einsum(
        "te,de->td", grad_attn, out_full, preferred_element_type=jnp.float32
    ).astype(jnp.bfloat16)
    grad_mixed_groups = grad_mixed.reshape(group_count, group_size, block_len, HEADS, HD)
    backward_entries = (
        queries,
        key_groups,
        value_groups,
        segquery_groups,
        segkey_groups,
        log_totals,
        grad_mixed_groups,
    )
    bias_zero = jnp.zeros((HEADS, block_len, seq_len), jnp.float32)

    def full_backward(bias_total_sum, group_items):
        softmax_probabilities, grad_scores, grad_query, row_inner = query_backward(
            group_items, complete_bias
        )
        query_part = group_items[0]
        grad_part = group_items[6]
        key_gradient = jnp.einsum(
            "ghqk,gqhd->gkhd", grad_scores, query_part, preferred_element_type=jnp.float32
        )
        grad_value = jnp.einsum(
            "ghqk,gqhd->gkhd",
            softmax_probabilities.astype(jnp.bfloat16),
            grad_part,
            preferred_element_type=jnp.float32,
        )
        bias_total_sum = bias_total_sum + jnp.sum(grad_scores.astype(jnp.float32), axis=0)
        return (bias_total_sum, (grad_query, key_gradient, grad_value))

    bias_total_sum, (grad_queries, grad_keys, grad_values) = lax.scan(
        full_backward, bias_zero, backward_entries
    )
    key_terms = grad_keys.reshape(seq_count, seq_len, model_width)
    value_terms = grad_values.reshape(seq_count, seq_len, model_width)
    key_sum, value_sum = (
        lax.psum_scatter(
            key_terms.astype(jnp.bfloat16), "seq", scatter_dimension=1, tiled=True
        ).astype(jnp.float32),
        lax.psum_scatter(
            value_terms.astype(jnp.bfloat16), "seq", scatter_dimension=1, tiled=True
        ).astype(jnp.float32),
    )
    key_low = key_sum.astype(jnp.bfloat16)
    value_low = value_sum.astype(jnp.bfloat16)
    grad_projected = jnp.concatenate(
        [
            grad_queries.reshape(row_count, model_width),
            key_low.reshape(row_count, model_width),
            value_low.reshape(row_count, model_width),
        ],
        axis=1,
    )
    grad_qkv = jnp.einsum(
        "td,te->de", first_normed, grad_projected, preferred_element_type=jnp.float32
    )
    grad_first_normed = jnp.einsum(
        "te,de->td", grad_projected, qkv_full, preferred_element_type=jnp.float32
    )
    grad_x_norm, grad_gain_first = norm_backward(flat_x, first_scale, first_gain, grad_first_normed)
    grad_tokens = (
        (grad_middle + grad_x_norm).astype(jnp.bfloat16).reshape(seq_count, block_len, model_width)
    )
    grad_table = jnp.einsum(
        "fuy,suy->fs",
        single_hot_vector.astype(jnp.float32),
        bias_total_sum,
        precision=lax.Precision.HIGHEST,
    ).reshape(BUCKETS * HEADS)
    owned = (
        lax.psum_scatter(grad_gain_first, ("dp", "seq"), scatter_dimension=0, tiled=True),
        lax.psum_scatter(grad_gain_second, ("dp", "seq"), scatter_dimension=0, tiled=True),
        lax.psum_scatter(grad_table, ("dp", "seq"), scatter_dimension=0, tiled=True),
        lax.psum_scatter(grad_qkv, ("dp", "seq"), scatter_dimension=0, tiled=True),
        lax.psum_scatter(grad_out, ("dp", "seq"), scatter_dimension=0, tiled=True),
        lax.psum_scatter(grad_in, ("dp", "seq"), scatter_dimension=0, tiled=True),
        lax.psum_scatter(grad_back, ("dp", "seq"), scatter_dimension=0, tiled=True),
    )
    owned_gain_one, owned_gain_two, owned_table, owned_qkv, owned_out, owned_in, owned_back = owned
    return (
        output,
        grad_tokens,
        owned_gain_one,
        owned_gain_two,
        owned_table,
        owned_qkv,
        owned_out,
        owned_in,
        owned_back,
    )


MESH = pl.DeviceIdType.MESH

def flip(i, bit):
    return i + bit - 2 * bit * ((i // bit) % 2)

def gather_kernel(items, *refs):
    n_arr = 5
    tok, seg = refs[0], refs[1]
    shards = refs[2:2 + n_arr]
    xf, sf = refs[2 + n_arr], refs[3 + n_arr]
    full = refs[4 + n_arr:4 + 2 * n_arr]
    loc_sem, t_send, t_recv, s_send, s_recv, z_send, z_recv, h_send, h_recv = refs[4 + 2 * n_arr:]
    dp, z = lax.axis_index("dp"), lax.axis_index("seq")
    n_z = 4
    peers = [(dp, lax.rem(z + s, n_z)) for s in range(1, n_z)] + [(flip(dp, b), z) for b in (1, 2, 4)]
    barrier = pltpu.get_barrier_semaphore()
    for p in peers:
        pl.semaphore_signal(barrier, inc=1, device_id=p, device_id_type=MESH)
    pl.semaphore_wait(barrier, len(peers))

    def block(it, d, zz):
        return full[items[it][0]].at[d * n_z + zz]

    def own(it):
        return shards[items[it][0]]

    n_it = len(items)
    def z_copy(it, way, step):
        src_z = z - step if way == 0 else z + step
        src = own(it) if step == 0 else block(it, dp, src_z)
        return pltpu.make_async_remote_copy(
            src_ref=src, dst_ref=block(it, dp, src_z), send_sem=z_send.at[it, way, step],
            recv_sem=z_recv.at[it, way, step], device_id=(dp, z + 1 if way == 0 else z - 1), device_id_type=MESH)

    def z_wait(it, way, step):
        src_z = z - 1 - step if way == 0 else z + 1 + step
        blk = block(it, dp, src_z)
        pltpu.make_async_remote_copy(src_ref=blk, dst_ref=blk, send_sem=z_send.at[it, way, step],
            recv_sem=z_recv.at[it, way, step], device_id=(dp, z), device_id_type=MESH).wait_recv()

    def can_send(way, step):
        return (z >= step) & (z <= n_z - 2) if way == 0 else (z + step <= n_z - 1) & (z >= 1)

    def can_recv(way, step):
        return z >= step + 1 if way == 0 else z + 1 + step <= n_z - 1

    def z_start(it, step):
        for way in (0, 1):
            @pl.when(can_send(way, step))
            def _():
                z_copy(it, way, step).start()

    def z_recv_all(it, step):
        for way in (0, 1):
            @pl.when(can_recv(way, step))
            def _():
                z_wait(it, way, step)

    def hops(it):
        b1, b2 = items[it][1:]
        return [(0, b1), (0, b2), (b1, b2), (0, 1), (b1, 1), (b2, 1), (b1 + b2, 1)]

    def flips(d, mask):
        for b in (1, 2, 4):
            if mask & b:
                d = flip(d, b)
        return d

    def hop(it, slot, zz):
        mask, to = hops(it)[slot]
        blk = block(it, flips(dp, mask), zz)
        return pltpu.make_async_remote_copy(src_ref=blk, dst_ref=blk, send_sem=h_send.at[it, slot, zz],
            recv_sem=h_recv.at[it, slot, zz], device_id=(flip(dp, to), z), device_id_type=MESH)

    def hop_wait(it, slot, zz):
        mask, to = hops(it)[slot]
        blk = block(it, flips(dp, mask ^ to), zz)
        pltpu.make_async_remote_copy(src_ref=blk, dst_ref=blk, send_sem=h_send.at[it, slot, zz],
            recv_sem=h_recv.at[it, slot, zz], device_id=(dp, z), device_id_type=MESH).wait_recv()

    def own_hop(it, slot):
        to = hops(it)[slot][1]
        return pltpu.make_async_remote_copy(src_ref=own(it), dst_ref=block(it, dp, z), send_sem=h_send.at[it, slot, z],
            recv_sem=h_recv.at[it, slot, z], device_id=(flip(dp, to), z), device_id_type=MESH)

    def tok_copy(s):
        to = lax.rem(z + s, n_z)
        return [pltpu.make_async_remote_copy(src_ref=a.at[to], dst_ref=f.at[z], send_sem=ss.at[s - 1], recv_sem=rs.at[s - 1],
                device_id=(dp, to), device_id_type=MESH) for a, f, ss, rs in ((tok, xf, t_send, t_recv), (seg, sf, s_send, s_recv))]

    def tok_wait(s):
        frm = lax.rem(z + n_z - s, n_z)
        for f, ss, rs in ((xf, t_send, t_recv), (sf, s_send, s_recv)):
            pltpu.make_async_remote_copy(src_ref=f.at[frm], dst_ref=f.at[frm], send_sem=ss.at[s - 1], recv_sem=rs.at[s - 1],
                device_id=(dp, z), device_id_type=MESH).wait_recv()

    for it in range(n_it):
        z_start(it, 0)
        for slot in (0, 1, 3):
            own_hop(it, slot).start()
    locs = []
    for it in range(n_it):
        locs.append(pltpu.make_async_copy(own(it), block(it, dp, z), loc_sem.at[it]))
    locs.append(pltpu.make_async_copy(tok.at[z], xf.at[z], loc_sem.at[n_it]))
    locs.append(pltpu.make_async_copy(seg.at[z], sf.at[z], loc_sem.at[n_it + 1]))
    for c in locs:
        c.start()

    def forward(it, zz):
        hop_wait(it, 0, zz)
        hop(it, 2, zz).start()
        hop(it, 4, zz).start()
        hop_wait(it, 1, zz)
        hop(it, 5, zz).start()

    def arrivals(step):
        return [(can_recv(0, step), 0, z - 1 - step), (can_recv(1, step), 1, z + 1 + step)]

    for step in range(n_z):
        if step < n_z - 1:
            for it in range(n_it):
                for ok, way, zz in arrivals(step):
                    @pl.when(ok)
                    def _():
                        z_wait(it, way, step)
                        if step < n_z - 2:
                            @pl.when(can_send(way, step + 1))
                            def _():
                                z_copy(it, way, step + 1).start()
                        for slot in (0, 1, 3):
                            hop(it, slot, zz).start()
        if step == 1:
            for s in range(1, n_z):
                for c in tok_copy(s):
                    c.start()
        for it in range(n_it):
            if step == 0:
                forward(it, z)
            else:
                for ok, way, zz in arrivals(step - 1):
                    @pl.when(ok)
                    def _():
                        forward(it, zz)
    for zz in range(n_z):
        for it in range(n_it):
            hop_wait(it, 2, zz)
            hop(it, 6, zz).start()
    for s in range(1, n_z):
        tok_wait(s)
    for zz in range(n_z):
        for it in range(n_it):
            for slot in (3, 4, 5, 6):
                hop_wait(it, slot, zz)
    for c in locs:
        c.wait()
    for it in range(n_it):
        for step in range(n_z - 1):
            for way in (0, 1):
                @pl.when(can_send(way, step))
                def _():
                    z_copy(it, way, step).wait_send()
        for zz in range(n_z):
            for slot in range(7):
                hop(it, slot, zz).wait_send()
    for s in range(1, n_z):
        for c in tok_copy(s):
            c.wait_send()

def gather(tokens, seg, shards, items, collective_id=0):
    n_it = len(items)
    D = pltpu.SemaphoreType.DMA
    out_shape = [jax.ShapeDtypeStruct(tokens.shape, tokens.dtype), jax.ShapeDtypeStruct(seg.shape, seg.dtype)]
    out_shape += [jax.ShapeDtypeStruct((32, *s.shape), s.dtype) for s in shards]
    anyspec = pl.BlockSpec(memory_space=pltpu.HBM)
    return pl.pallas_call(
        functools.partial(gather_kernel, items),
        out_shape=out_shape,
        in_specs=[pl.BlockSpec(memory_space=pltpu.VMEM)] * (2 + len(shards)),
        out_specs=[anyspec] * len(out_shape),
        scratch_shapes=[D((n_it + 2,)), D((3,)), D((3,)), D((3,)), D((3,)), D((n_it, 2, 3)), D((n_it, 2, 3)), D((n_it, 7, 4)), D((n_it, 7, 4))],
        compiler_params=pltpu.CompilerParams(collective_id=collective_id, has_side_effects=True),
    )(tokens, seg, *shards)


LOG2E = 1.4426950408889634
BIG = -1e30
F32 = jnp.float32
BF = jnp.bfloat16

def extras(seg):
    L = seg.shape[0]
    nb = L.bit_length()
    nblk = L // 128
    lane = jnp.arange(128)[None, :] % 64
    row_blk = (jnp.arange(L) // 128)[:, None]
    b = lane - (nblk + 3)
    inb = (b >= 0) & (b < 2 * nb)
    bit = (seg[:, None] >> (jnp.clip(b, 0, 2 * nb - 1) // 2)) & 1
    flip = b % 2
    u = jnp.where(inb, (bit ^ flip), 0).astype(BF)
    w = jnp.where(inb & ((bit ^ flip) == 0), BIG, 0.0)
    onehot = (lane < nblk) & (lane == row_blk)
    ones = (lane >= nblk) & (lane < nblk + 3)
    exk = (w + (onehot | ones)).astype(BF)
    farl = ((lane < nblk) & (lane <= row_blk - 2)).astype(BF)
    farr = ((lane < nblk) & (lane >= row_blk + 2)).astype(BF)
    return u, exk, farl, farr

def strips(table):
    a = jnp.arange(128)[:, None]; c = jnp.arange(384)[None, :]
    bq = bucket_of(c - 128 - a)
    bk = bucket_of(a + 128 - c)
    def look(bk_):
        oh = (bk_[None] == jnp.arange(32)[:, None, None]).astype(BF)
        return jnp.einsum('bac,bh->hac', oh, table.astype(BF), preferred_element_type=F32)
    return look(bq), look(bk)

def fwd_kernel(nblk, bl_ref, q_ref, k_ref, v_ref, exq_ref, exk_ref, fl_ref, fr_ref, strip_ref, o_ref, qa_ref):
    L = q_ref.shape[0]
    hp = pl.program_id(0)
    lane = lax.broadcasted_iota(jnp.int32, (L, 128), 1)
    QB = 256
    outs = []
    for h in range(2):
        sel = (lane < 64) if h == 0 else (lane >= 64)
        bl = bl_ref[hp * 2 + h, 0].astype(BF); br = bl_ref[hp * 2 + h, 1].astype(BF)
        qa = jnp.where(sel, q_ref[...], exq_ref[...] + fl_ref[...] * bl + fr_ref[...] * br)
        ka = jnp.where(sel, k_ref[...], exk_ref[...])
        va = jnp.where(sel, v_ref[...], jnp.ones((L, 128), BF))
        lane_l = 64 * (1 - h)
        for blk in range(L // QB):
            r0 = blk * QB
            qb = qa[r0:r0 + QB]
            s = lax.dot_general(qb, ka, (((1,), (1,)), ((), ())), preferred_element_type=F32)
            rows = []
            for sub in range(QB // 128):
                I = blk * (QB // 128) + sub
                lo = max(I - 1, 0); hi = min(I + 1, nblk - 1)
                srow = s[sub * 128:(sub + 1) * 128]
                parts = []
                if lo > 0: parts.append(srow[:, :lo * 128])
                parts.append(srow[:, lo * 128:(hi + 1) * 128] + strip_ref[h, :, (lo - I + 1) * 128:(hi - I + 2) * 128])
                if hi < nblk - 1: parts.append(srow[:, (hi + 1) * 128:])
                rows.append(jnp.concatenate(parts, axis=1))
            s = jnp.concatenate(rows, axis=0)
            m = jnp.max(s, axis=1, keepdims=True)
            p = jnp.exp2((s - m) * LOG2E).astype(BF)
            o = jnp.dot(p, va, preferred_element_type=F32)
            l = o[:, lane_l:lane_l + 1]
            outs.append(o / l)
            lse = m + jnp.log(l)
            hi_ = (-lse).astype(BF); rest = -lse - hi_.astype(F32)
            mid = rest.astype(BF); low = (rest - mid.astype(F32)).astype(BF)
            base = 64 * (1 - h) + nblk
            ln = lane[:QB]
            qx = jnp.where(ln == base, hi_, jnp.where(ln == base + 1, mid, jnp.where(ln == base + 2, low, qb)))
            qa_ref[h, r0:r0 + QB, :] = qx
    n = L // QB
    for blk in range(n):
        o_ref[blk * QB:(blk + 1) * QB, :] = jnp.where(lane[:QB] < 64, outs[blk], outs[n + blk]).astype(BF)

def attn_fwd(qkv, ex, strip, far, interpret=False):
    L, W = qkv.shape
    D = W // 3
    H = D // HD
    npair = H // 2
    nblk = L // 128
    exq, exk, fl, fr = ex
    full = lambda: pl.BlockSpec((L, 128), lambda i: (0, 0))
    return pl.pallas_call(
        functools.partial(fwd_kernel, nblk),
        grid=(npair,),
        in_specs=[pl.BlockSpec(memory_space=pltpu.SMEM),
                  pl.BlockSpec((L, 128), lambda i: (0, i)),
                  pl.BlockSpec((L, 128), lambda i: (0, npair + i)),
                  pl.BlockSpec((L, 128), lambda i: (0, 2 * npair + i)),
                  full(), full(), full(), full(),
                  pl.BlockSpec((2, 128, 384), lambda i: (i, 0, 0))],
        out_specs=[pl.BlockSpec((L, 128), lambda i: (0, i)), pl.BlockSpec((2, L, 128), lambda i: (i, 0, 0))],
        out_shape=[jax.ShapeDtypeStruct((L, D), BF), jax.ShapeDtypeStruct((H, L, 128), BF)],
        compiler_params=pltpu.CompilerParams(vmem_limit_bytes=48 << 20),
        cost_estimate=pl.CostEstimate(flops=4 * L * L * D * 4, bytes_accessed=L * W * 4, transcendentals=L * L * H),
    )(far, qkv, qkv, qkv, exq, exk, fl, fr, strip)

def bwd_kernel(nblk, qa_ref, k_ref, v_ref, do_ref, o_ref, exk_ref, strip_ref,
               dq_ref, dk_ref, dv_ref, near_ref, far_ref):
    L = k_ref.shape[0]
    lane = lax.broadcasted_iota(jnp.int32, (L, 128), 1)
    KB = 256
    nsub = KB // 128
    prod = do_ref[...].astype(F32) * o_ref[...].astype(F32)
    dqs = []; dks = []; dvs = []
    for h in range(2):
        sel = (lane < 64) if h == 0 else (lane >= 64)
        other = 64 * (1 - h)
        qa = qa_ref[h]
        ka = jnp.where(sel, k_ref[...], exk_ref[...])
        va = jnp.where(sel, v_ref[...], ((lane >= other + nblk) & (lane < other + nblk + 3)).astype(BF))
        delta = -jnp.sum(jnp.where(sel, prod, 0.0), axis=1, keepdims=True)
        hi_ = delta.astype(BF); rest = delta - hi_.astype(F32)
        mid = rest.astype(BF); low = (rest - mid.astype(F32)).astype(BF)
        base = other + nblk
        doa = jnp.where(sel, do_ref[...], jnp.where(lane == base, hi_, jnp.where(lane == base + 1, mid, jnp.where(lane == base + 2, low, jnp.zeros((L, 128), BF)))))
        near = jnp.zeros((128, 384), F32)
        dqt = jnp.zeros((128, L), F32)
        for kb in range(L // KB):
            r0 = kb * KB
            kab = ka[r0:r0 + KB]
            s = lax.dot_general(kab, qa, (((1,), (1,)), ((), ())), preferred_element_type=F32)
            dp = lax.dot_general(va[r0:r0 + KB], doa, (((1,), (1,)), ((), ())), preferred_element_type=F32)
            prow = []; dsrow = []
            for sub in range(nsub):
                J = kb * nsub + sub
                lo = max(J - 1, 0); hi = min(J + 1, nblk - 1)
                srow = s[sub * 128:(sub + 1) * 128]
                parts = []
                if lo > 0: parts.append(srow[:, :lo * 128])
                parts.append(srow[:, lo * 128:(hi + 1) * 128] + strip_ref[h, :, (lo - J + 1) * 128:(hi - J + 2) * 128])
                if hi < nblk - 1: parts.append(srow[:, (hi + 1) * 128:])
                srow = jnp.concatenate(parts, axis=1)
                p = jnp.exp2(srow * LOG2E)
                ds = p * dp[sub * 128:(sub + 1) * 128]
                nr = ds[:, lo * 128:(hi + 1) * 128]
                if lo > J - 1: nr = jnp.concatenate([jnp.zeros((128, 128), F32), nr], axis=1)
                if hi < J + 1: nr = jnp.concatenate([nr, jnp.zeros((128, 128), F32)], axis=1)
                near = near + nr
                prow.append(p.astype(BF)); dsrow.append(ds.astype(BF))
            pb = jnp.concatenate(prow, axis=0); dsb = jnp.concatenate(dsrow, axis=0)
            dvs.append(jnp.dot(pb, doa, preferred_element_type=F32))
            dks.append(jnp.dot(dsb, qa, preferred_element_type=F32))
            dqt = dqt + lax.dot_general(kab, dsb, (((0,), (0,)), ((), ())), preferred_element_type=F32)
        near_ref[h] = near
        far_ref[h] = dqt[other:other + 8]
        dqs.append(dqt[64 * h:64 * h + 64])
    n = L // KB
    first = lane[:KB] < 64
    for kb in range(n):
        dk_ref[kb * KB:(kb + 1) * KB, :] = jnp.where(first, dks[kb], dks[n + kb]).astype(BF)
        dv_ref[kb * KB:(kb + 1) * KB, :] = jnp.where(first, dvs[kb], dvs[n + kb]).astype(BF)
    dq_ref[...] = jnp.concatenate(dqs, axis=0).T.astype(BF)

def attn_bwd(qa, qkv, do, o, exk, stripT):
    L, W = qkv.shape
    D = W // 3
    H = D // HD
    npair = H // 2
    nblk = L // 128
    col = lambda off: pl.BlockSpec((L, 128), lambda i: (0, off + i))
    return pl.pallas_call(
        functools.partial(bwd_kernel, nblk),
        grid=(npair,),
        in_specs=[pl.BlockSpec((2, L, 128), lambda i: (i, 0, 0)), col(npair), col(2 * npair), col(0), col(0),
                  pl.BlockSpec((L, 128), lambda i: (0, 0)), pl.BlockSpec((2, 128, 384), lambda i: (i, 0, 0))],
        out_specs=[col(0), col(0), col(0), pl.BlockSpec((2, 128, 384), lambda i: (i, 0, 0)), pl.BlockSpec((2, 8, L), lambda i: (i, 0, 0))],
        out_shape=[jax.ShapeDtypeStruct((L, D), BF)] * 3 + [jax.ShapeDtypeStruct((H, 128, 384), F32), jax.ShapeDtypeStruct((H, 8, L), F32)],
        compiler_params=pltpu.CompilerParams(vmem_limit_bytes=48 << 20),
        cost_estimate=pl.CostEstimate(flops=10 * L * L * D * 4, bytes_accessed=L * W * 6, transcendentals=L * L * H),
    )(qa, qkv, qkv, do, o, exk, stripT)


GELU_A = 0.7978845608028654
GELU_B = 0.044715


def mm(a, b, dims=((1,), (0,))):
    return lax.dot_general(a, b, (dims, ((), ())), preferred_element_type=F32)


def ffn_kernel(x_ref, mixed_ref, g_ref, gain_ref, wo_ref, wi_ref, wb_ref,
               out_ref, gm_ref, gmix_ref, dwo_ref, dwi_ref, dwb_ref, dgain_ref,
               mid_ref, h_ref, ht_ref, acc_ref, dh_ref):
    step = pl.program_id(0)
    rows = x_ref.shape[0]
    half = 256

    @pl.when(step == 0)
    def _():
        for r in range(0, rows, half):
            part = pl.ds(r, half)
            middle = x_ref[part].astype(F32) + mm(mixed_ref[part], wo_ref[...])
            mid_ref[part] = middle
            acc_ref[part] = middle
            scale = lax.rsqrt(jnp.mean(middle * middle, axis=-1, keepdims=True) + EPS)
            normed = (middle * scale * gain_ref[...]).astype(BF)
            h_ref[part] = normed
            ht_ref[:, part] = normed.T
            dh_ref[part] = jnp.zeros((half, x_ref.shape[1]), F32)

    gates = []
    hiddens = []
    for r in range(0, rows, half):
        part = pl.ds(r, half)
        pre = mm(h_ref[part], wi_ref[...])
        dhid = mm(g_ref[part], wb_ref[...], ((1,), (1,)))
        sq = pre * pre
        t = jnp.tanh(pre * (GELU_A + GELU_A * GELU_B * sq))
        half_t = 0.5 + 0.5 * t
        hidden = (pre * half_t).astype(BF)
        slope = half_t + pre * (0.5 - 0.5 * t * t) * (GELU_A + 3.0 * GELU_A * GELU_B * sq)
        dpre = (dhid * slope).astype(BF)
        acc_ref[part] += mm(hidden, wb_ref[...])
        dh_ref[part] += mm(dpre, wi_ref[...], ((1,), (1,)))
        hiddens.append(hidden)
        gates.append(dpre)
    dwi_ref[...] = mm(ht_ref[...], jnp.concatenate(gates, axis=0)).astype(BF)
    dwb_ref[...] = mm(jnp.concatenate(hiddens, axis=0), g_ref[...], ((0,), (0,))).astype(BF)

    @pl.when(step == pl.num_programs(0) - 1)
    def _():
        dgain = jnp.zeros((1, x_ref.shape[1]), F32)
        for r in range(0, rows, half):
            part = pl.ds(r, half)
            out_ref[part] = acc_ref[part].astype(BF)
            middle = mid_ref[part]
            dh = dh_ref[part]
            scale = lax.rsqrt(jnp.mean(middle * middle, axis=-1, keepdims=True) + EPS)
            dgain += jnp.sum(dh * (middle * scale), axis=0, keepdims=True)
            u = dh * gain_ref[...]
            inner = jnp.mean(u * middle, axis=-1, keepdims=True)
            gm = g_ref[part].astype(F32) + scale * u - middle * (scale * scale * scale * inner)
            gm_ref[part] = gm
            low = gm.astype(BF)
            h_ref[part] = low
            gmix_ref[part] = mm(low, wo_ref[...], ((1,), (1,))).astype(BF)
        dgain_ref[...] = dgain
        dwo_ref[...] = mm(mixed_ref[...], h_ref[...], ((0,), (0,))).astype(BF)


def ffn(x, mixed, g, gain, wo, wi, wb, chunk=512):
    rows, width = x.shape
    ff = wi.shape[1]
    whole = lambda s: pl.BlockSpec(s, lambda i: (0, 0), pipeline_mode=pl.Buffered(1))
    S = jax.ShapeDtypeStruct
    return pl.pallas_call(
        ffn_kernel,
        grid=(ff // chunk,),
        in_specs=[whole((rows, width))] * 3 + [whole((1, width)), whole((width, width)),
                  pl.BlockSpec((width, chunk), lambda i: (0, i)), pl.BlockSpec((chunk, width), lambda i: (i, 0))],
        out_specs=[whole((rows, width))] * 3 + [whole((width, width)), pl.BlockSpec((width, chunk), lambda i: (0, i)),
                   pl.BlockSpec((chunk, width), lambda i: (i, 0)), whole((1, width))],
        out_shape=[S((rows, width), BF), S((rows, width), F32), S((rows, width), BF), S((width, width), BF),
                   S((width, ff), BF), S((ff, width), BF), S((1, width), F32)],
        scratch_shapes=[pltpu.VMEM((rows, width), F32), pltpu.VMEM((rows, width), BF), pltpu.VMEM((width, rows), BF),
                        pltpu.VMEM((rows, width), F32), pltpu.VMEM((rows, width), F32)],
        compiler_params=pltpu.CompilerParams(vmem_limit_bytes=56 << 20),
        cost_estimate=pl.CostEstimate(flops=12 * rows * width * ff + 6 * rows * width * width, bytes_accessed=50 << 20, transcendentals=rows * ff),
    )(x, mixed, g, gain, wo, wi, wb)


def tail_kernel(dq_ref, dk_ref, dv_ref, x_ref, gm_ref, gain_ref, w_ref, gx_ref, dw_ref, dgain_ref, ht_ref):
    rows, width = x_ref.shape
    half = 256
    dgain = jnp.zeros((1, width), F32)
    for r in range(0, rows, half):
        part = pl.ds(r, half)
        x = x_ref[part].astype(F32)
        scale = lax.rsqrt(jnp.mean(x * x, axis=-1, keepdims=True) + EPS)
        ht_ref[:, part] = (x * scale * gain_ref[...]).astype(BF).T
        dh = sum(mm(d[part], w_ref[:, i * width:(i + 1) * width], ((1,), (1,))) for i, d in enumerate((dq_ref, dk_ref, dv_ref)))
        dgain += jnp.sum(dh * (x * scale), axis=0, keepdims=True)
        u = dh * gain_ref[...]
        inner = jnp.mean(u * x, axis=-1, keepdims=True)
        gx_ref[part] = (gm_ref[part] + scale * u - x * (scale * scale * scale * inner)).astype(BF)
    dgain_ref[...] = dgain
    for i, d in enumerate((dq_ref, dk_ref, dv_ref)):
        dw_ref[:, i * width:(i + 1) * width] = mm(ht_ref[...], d[...]).astype(BF)


def tail(dq, dk, dv, x, gm, gain, w):
    rows, width = x.shape
    S = jax.ShapeDtypeStruct
    return pl.pallas_call(
        tail_kernel,
        out_shape=[S((rows, width), BF), S((width, 3 * width), BF), S((1, width), F32)],
        scratch_shapes=[pltpu.VMEM((width, rows), BF)],
        compiler_params=pltpu.CompilerParams(vmem_limit_bytes=56 << 20),
        cost_estimate=pl.CostEstimate(flops=12 * rows * width * width, bytes_accessed=24 << 20, transcendentals=0),
    )(dq, dk, dv, x, gm, gain, w)


def scatter_kernel(routes, *refs):
    n_it = len(routes)
    n_z = 4
    gx = refs[0]
    part = refs[1:1 + n_it]
    gx_out = refs[1 + n_it]
    outs = refs[2 + n_it:2 + 2 * n_it]
    scr = refs[2 + 2 * n_it:]
    rc, r2, r1, zo, zu, zd = (scr[k * n_it:(k + 1) * n_it] for k in range(6))
    loc_sem, t_send, t_recv, c_send, c_recv, x2_send, x2_recv, x1_send, x1_recv, z_send, z_recv = scr[6 * n_it:]
    dp, z = lax.axis_index("dp"), lax.axis_index("seq")
    core = lax.rem(dp, 2)
    quad = dp // 2
    peers = [(dp, lax.rem(z + s, n_z)) for s in range(1, n_z)] + [(flip(dp, b), z) for b in (1, 2, 4)]
    barrier = pltpu.get_barrier_semaphore()
    for p in peers:
        pl.semaphore_signal(barrier, inc=1, device_id=p, device_id_type=MESH)
    pl.semaphore_wait(barrier, len(peers))

    def remote(src, dst, ss, rs, to):
        return pltpu.make_async_remote_copy(src_ref=src, dst_ref=dst, send_sem=ss, recv_sem=rs, device_id=to, device_id_type=MESH)

    def add_into(dst, src, chunk=16):
        rows = dst.shape[0]
        chunk = min(chunk, rows)
        @pl.loop(0, rows // chunk)
        def _(i):
            at = pl.ds(pl.multiple_of(i * chunk, chunk), chunk)
            dst[at] = (dst[at].astype(F32) + src[at].astype(F32)).astype(dst.dtype)

    def q_at(it, f1, f2):
        b1, b2 = routes[it]
        q = quad
        if f1: q = flip(q, b1 // 2)
        if f2: q = flip(q, b2 // 2)
        return q

    def c_copy(it, q):
        return remote(part[it].at[2 * q + 1 - core], rc[it].at[q], c_send.at[it, q], c_recv.at[it, q], (flip(dp, 1), z))

    def x2_copy(it, f1):
        q = q_at(it, f1, True)
        k = (q // (routes[it][0] // 2)) % 2
        return remote(rc[it].at[q], r2[it].at[k], x2_send.at[it, k], x2_recv.at[it, k], (flip(dp, routes[it][1]), z))

    def x2_slot(it, f1):
        return (q_at(it, f1, False) // (routes[it][0] // 2)) % 2

    def x1_copy(it):
        return remote(rc[it].at[q_at(it, True, False)], r1[it], x1_send.at[it], x1_recv.at[it], (flip(dp, routes[it][0]), z))

    def tok_copy(s):
        to = lax.rem(z + s, n_z)
        return remote(gx.at[to], gx_out.at[z], t_send.at[s - 1], t_recv.at[s - 1], (dp, to))

    for it in range(n_it):
        for f1, f2 in ((False, True), (True, True), (True, False), (False, False)):
            c_copy(it, q_at(it, f1, f2)).start()
    loc = pltpu.make_async_copy(gx.at[z], gx_out.at[z], loc_sem.at[0])
    loc.start()
    for s in range(1, n_z):
        tok_copy(s).start()

    def core_sum(it, f1, f2):
        q = q_at(it, f1, f2)
        c_copy(it, q).wait_recv()
        add_into(rc[it].at[q], part[it].at[2 * q + core])

    for it in range(n_it):
        for f1 in (True, False):
            core_sum(it, f1, True)
            x2_copy(it, f1).start()
    for it in range(n_it):
        core_sum(it, True, False)
        core_sum(it, False, False)
    for it in range(n_it):
        for f1 in (True, False):
            k = x2_slot(it, f1)
            remote(rc[it].at[0], r2[it].at[k], x2_send.at[it, k], x2_recv.at[it, k], (dp, z)).wait_recv()
            add_into(rc[it].at[q_at(it, f1, False)], r2[it].at[k])
            if f1:
                x1_copy(it).start()

    def z_copy(it, way, j):
        src = zo[it].at[j]
        dst = (zu if way == 0 else zd)[it].at[j]
        return remote(src, dst, z_send.at[it, way, j], z_recv.at[it, way, j], (dp, z + 1 if way == 0 else z - 1))

    def z_wait(it, way, j):
        buf = (zu if way == 0 else zd)[it].at[j]
        remote(buf, buf, z_send.at[it, way, j], z_recv.at[it, way, j], (dp, z)).wait_recv()

    for it in range(n_it):
        x1_copy(it).wait_recv()
        rows = zo[it].shape[1]
        for j in range(n_z):
            at = pl.ds(j * rows, rows)
            zo[it][j] = (rc[it][quad, at].astype(F32) + r1[it][at].astype(F32)).astype(zo[it].dtype)
        for k in range(n_z - 1):
            for way, j in ((0, n_z - 1 - k), (1, k)):
                ahead, behind = (j > z, z > 0) if way == 0 else (j < z, z < n_z - 1)
                @pl.when(ahead)
                def _():
                    @pl.when(behind)
                    def _():
                        z_wait(it, way, j)
                        buf = (zu if way == 0 else zd)[it]
                        zo[it][j] = (zo[it][j].astype(F32) + buf[j].astype(F32)).astype(zo[it].dtype)
                    z_copy(it, way, j).start()
    for it in range(n_it):
        outs[it][...] = zo[it][z].astype(F32)
        @pl.when(z > 0)
        def _():
            z_wait(it, 0, z)
            outs[it][...] += zu[it][z].astype(F32)
        @pl.when(z < n_z - 1)
        def _():
            z_wait(it, 1, z)
            outs[it][...] += zd[it][z].astype(F32)
    for s in range(1, n_z):
        frm = lax.rem(z + n_z - s, n_z)
        remote(gx_out.at[frm], gx_out.at[frm], t_send.at[s - 1], t_recv.at[s - 1], (dp, z)).wait_recv()
    loc.wait()
    for s in range(1, n_z):
        tok_copy(s).wait_send()
    for it in range(n_it):
        for q in range(4):
            c_copy(it, q).wait_send()
        for f1 in (True, False):
            x2_copy(it, f1).wait_send()
        x1_copy(it).wait_send()
        for j in range(n_z):
            for way in (0, 1):
                @pl.when(j > z if way == 0 else j < z)
                def _():
                    z_copy(it, way, j).wait_send()

def scatter(gx, parts, routes, collective_id=1):
    n_it = len(parts)
    D = pltpu.SemaphoreType.DMA
    V = lambda p, *lead: pltpu.VMEM((*lead, *p.shape[1:]), p.dtype)
    zs = lambda p: pltpu.VMEM((4, p.shape[1] // 4, p.shape[2]), p.dtype)
    vm = pl.BlockSpec(memory_space=pltpu.VMEM)
    scratch = [V(p, 4) for p in parts] + [V(p, 2) for p in parts] + [V(p) for p in parts] + [zs(p) for p in parts] * 3
    scratch += [D((1,)), D((3,)), D((3,)), D((n_it, 4)), D((n_it, 4)), D((n_it, 2)), D((n_it, 2)), D((n_it,)), D((n_it,)), D((n_it, 2, 4)), D((n_it, 2, 4))]
    return pl.pallas_call(
        functools.partial(scatter_kernel, routes),
        out_shape=[jax.ShapeDtypeStruct(gx.shape, gx.dtype)] + [jax.ShapeDtypeStruct((p.shape[1] // 4, p.shape[2]), F32) for p in parts],
        in_specs=[vm] * (1 + n_it),
        out_specs=[pl.BlockSpec(memory_space=pltpu.HBM)] + [vm] * n_it,
        scratch_shapes=scratch,
        compiler_params=pltpu.CompilerParams(collective_id=collective_id, has_side_effects=True, vmem_limit_bytes=56 << 20),
    )(gx, *parts)


def fits(mesh):
    return mesh.shape["dp"] == 8 and mesh.shape["seq"] == 4


ITEMS = ((0, 4, 2), (4, 2, 4), (1, 2, 4), (2, 4, 2), (3, 2, 4))
ROUTES = ((4, 2), (2, 4), (2, 4), (4, 2), (2, 4))


def fast_shards(
    tokens,
    segment_ids,
    valid_mask,
    cotangent,
    gain_one,
    gain_two,
    bias_table,
    qkv_weight,
    out_weight,
    in_weight,
    back_weight,
):
    n_z = lax.axis_size("seq")
    seq_count, block_len, width = tokens.shape
    seq_len = n_z * block_len
    n_dev = n_z * lax.axis_size("dp")
    g_rows, t_rows = gain_one.shape[0], bias_table.shape[0]
    small = jnp.concatenate([gain_one, gain_two, bias_table])
    small = jnp.pad(small[None], ((0, 7), (0, 128 - small.shape[0])))
    grad_local = cotangent * valid_mask[..., None].astype(BF)
    x4, seg4, qkv_full, out_full, in_full, back_full, small_full = gather(
        tokens,
        segment_ids.reshape(seq_count, 1, block_len),
        (qkv_weight, out_weight, in_weight, back_weight, small),
        ITEMS,
    )
    qkv_full = qkv_full.reshape(width, 3 * width)
    out_full = out_full.reshape(width, width)
    in_full = in_full.reshape(width, -1)
    back_full = back_full.reshape(-1, width)
    small_full = small_full[:, 0]
    gain_first = small_full[:, :g_rows].reshape(1, width).astype(F32)
    gain_second = small_full[:, g_rows : 2 * g_rows].reshape(1, width).astype(F32)
    table = small_full[:, 2 * g_rows : 2 * g_rows + t_rows].reshape(BUCKETS, HEADS)
    grad_local, x4 = lax.optimization_barrier((grad_local, x4))
    g_low = lax.all_to_all(grad_local, "seq", 0, 1, tiled=True).reshape(seq_len, width)
    x = x4.reshape(seq_len, width)
    flat_x = x.astype(F32)
    seg = seg4.reshape(seq_len)
    exq, exk, far_left, far_right = extras(seg)
    strip, strip_t = strips(table.astype(F32))
    far = jnp.stack([table[BUCKETS // 2 - 1], table[BUCKETS - 1]], axis=1).astype(F32)
    first_normed = (flat_x * rms_scale(flat_x) * gain_first).astype(BF)
    projected = jnp.dot(first_normed, qkv_full, preferred_element_type=F32).astype(BF)
    mixed, q_aug = attn_fwd(projected, (exq, exk, far_left, far_right), strip, far)
    result, grad_middle, grad_mixed, grad_out, grad_in, grad_back, grad_gain_second = ffn(
        x, mixed, g_low, gain_second, out_full, in_full, back_full
    )
    output = lax.all_to_all(result.reshape(1, seq_len, width), "seq", 1, 0, tiled=True)
    dq, dk, dv, near, far_sums = attn_bwd(q_aug, projected, grad_mixed, mixed, exk, strip_t)
    grad_x, grad_qkv, grad_gain_first = tail(dq, dk, dv, x, grad_middle, gain_first, qkv_full)
    near_bucket = bucket_of(jnp.arange(128)[:, None] + 128 - jnp.arange(384)[None, :])
    near_hot = (near_bucket[None] == jnp.arange(BUCKETS)[:, None, None]).astype(F32)
    grad_table = jnp.einsum("bac,hac->bh", near_hot, near, precision=lax.Precision.HIGHEST)
    query_block = jnp.arange(seq_len)[None, :] // 128
    key_block = jnp.arange(8)[:, None]
    left_sum = jnp.sum(jnp.where(key_block <= query_block - 2, far_sums, 0.0), axis=(1, 2))
    right_sum = jnp.sum(jnp.where(key_block >= query_block + 2, far_sums, 0.0), axis=(1, 2))
    grad_table = grad_table.at[BUCKETS // 2 - 1].add(left_sum).at[BUCKETS - 1].add(right_sum)
    small_grad = jnp.concatenate(
        [
            grad_gain_first.reshape(n_dev, g_rows),
            grad_gain_second.reshape(n_dev, g_rows),
            grad_table.reshape(n_dev, t_rows),
        ],
        axis=1,
    )
    small_grad = jnp.pad(small_grad[:, None], ((0, 0), (0, 7), (0, 128 - small_grad.shape[1])))
    parts = (grad_qkv, small_grad.reshape(n_dev * 8, 128), grad_out, grad_in, grad_back)
    grad_tokens, own_qkv, own_small, own_out, own_in, own_back = scatter(
        grad_x.reshape(n_z, block_len, width),
        [p.reshape(8, -1, p.shape[1]) for p in parts],
        ROUTES,
    )
    own_small = own_small[0]
    return (
        output,
        grad_tokens,
        own_small[:g_rows],
        own_small[g_rows : 2 * g_rows],
        own_small[2 * g_rows : 2 * g_rows + t_rows],
        own_qkv,
        own_out,
        own_in,
        own_back,
    )


def solution(mesh):
    in_specs = (
        P("dp", "seq", None),
        P("dp", "seq"),
        P("dp", "seq"),
        P("dp", "seq", None),
        P(("dp", "seq")),
        P(("dp", "seq")),
        P(("dp", "seq")),
        P(("dp", "seq"), None),
        P(("dp", "seq"), None),
        P(("dp", "seq"), None),
        P(("dp", "seq"), None),
    )
    out_specs = (
        P("dp", "seq", None),
        P("dp", "seq", None),
        P(("dp", "seq")),
        P(("dp", "seq")),
        P(("dp", "seq")),
        P(("dp", "seq"), None),
        P(("dp", "seq"), None),
        P(("dp", "seq"), None),
        P(("dp", "seq"), None),
    )
    return jax.shard_map(fast_shards if fits(mesh) else general_shards, mesh=mesh, in_specs=in_specs, out_specs=out_specs, check_vma=False)
```

```python
import functools

import jax
import jax.numpy as jnp
from jax import lax
from jax.experimental import pallas as pl
from jax.experimental.pallas import tpu as pltpu
from jax.sharding import PartitionSpec as P

HEADS = 12
HD = 64
BUCKETS = 32


EPS = 1e-06
NEGATIVE = -1e30
bucket_limits = (12, 16, 23, 32, 46, 64, 91)


def bucket_of(relative):
    distance = jnp.abs(relative)
    counted = jnp.zeros_like(distance)
    for threshold in bucket_limits:
        counted = counted + (distance >= threshold).astype(jnp.int32)
    inside = jnp.where(distance < 8, distance, 8 + counted)
    return inside + 16 * (relative > 0).astype(jnp.int32)


def rms_scale(values):
    return lax.rsqrt(jnp.mean(values * values, axis=-1, keepdims=True) + EPS)


def smooth_gate(values):
    return jax.nn.gelu(values, approximate=True)


def norm_backward(values, scale_inv, gain_vec, grad_normed):
    weighted = grad_normed * gain_vec
    grad_gain = jnp.sum(grad_normed * values * scale_inv, axis=0)
    cubed = scale_inv * scale_inv * scale_inv
    grad_values = scale_inv * weighted - values * cubed * jnp.mean(
        weighted * values, axis=-1, keepdims=True
    )
    return (grad_values, grad_gain)


def group_scores(query_part, key_part, seg_query, seg_key, complete_bias):
    scores = (
        jnp.einsum("gqhd,gkhd->ghqk", query_part, key_part, preferred_element_type=jnp.float32)
        + complete_bias[None]
    )
    allowed = (seg_query[:, :, None] == seg_key[:, None, :])[:, None]
    return jnp.where(allowed, scores, NEGATIVE)


def query_backward(items, complete_bias):
    query_part, key_part, value_part, seg_query, seg_key, log_total, grad_part = items
    scores = group_scores(query_part, key_part, seg_query, seg_key, complete_bias)
    softmax_probabilities = jnp.exp(scores - log_total)
    grad_probs = jnp.einsum(
        "gqhd,gkhd->ghqk", grad_part, value_part, preferred_element_type=jnp.float32
    )
    row_inner = jnp.sum(softmax_probabilities * grad_probs, axis=-1, keepdims=True)
    grad_scores = (softmax_probabilities * (grad_probs - row_inner)).astype(jnp.bfloat16)
    grad_query = jnp.einsum(
        "ghqk,gkhd->gqhd", grad_scores, key_part, preferred_element_type=jnp.float32
    ).astype(jnp.bfloat16)
    return (softmax_probabilities, grad_scores, grad_query, row_inner)


def general_shards(
    tokens,
    segment_ids,
    valid_mask,
    cotangent,
    gain_one,
    gain_two,
    bias_table,
    qkv_weight,
    out_weight,
    in_weight,
    back_weight,
):
    gathered = (
        lax.all_gather(gain_one, ("dp", "seq"), axis=0, tiled=True),
        lax.all_gather(gain_two, ("dp", "seq"), axis=0, tiled=True),
        lax.all_gather(bias_table, ("dp", "seq"), axis=0, tiled=True),
        lax.all_gather(qkv_weight, ("dp", "seq"), axis=0, tiled=True),
        lax.all_gather(out_weight, ("dp", "seq"), axis=0, tiled=True),
        lax.all_gather(in_weight, ("dp", "seq"), axis=0, tiled=True),
        lax.all_gather(back_weight, ("dp", "seq"), axis=0, tiled=True),
    )
    gain_first, gain_second, table_flat, qkv_full, out_full, in_full, back_full = gathered
    seq_count, block_len, model_width = tokens.shape
    seq_len = block_len * lax.axis_size("seq")
    row_count = seq_count * block_len
    group_size = seq_count
    while group_size % 2 == 0 and group_size // 2 * block_len >= 512:
        group_size = group_size // 2
    group_count = seq_count // group_size
    flat_x = tokens.reshape(row_count, model_width).astype(jnp.float32)
    first_scale = rms_scale(flat_x)
    first_gain = gain_first.astype(jnp.float32)
    first_normed = (flat_x * first_scale * first_gain).astype(jnp.bfloat16)
    projected = jnp.dot(first_normed, qkv_full, preferred_element_type=jnp.float32).astype(
        jnp.bfloat16
    )
    queries = projected[:, :model_width].reshape(group_count, group_size, block_len, HEADS, HD)
    local_keys = projected[:, model_width : 2 * model_width].reshape(
        seq_count, block_len, model_width
    )
    local_values = projected[:, 2 * model_width :].reshape(seq_count, block_len, model_width)
    all_keys, all_values, all_segments = (
        lax.all_gather(local_keys, "seq", axis=1, tiled=True),
        lax.all_gather(local_values, "seq", axis=1, tiled=True),
        lax.all_gather(segment_ids, "seq", axis=1, tiled=True),
    )
    key_groups = all_keys.reshape(group_count, group_size, seq_len, HEADS, HD)
    value_groups = all_values.reshape(group_count, group_size, seq_len, HEADS, HD)
    segkey_groups = all_segments.reshape(group_count, group_size, seq_len)
    segquery_groups = segment_ids.reshape(group_count, group_size, block_len)
    offset = lax.axis_index("seq") * block_len
    query_places = offset + jnp.arange(block_len, dtype=jnp.int32)
    key_places = jnp.arange(seq_len, dtype=jnp.int32)
    buckets = bucket_of(key_places[None, :] - query_places[:, None])
    single_hot_vector = (
        buckets[None] == jnp.arange(BUCKETS, dtype=jnp.int32)[:, None, None]
    ).astype(jnp.bfloat16)
    bias_matrix = table_flat.reshape(BUCKETS, HEADS)
    complete_bias = jnp.einsum(
        "dto,dl->lto", single_hot_vector, bias_matrix, preferred_element_type=jnp.float32
    )

    def attend(group_items):
        query_part, key_part, value_part, seg_query, seg_key = group_items
        scores = group_scores(query_part, key_part, seg_query, seg_key, complete_bias)
        row_peak = jnp.max(scores, axis=-1, keepdims=True)
        shifted = jnp.exp(scores - row_peak)
        row_total = jnp.sum(shifted, axis=-1, keepdims=True)
        softmax_probabilities = (shifted / row_total).astype(jnp.bfloat16)
        attn_part = jnp.einsum(
            "ghqk,gkhd->gqhd", softmax_probabilities, value_part, preferred_element_type=jnp.float32
        )
        return (attn_part.astype(jnp.bfloat16), row_peak + jnp.log(row_total))

    attn_mixed, log_totals = lax.map(
        attend, (queries, key_groups, value_groups, segquery_groups, segkey_groups)
    )
    mixed_flat = attn_mixed.reshape(row_count, model_width)
    middle = flat_x + jnp.dot(mixed_flat, out_full, preferred_element_type=jnp.float32)
    second_scale = rms_scale(middle)
    second_gain = gain_second.astype(jnp.float32)
    second_normed = (middle * second_scale * second_gain).astype(jnp.bfloat16)
    hidden_pre = jnp.dot(second_normed, in_full, preferred_element_type=jnp.float32)
    hidden_float, gate_pullback = jax.vjp(smooth_gate, hidden_pre)
    hidden = hidden_float.astype(jnp.bfloat16)
    result = middle + jnp.dot(hidden, back_full, preferred_element_type=jnp.float32)
    output = result.astype(jnp.bfloat16).reshape(seq_count, block_len, model_width)
    grad_result = cotangent.reshape(row_count, model_width).astype(
        jnp.float32
    ) * valid_mask.reshape(row_count, 1).astype(jnp.float32)
    grad_branch = grad_result.astype(jnp.bfloat16)
    grad_back = jnp.einsum("tf,td->fd", hidden, grad_branch, preferred_element_type=jnp.float32)
    grad_hidden = jnp.einsum(
        "td,fd->tf", grad_branch, back_full, preferred_element_type=jnp.float32
    )
    grad_pre = gate_pullback(grad_hidden)[0].astype(jnp.bfloat16)
    grad_in = jnp.einsum("td,tf->df", second_normed, grad_pre, preferred_element_type=jnp.float32)
    grad_second_normed = jnp.einsum(
        "tf,df->td", grad_pre, in_full, preferred_element_type=jnp.float32
    )
    grad_middle_norm, grad_gain_second = norm_backward(
        middle, second_scale, second_gain, grad_second_normed
    )
    grad_middle = grad_result + grad_middle_norm
    grad_attn = grad_middle.astype(jnp.bfloat16)
    grad_out = jnp.einsum("td,te->de", mixed_flat, grad_attn, preferred_element_type=jnp.float32)
    grad_mixed = jnp.einsum(
        "te,de->td", grad_attn, out_full, preferred_element_type=jnp.float32
    ).astype(jnp.bfloat16)
    grad_mixed_groups = grad_mixed.reshape(group_count, group_size, block_len, HEADS, HD)
    backward_entries = (
        queries,
        key_groups,
        value_groups,
        segquery_groups,
        segkey_groups,
        log_totals,
        grad_mixed_groups,
    )
    bias_zero = jnp.zeros((HEADS, block_len, seq_len), jnp.float32)

    def full_backward(bias_total_sum, group_items):
        softmax_probabilities, grad_scores, grad_query, row_inner = query_backward(
            group_items, complete_bias
        )
        query_part = group_items[0]
        grad_part = group_items[6]
        key_gradient = jnp.einsum(
            "ghqk,gqhd->gkhd", grad_scores, query_part, preferred_element_type=jnp.float32
        )
        grad_value = jnp.einsum(
            "ghqk,gqhd->gkhd",
            softmax_probabilities.astype(jnp.bfloat16),
            grad_part,
            preferred_element_type=jnp.float32,
        )
        bias_total_sum = bias_total_sum + jnp.sum(grad_scores.astype(jnp.float32), axis=0)
        return (bias_total_sum, (grad_query, key_gradient, grad_value))

    bias_total_sum, (grad_queries, grad_keys, grad_values) = lax.scan(
        full_backward, bias_zero, backward_entries
    )
    key_terms = grad_keys.reshape(seq_count, seq_len, model_width)
    value_terms = grad_values.reshape(seq_count, seq_len, model_width)
    key_sum, value_sum = (
        lax.psum_scatter(
            key_terms.astype(jnp.bfloat16), "seq", scatter_dimension=1, tiled=True
        ).astype(jnp.float32),
        lax.psum_scatter(
            value_terms.astype(jnp.bfloat16), "seq", scatter_dimension=1, tiled=True
        ).astype(jnp.float32),
    )
    key_low = key_sum.astype(jnp.bfloat16)
    value_low = value_sum.astype(jnp.bfloat16)
    grad_projected = jnp.concatenate(
        [
            grad_queries.reshape(row_count, model_width),
            key_low.reshape(row_count, model_width),
            value_low.reshape(row_count, model_width),
        ],
        axis=1,
    )
    grad_qkv = jnp.einsum(
        "td,te->de", first_normed, grad_projected, preferred_element_type=jnp.float32
    )
    grad_first_normed = jnp.einsum(
        "te,de->td", grad_projected, qkv_full, preferred_element_type=jnp.float32
    )
    grad_x_norm, grad_gain_first = norm_backward(flat_x, first_scale, first_gain, grad_first_normed)
    grad_tokens = (
        (grad_middle + grad_x_norm).astype(jnp.bfloat16).reshape(seq_count, block_len, model_width)
    )
    grad_table = jnp.einsum(
        "fuy,suy->fs",
        single_hot_vector.astype(jnp.float32),
        bias_total_sum,
        precision=lax.Precision.HIGHEST,
    ).reshape(BUCKETS * HEADS)
    owned = (
        lax.psum_scatter(grad_gain_first, ("dp", "seq"), scatter_dimension=0, tiled=True),
        lax.psum_scatter(grad_gain_second, ("dp", "seq"), scatter_dimension=0, tiled=True),
        lax.psum_scatter(grad_table, ("dp", "seq"), scatter_dimension=0, tiled=True),
        lax.psum_scatter(grad_qkv, ("dp", "seq"), scatter_dimension=0, tiled=True),
        lax.psum_scatter(grad_out, ("dp", "seq"), scatter_dimension=0, tiled=True),
        lax.psum_scatter(grad_in, ("dp", "seq"), scatter_dimension=0, tiled=True),
        lax.psum_scatter(grad_back, ("dp", "seq"), scatter_dimension=0, tiled=True),
    )
    owned_gain_one, owned_gain_two, owned_table, owned_qkv, owned_out, owned_in, owned_back = owned
    return (
        output,
        grad_tokens,
        owned_gain_one,
        owned_gain_two,
        owned_table,
        owned_qkv,
        owned_out,
        owned_in,
        owned_back,
    )


MESH = pl.DeviceIdType.MESH

def flip(i, bit):
    return i + bit - 2 * bit * ((i // bit) % 2)

def gather_kernel(items, *refs):
    n_arr = 5
    tok, seg = refs[0], refs[1]
    shards = refs[2:2 + n_arr]
    xf, sf = refs[2 + n_arr], refs[3 + n_arr]
    full = refs[4 + n_arr:4 + 2 * n_arr]
    loc_sem, t_send, t_recv, s_send, s_recv, z_send, z_recv, h_send, h_recv = refs[4 + 2 * n_arr:]
    dp, z = lax.axis_index("dp"), lax.axis_index("seq")
    n_z = 4
    peers = [(dp, lax.rem(z + s, n_z)) for s in range(1, n_z)] + [(flip(dp, b), z) for b in (1, 2, 4)]
    barrier = pltpu.get_barrier_semaphore()
    for p in peers:
        pl.semaphore_signal(barrier, inc=1, device_id=p, device_id_type=MESH)
    pl.semaphore_wait(barrier, len(peers))

    def block(it, d, zz):
        return full[items[it][0]].at[d * n_z + zz]

    def own(it):
        return shards[items[it][0]]

    n_it = len(items)
    def z_copy(it, way, step):
        src_z = z - step if way == 0 else z + step
        src = own(it) if step == 0 else block(it, dp, src_z)
        return pltpu.make_async_remote_copy(
            src_ref=src, dst_ref=block(it, dp, src_z), send_sem=z_send.at[it, way, step],
            recv_sem=z_recv.at[it, way, step], device_id=(dp, z + 1 if way == 0 else z - 1), device_id_type=MESH)

    def z_wait(it, way, step):
        src_z = z - 1 - step if way == 0 else z + 1 + step
        blk = block(it, dp, src_z)
        pltpu.make_async_remote_copy(src_ref=blk, dst_ref=blk, send_sem=z_send.at[it, way, step],
            recv_sem=z_recv.at[it, way, step], device_id=(dp, z), device_id_type=MESH).wait_recv()

    def can_send(way, step):
        return (z >= step) & (z <= n_z - 2) if way == 0 else (z + step <= n_z - 1) & (z >= 1)

    def can_recv(way, step):
        return z >= step + 1 if way == 0 else z + 1 + step <= n_z - 1

    def z_start(it, step):
        for way in (0, 1):
            @pl.when(can_send(way, step))
            def _():
                z_copy(it, way, step).start()

    def z_recv_all(it, step):
        for way in (0, 1):
            @pl.when(can_recv(way, step))
            def _():
                z_wait(it, way, step)

    def hops(it):
        b1, b2 = items[it][1:]
        return [(0, b1), (0, b2), (b1, b2), (0, 1), (b1, 1), (b2, 1), (b1 + b2, 1)]

    def flips(d, mask):
        for b in (1, 2, 4):
            if mask & b:
                d = flip(d, b)
        return d

    def hop(it, slot, zz):
        mask, to = hops(it)[slot]
        blk = block(it, flips(dp, mask), zz)
        return pltpu.make_async_remote_copy(src_ref=blk, dst_ref=blk, send_sem=h_send.at[it, slot, zz],
            recv_sem=h_recv.at[it, slot, zz], device_id=(flip(dp, to), z), device_id_type=MESH)

    def hop_wait(it, slot, zz):
        mask, to = hops(it)[slot]
        blk = block(it, flips(dp, mask ^ to), zz)
        pltpu.make_async_remote_copy(src_ref=blk, dst_ref=blk, send_sem=h_send.at[it, slot, zz],
            recv_sem=h_recv.at[it, slot, zz], device_id=(dp, z), device_id_type=MESH).wait_recv()

    def own_hop(it, slot):
        to = hops(it)[slot][1]
        return pltpu.make_async_remote_copy(src_ref=own(it), dst_ref=block(it, dp, z), send_sem=h_send.at[it, slot, z],
            recv_sem=h_recv.at[it, slot, z], device_id=(flip(dp, to), z), device_id_type=MESH)

    def tok_copy(s):
        to = lax.rem(z + s, n_z)
        return [pltpu.make_async_remote_copy(src_ref=a.at[to], dst_ref=f.at[z], send_sem=ss.at[s - 1], recv_sem=rs.at[s - 1],
                device_id=(dp, to), device_id_type=MESH) for a, f, ss, rs in ((tok, xf, t_send, t_recv), (seg, sf, s_send, s_recv))]

    def tok_wait(s):
        frm = lax.rem(z + n_z - s, n_z)
        for f, ss, rs in ((xf, t_send, t_recv), (sf, s_send, s_recv)):
            pltpu.make_async_remote_copy(src_ref=f.at[frm], dst_ref=f.at[frm], send_sem=ss.at[s - 1], recv_sem=rs.at[s - 1],
                device_id=(dp, z), device_id_type=MESH).wait_recv()

    for it in range(n_it):
        z_start(it, 0)
        for slot in (0, 1, 3):
            own_hop(it, slot).start()
    locs = []
    for it in range(n_it):
        locs.append(pltpu.make_async_copy(own(it), block(it, dp, z), loc_sem.at[it]))
    locs.append(pltpu.make_async_copy(tok.at[z], xf.at[z], loc_sem.at[n_it]))
    locs.append(pltpu.make_async_copy(seg.at[z], sf.at[z], loc_sem.at[n_it + 1]))
    for c in locs:
        c.start()

    def forward(it, zz):
        hop_wait(it, 0, zz)
        hop(it, 2, zz).start()
        hop(it, 4, zz).start()
        hop_wait(it, 1, zz)
        hop(it, 5, zz).start()

    def arrivals(step):
        return [(can_recv(0, step), 0, z - 1 - step), (can_recv(1, step), 1, z + 1 + step)]

    for step in range(n_z):
        if step < n_z - 1:
            for it in range(n_it):
                for ok, way, zz in arrivals(step):
                    @pl.when(ok)
                    def _():
                        z_wait(it, way, step)
                        if step < n_z - 2:
                            @pl.when(can_send(way, step + 1))
                            def _():
                                z_copy(it, way, step + 1).start()
                        for slot in (0, 1, 3):
                            hop(it, slot, zz).start()
        if step == 1:
            for s in range(1, n_z):
                for c in tok_copy(s):
                    c.start()
        for it in range(n_it):
            if step == 0:
                forward(it, z)
            else:
                for ok, way, zz in arrivals(step - 1):
                    @pl.when(ok)
                    def _():
                        forward(it, zz)
    for zz in range(n_z):
        for it in range(n_it):
            hop_wait(it, 2, zz)
            hop(it, 6, zz).start()
    for s in range(1, n_z):
        tok_wait(s)
    for zz in range(n_z):
        for it in range(n_it):
            for slot in (3, 4, 5, 6):
                hop_wait(it, slot, zz)
    for c in locs:
        c.wait()
    for it in range(n_it):
        for step in range(n_z - 1):
            for way in (0, 1):
                @pl.when(can_send(way, step))
                def _():
                    z_copy(it, way, step).wait_send()
        for zz in range(n_z):
            for slot in range(7):
                hop(it, slot, zz).wait_send()
    for s in range(1, n_z):
        for c in tok_copy(s):
            c.wait_send()

def gather(tokens, seg, shards, items, collective_id=0):
    n_it = len(items)
    D = pltpu.SemaphoreType.DMA
    out_shape = [jax.ShapeDtypeStruct(tokens.shape, tokens.dtype), jax.ShapeDtypeStruct(seg.shape, seg.dtype)]
    out_shape += [jax.ShapeDtypeStruct((32, *s.shape), s.dtype) for s in shards]
    anyspec = pl.BlockSpec(memory_space=pltpu.HBM)
    return pl.pallas_call(
        functools.partial(gather_kernel, items),
        out_shape=out_shape,
        in_specs=[pl.BlockSpec(memory_space=pltpu.VMEM)] * (2 + len(shards)),
        out_specs=[anyspec] * len(out_shape),
        scratch_shapes=[D((n_it + 2,)), D((3,)), D((3,)), D((3,)), D((3,)), D((n_it, 2, 3)), D((n_it, 2, 3)), D((n_it, 7, 4)), D((n_it, 7, 4))],
        compiler_params=pltpu.CompilerParams(collective_id=collective_id, has_side_effects=True),
    )(tokens, seg, *shards)


LOG2E = 1.4426950408889634
BIG = -1e30
F32 = jnp.float32
BF = jnp.bfloat16

def extras(seg):
    L = seg.shape[0]
    nb = L.bit_length()
    nblk = L // 128
    lane = jnp.arange(128)[None, :] % 64
    row_blk = (jnp.arange(L) // 128)[:, None]
    b = lane - (nblk + 3)
    inb = (b >= 0) & (b < 2 * nb)
    bit = (seg[:, None] >> (jnp.clip(b, 0, 2 * nb - 1) // 2)) & 1
    flip = b % 2
    u = jnp.where(inb, (bit ^ flip), 0).astype(BF)
    w = jnp.where(inb & ((bit ^ flip) == 0), BIG, 0.0)
    onehot = (lane < nblk) & (lane == row_blk)
    ones = (lane >= nblk) & (lane < nblk + 3)
    exk = (w + (onehot | ones)).astype(BF)
    farl = ((lane < nblk) & (lane <= row_blk - 2)).astype(BF)
    farr = ((lane < nblk) & (lane >= row_blk + 2)).astype(BF)
    return u, exk, farl, farr

def diagonals(table):
    m = jnp.arange(512)
    rel = jnp.concatenate([(m + 127) % 512 - 255, 128 - m + 512 * (m >= 384)])
    hot = (bucket_of(rel)[:, None] == jnp.arange(table.shape[0])[None, :]).astype(BF)
    vec = jnp.dot(hot, table.astype(BF), preferred_element_type=F32)
    pair = vec.reshape(2, 512, -1, 2).transpose(2, 0, 3, 1).reshape(-1, 4, 512)
    return jnp.pad(pair, ((0, 0), (0, 4), (0, 0)))


def skewed(row):
    return pltpu.roll(jnp.broadcast_to(row, (128, 512)), 0, 1, stride=1, stride_axis=0)[:, :384]


def diagonal_sums(near):
    rows = 64
    x = jnp.concatenate([near, jnp.zeros((128, 128), F32)], axis=1)
    while rows >= 1:
        x = x[:rows] + pltpu.roll(x[rows:], 512 - rows, 1)
        rows //= 2
    return x


def fwd_kernel(nblk, bl_ref, q_ref, k_ref, v_ref, exq_ref, exk_ref, fl_ref, fr_ref, strip_ref, o_ref, qa_ref):
    L = q_ref.shape[0]
    hp = pl.program_id(0)
    lane = lax.broadcasted_iota(jnp.int32, (L, 128), 1)
    QB = 256
    outs = []
    for h in range(2):
        sel = (lane < 64) if h == 0 else (lane >= 64)
        strip = skewed(strip_ref[0, h:h + 1])
        bl = bl_ref[hp * 2 + h, 0].astype(BF); br = bl_ref[hp * 2 + h, 1].astype(BF)
        qa = jnp.where(sel, q_ref[...], exq_ref[...] + fl_ref[...] * bl + fr_ref[...] * br)
        ka = jnp.where(sel, k_ref[...], exk_ref[...])
        va = jnp.where(sel, v_ref[...], jnp.ones((L, 128), BF))
        lane_l = 64 * (1 - h)
        for blk in range(L // QB):
            r0 = blk * QB
            qb = qa[r0:r0 + QB]
            s = lax.dot_general(qb, ka, (((1,), (1,)), ((), ())), preferred_element_type=F32)
            rows = []
            for sub in range(QB // 128):
                I = blk * (QB // 128) + sub
                lo = max(I - 1, 0); hi = min(I + 1, nblk - 1)
                srow = s[sub * 128:(sub + 1) * 128]
                parts = []
                if lo > 0: parts.append(srow[:, :lo * 128])
                parts.append(srow[:, lo * 128:(hi + 1) * 128] + strip[:, (lo - I + 1) * 128:(hi - I + 2) * 128])
                if hi < nblk - 1: parts.append(srow[:, (hi + 1) * 128:])
                rows.append(jnp.concatenate(parts, axis=1))
            s = jnp.concatenate(rows, axis=0)
            m = jnp.max(s, axis=1, keepdims=True)
            p = jnp.exp2((s - m) * LOG2E).astype(BF)
            o = jnp.dot(p, va, preferred_element_type=F32)
            l = o[:, lane_l:lane_l + 1]
            outs.append(o / l)
            lse = m + jnp.log(l)
            hi_ = (-lse).astype(BF); rest = -lse - hi_.astype(F32)
            mid = rest.astype(BF); low = (rest - mid.astype(F32)).astype(BF)
            base = 64 * (1 - h) + nblk
            ln = lane[:QB]
            qx = jnp.where(ln == base, hi_, jnp.where(ln == base + 1, mid, jnp.where(ln == base + 2, low, qb)))
            qa_ref[h, r0:r0 + QB, :] = qx
    n = L // QB
    for blk in range(n):
        o_ref[blk * QB:(blk + 1) * QB, :] = jnp.where(lane[:QB] < 64, outs[blk], outs[n + blk]).astype(BF)

def attn_fwd(qkv, ex, strip, far, interpret=False):
    L, W = qkv.shape
    D = W // 3
    H = D // HD
    npair = H // 2
    nblk = L // 128
    exq, exk, fl, fr = ex
    full = lambda: pl.BlockSpec((L, 128), lambda i: (0, 0))
    return pl.pallas_call(
        functools.partial(fwd_kernel, nblk),
        grid=(npair,),
        in_specs=[pl.BlockSpec(memory_space=pltpu.SMEM),
                  pl.BlockSpec((L, 128), lambda i: (0, i)),
                  pl.BlockSpec((L, 128), lambda i: (0, npair + i)),
                  pl.BlockSpec((L, 128), lambda i: (0, 2 * npair + i)),
                  full(), full(), full(), full(),
                  pl.BlockSpec((1, 8, 512), lambda i: (i, 0, 0))],
        out_specs=[pl.BlockSpec((L, 128), lambda i: (0, i)), pl.BlockSpec((2, L, 128), lambda i: (i, 0, 0))],
        out_shape=[jax.ShapeDtypeStruct((L, D), BF), jax.ShapeDtypeStruct((H, L, 128), BF)],
        compiler_params=pltpu.CompilerParams(vmem_limit_bytes=48 << 20),
        cost_estimate=pl.CostEstimate(flops=4 * L * L * D * 4, bytes_accessed=L * W * 4, transcendentals=L * L * H),
    )(far, qkv, qkv, qkv, exq, exk, fl, fr, strip)

def bwd_kernel(nblk, qa_ref, k_ref, v_ref, do_ref, o_ref, exk_ref, strip_ref,
               dq_ref, dk_ref, dv_ref, diag_ref):
    L = k_ref.shape[0]
    lane = lax.broadcasted_iota(jnp.int32, (L, 128), 1)
    KB = 256
    nsub = KB // 128
    prod = do_ref[...].astype(F32) * o_ref[...].astype(F32)
    dqs = []; dks = []; dvs = []
    for h in range(2):
        sel = (lane < 64) if h == 0 else (lane >= 64)
        other = 64 * (1 - h)
        qa = qa_ref[h]
        ka = jnp.where(sel, k_ref[...], exk_ref[...])
        va = jnp.where(sel, v_ref[...], ((lane >= other + nblk) & (lane < other + nblk + 3)).astype(BF))
        delta = -jnp.sum(jnp.where(sel, prod, 0.0), axis=1, keepdims=True)
        hi_ = delta.astype(BF); rest = delta - hi_.astype(F32)
        mid = rest.astype(BF); low = (rest - mid.astype(F32)).astype(BF)
        base = other + nblk
        doa = jnp.where(sel, do_ref[...], jnp.where(lane == base, hi_, jnp.where(lane == base + 1, mid, jnp.where(lane == base + 2, low, jnp.zeros((L, 128), BF)))))
        near = jnp.zeros((128, 384), F32)
        strip = skewed(strip_ref[0, 2 + h:3 + h])
        dqt = jnp.zeros((128, L), F32)
        for kb in range(L // KB):
            r0 = kb * KB
            kab = ka[r0:r0 + KB]
            s = lax.dot_general(kab, qa, (((1,), (1,)), ((), ())), preferred_element_type=F32)
            dp = lax.dot_general(va[r0:r0 + KB], doa, (((1,), (1,)), ((), ())), preferred_element_type=F32)
            prow = []; dsrow = []
            for sub in range(nsub):
                J = kb * nsub + sub
                lo = max(J - 1, 0); hi = min(J + 1, nblk - 1)
                srow = s[sub * 128:(sub + 1) * 128]
                parts = []
                if lo > 0: parts.append(srow[:, :lo * 128])
                parts.append(srow[:, lo * 128:(hi + 1) * 128] + strip[:, (lo - J + 1) * 128:(hi - J + 2) * 128])
                if hi < nblk - 1: parts.append(srow[:, (hi + 1) * 128:])
                srow = jnp.concatenate(parts, axis=1)
                p = jnp.exp2(srow * LOG2E)
                ds = p * dp[sub * 128:(sub + 1) * 128]
                nr = ds[:, lo * 128:(hi + 1) * 128]
                if lo > J - 1: nr = jnp.concatenate([jnp.zeros((128, 128), F32), nr], axis=1)
                if hi < J + 1: nr = jnp.concatenate([nr, jnp.zeros((128, 128), F32)], axis=1)
                near = near + nr
                prow.append(p.astype(BF)); dsrow.append(ds.astype(BF))
            pb = jnp.concatenate(prow, axis=0); dsb = jnp.concatenate(dsrow, axis=0)
            dvs.append(jnp.dot(pb, doa, preferred_element_type=F32))
            dks.append(jnp.dot(dsb, qa, preferred_element_type=F32))
            dqt = dqt + lax.dot_general(kab, dsb, (((0,), (0,)), ((), ())), preferred_element_type=F32)
        far = dqt[other:other + 8]
        key_block = lax.broadcasted_iota(jnp.int32, far.shape, 0)
        query_block = lax.broadcasted_iota(jnp.int32, far.shape, 1) // 128
        left = jnp.sum(jnp.where(key_block <= query_block - 2, far, 0.0))
        right = jnp.sum(jnp.where(key_block >= query_block + 2, far, 0.0))
        column = lax.broadcasted_iota(jnp.int32, (1, 512), 1)
        sums = diagonal_sums(near)
        diag_ref[0, h:h + 1] = sums + jnp.where(column == 383, left, 0.0) + jnp.where(column == 385, right, 0.0)
        dqs.append(dqt[64 * h:64 * h + 64])
    n = L // KB
    first = lane[:KB] < 64
    for kb in range(n):
        dk_ref[kb * KB:(kb + 1) * KB, :] = jnp.where(first, dks[kb], dks[n + kb]).astype(BF)
        dv_ref[kb * KB:(kb + 1) * KB, :] = jnp.where(first, dvs[kb], dvs[n + kb]).astype(BF)
    dq_ref[...] = jnp.concatenate(dqs, axis=0).T.astype(BF)

def attn_bwd(qa, qkv, do, o, exk, stripT):
    L, W = qkv.shape
    D = W // 3
    H = D // HD
    npair = H // 2
    nblk = L // 128
    col = lambda off: pl.BlockSpec((L, 128), lambda i: (0, off + i))
    return pl.pallas_call(
        functools.partial(bwd_kernel, nblk),
        grid=(npair,),
        in_specs=[pl.BlockSpec((2, L, 128), lambda i: (i, 0, 0)), col(npair), col(2 * npair), col(0), col(0),
                  pl.BlockSpec((L, 128), lambda i: (0, 0)), pl.BlockSpec((1, 8, 512), lambda i: (i, 0, 0))],
        out_specs=[col(0), col(0), col(0), pl.BlockSpec((1, 8, 512), lambda i: (i, 0, 0))],
        out_shape=[jax.ShapeDtypeStruct((L, D), BF)] * 3 + [jax.ShapeDtypeStruct((npair, 8, 512), F32)],
        compiler_params=pltpu.CompilerParams(vmem_limit_bytes=48 << 20),
        cost_estimate=pl.CostEstimate(flops=10 * L * L * D * 4, bytes_accessed=L * W * 6, transcendentals=L * L * H),
    )(qa, qkv, qkv, do, o, exk, stripT)


def table_sums(diag, buckets):
    m = jnp.arange(512)
    hot = (bucket_of(128 - m + 512 * (m >= 384))[:, None] == jnp.arange(buckets)[None, :]).astype(F32)
    sums = jnp.einsum("phm,mb->phb", diag[:, :2], hot, precision=lax.Precision.HIGHEST)
    return sums.reshape(-1, buckets).T


GELU_A = 0.7978845608028654
GELU_B = 0.044715


def mm(a, b, dims=((1,), (0,))):
    return lax.dot_general(a, b, (dims, ((), ())), preferred_element_type=F32)


def ffn_kernel(x_ref, mixed_ref, g_ref, gain_ref, wo_ref, wi_ref, wb_ref,
               out_ref, gm_ref, gmix_ref, dwo_ref, dwi_ref, dwb_ref, dgain_ref,
               mid_ref, h_ref, ht_ref, acc_ref, dh_ref):
    step = pl.program_id(0)
    rows = x_ref.shape[0]
    half = 256

    @pl.when(step == 0)
    def _():
        for r in range(0, rows, half):
            part = pl.ds(r, half)
            middle = x_ref[part].astype(F32) + mm(mixed_ref[part], wo_ref[...])
            mid_ref[part] = middle
            acc_ref[part] = middle
            scale = lax.rsqrt(jnp.mean(middle * middle, axis=-1, keepdims=True) + EPS)
            normed = (middle * scale * gain_ref[...]).astype(BF)
            h_ref[part] = normed
            ht_ref[:, part] = normed.T
            dh_ref[part] = jnp.zeros((half, x_ref.shape[1]), F32)

    gates = []
    hiddens = []
    for r in range(0, rows, half):
        part = pl.ds(r, half)
        pre = mm(h_ref[part], wi_ref[...])
        dhid = mm(g_ref[part], wb_ref[...], ((1,), (1,)))
        sq = pre * pre
        t = jnp.tanh(pre * (GELU_A + GELU_A * GELU_B * sq))
        half_t = 0.5 + 0.5 * t
        hidden = (pre * half_t).astype(BF)
        slope = half_t + pre * (0.5 - 0.5 * t * t) * (GELU_A + 3.0 * GELU_A * GELU_B * sq)
        dpre = (dhid * slope).astype(BF)
        acc_ref[part] += mm(hidden, wb_ref[...])
        dh_ref[part] += mm(dpre, wi_ref[...], ((1,), (1,)))
        hiddens.append(hidden)
        gates.append(dpre)
    dwi_ref[...] = mm(ht_ref[...], jnp.concatenate(gates, axis=0)).astype(BF)
    dwb_ref[...] = mm(jnp.concatenate(hiddens, axis=0), g_ref[...], ((0,), (0,))).astype(BF)

    @pl.when(step == pl.num_programs(0) - 1)
    def _():
        dgain = jnp.zeros((1, x_ref.shape[1]), F32)
        for r in range(0, rows, half):
            part = pl.ds(r, half)
            out_ref[part] = acc_ref[part].astype(BF)
            middle = mid_ref[part]
            dh = dh_ref[part]
            scale = lax.rsqrt(jnp.mean(middle * middle, axis=-1, keepdims=True) + EPS)
            dgain += jnp.sum(dh * (middle * scale), axis=0, keepdims=True)
            u = dh * gain_ref[...]
            inner = jnp.mean(u * middle, axis=-1, keepdims=True)
            gm = g_ref[part].astype(F32) + scale * u - middle * (scale * scale * scale * inner)
            gm_ref[part] = gm
            low = gm.astype(BF)
            h_ref[part] = low
            gmix_ref[part] = mm(low, wo_ref[...], ((1,), (1,))).astype(BF)
        dgain_ref[...] = dgain
        dwo_ref[...] = mm(mixed_ref[...], h_ref[...], ((0,), (0,))).astype(BF)


def ffn(x, mixed, g, gain, wo, wi, wb, chunk=512):
    rows, width = x.shape
    ff = wi.shape[1]
    whole = lambda s: pl.BlockSpec(s, lambda i: (0, 0), pipeline_mode=pl.Buffered(1))
    S = jax.ShapeDtypeStruct
    return pl.pallas_call(
        ffn_kernel,
        grid=(ff // chunk,),
        in_specs=[whole((rows, width))] * 3 + [whole((1, width)), whole((width, width)),
                  pl.BlockSpec((width, chunk), lambda i: (0, i)), pl.BlockSpec((chunk, width), lambda i: (i, 0))],
        out_specs=[whole((rows, width))] * 3 + [whole((width, width)), pl.BlockSpec((width, chunk), lambda i: (0, i)),
                   pl.BlockSpec((chunk, width), lambda i: (i, 0)), whole((1, width))],
        out_shape=[S((rows, width), BF), S((rows, width), F32), S((rows, width), BF), S((width, width), BF),
                   S((width, ff), BF), S((ff, width), BF), S((1, width), F32)],
        scratch_shapes=[pltpu.VMEM((rows, width), F32), pltpu.VMEM((rows, width), BF), pltpu.VMEM((width, rows), BF),
                        pltpu.VMEM((rows, width), F32), pltpu.VMEM((rows, width), F32)],
        compiler_params=pltpu.CompilerParams(vmem_limit_bytes=56 << 20),
        cost_estimate=pl.CostEstimate(flops=12 * rows * width * ff + 6 * rows * width * width, bytes_accessed=50 << 20, transcendentals=rows * ff),
    )(x, mixed, g, gain, wo, wi, wb)


def tail_kernel(dq_ref, dk_ref, dv_ref, x_ref, gm_ref, gain_ref, w_ref, gx_ref, dw_ref, dgain_ref, ht_ref):
    rows, width = x_ref.shape
    half = 256
    dgain = jnp.zeros((1, width), F32)
    for r in range(0, rows, half):
        part = pl.ds(r, half)
        x = x_ref[part].astype(F32)
        scale = lax.rsqrt(jnp.mean(x * x, axis=-1, keepdims=True) + EPS)
        ht_ref[:, part] = (x * scale * gain_ref[...]).astype(BF).T
        dh = sum(mm(d[part], w_ref[:, i * width:(i + 1) * width], ((1,), (1,))) for i, d in enumerate((dq_ref, dk_ref, dv_ref)))
        dgain += jnp.sum(dh * (x * scale), axis=0, keepdims=True)
        u = dh * gain_ref[...]
        inner = jnp.mean(u * x, axis=-1, keepdims=True)
        gx_ref[part] = (gm_ref[part] + scale * u - x * (scale * scale * scale * inner)).astype(BF)
    dgain_ref[...] = dgain
    for i, d in enumerate((dq_ref, dk_ref, dv_ref)):
        dw_ref[:, i * width:(i + 1) * width] = mm(ht_ref[...], d[...]).astype(BF)


def tail(dq, dk, dv, x, gm, gain, w):
    rows, width = x.shape
    S = jax.ShapeDtypeStruct
    return pl.pallas_call(
        tail_kernel,
        out_shape=[S((rows, width), BF), S((width, 3 * width), BF), S((1, width), F32)],
        scratch_shapes=[pltpu.VMEM((width, rows), BF)],
        compiler_params=pltpu.CompilerParams(vmem_limit_bytes=56 << 20),
        cost_estimate=pl.CostEstimate(flops=12 * rows * width * width, bytes_accessed=24 << 20, transcendentals=0),
    )(dq, dk, dv, x, gm, gain, w)


def scatter_kernel(chunks, n_arr, *refs):
    n_it = len(chunks)
    n_z = 4
    gx = refs[0]
    part = refs[1:1 + n_arr]
    gx_out = refs[1 + n_arr]
    outs = refs[2 + n_arr:2 + 2 * n_arr]
    scr = refs[2 + 2 * n_arr:]
    rc, r2, r1, zo, zu, zd = (scr[k * n_it:(k + 1) * n_it] for k in range(6))
    loc_sem, t_send, t_recv, c_send, c_recv, x2_send, x2_recv, x1_send, x1_recv, z_send, z_recv = scr[6 * n_it:]
    dp, z = lax.axis_index("dp"), lax.axis_index("seq")
    core = lax.rem(dp, 2)
    quad = dp // 2
    peers = [(dp, lax.rem(z + s, n_z)) for s in range(1, n_z)] + [(flip(dp, b), z) for b in (1, 2, 4)]
    barrier = pltpu.get_barrier_semaphore()
    for p in peers:
        pl.semaphore_signal(barrier, inc=1, device_id=p, device_id_type=MESH)
    pl.semaphore_wait(barrier, len(peers))

    def remote(src, dst, ss, rs, to):
        return pltpu.make_async_remote_copy(src_ref=src, dst_ref=dst, send_sem=ss, recv_sem=rs, device_id=to, device_id_type=MESH)

    def piece(it, d):
        a, c0, w = chunks[it][:3]
        return part[a].at[d, :, pl.ds(c0, w)]

    def add_into(dst, src, chunk=16):
        rows = dst.shape[0]
        chunk = min(chunk, rows)
        @pl.loop(0, rows // chunk)
        def _(i):
            at = pl.ds(pl.multiple_of(i * chunk, chunk), chunk)
            dst[at] = (dst[at].astype(F32) + src[at].astype(F32)).astype(dst.dtype)

    def q_at(it, f1, f2):
        b1, b2 = chunks[it][3:]
        q = quad
        if f1: q = flip(q, b1 // 2)
        if f2: q = flip(q, b2 // 2)
        return q

    def c_copy(it, q):
        return remote(piece(it, 2 * q + 1 - core), rc[it].at[q], c_send.at[it, q], c_recv.at[it, q], (flip(dp, 1), z))

    def x2_copy(it, f1):
        q = q_at(it, f1, True)
        k = (q // (chunks[it][3] // 2)) % 2
        return remote(rc[it].at[q], r2[it].at[k], x2_send.at[it, k], x2_recv.at[it, k], (flip(dp, chunks[it][4]), z))

    def x1_copy(it):
        return remote(rc[it].at[q_at(it, True, False)], r1[it], x1_send.at[it], x1_recv.at[it], (flip(dp, chunks[it][3]), z))

    def tok_copy(s):
        to = lax.rem(z + s, n_z)
        return remote(gx.at[to], gx_out.at[z], t_send.at[s - 1], t_recv.at[s - 1], (dp, to))

    def core_start(it):
        for f1, f2 in ((True, True), (False, True), (True, False), (False, False)):
            c_copy(it, q_at(it, f1, f2)).start()

    def core_sum(it, f1, f2):
        q = q_at(it, f1, f2)
        c_copy(it, q).wait_recv()
        add_into(rc[it].at[q], piece(it, 2 * q + core))

    def stage_core(it):
        for f1 in (True, False):
            core_sum(it, f1, True)
            x2_copy(it, f1).start()
        for f1 in (True, False):
            core_sum(it, f1, False)

    def stage_x2(it):
        for f1 in (True, False):
            q = q_at(it, f1, False)
            k = (q // (chunks[it][3] // 2)) % 2
            remote(rc[it].at[0], r2[it].at[k], x2_send.at[it, k], x2_recv.at[it, k], (dp, z)).wait_recv()
            add_into(rc[it].at[q], r2[it].at[k])
            if f1:
                x1_copy(it).start()

    def z_copy(it, way, j):
        src = zo[it].at[j]
        dst = (zu if way == 0 else zd)[it].at[j]
        return remote(src, dst, z_send.at[it, way, j], z_recv.at[it, way, j], (dp, z + 1 if way == 0 else z - 1))

    def z_add(it, way, j):
        buf = (zu if way == 0 else zd)[it]
        remote(buf.at[j], buf.at[j], z_send.at[it, way, j], z_recv.at[it, way, j], (dp, z)).wait_recv()
        zo[it][j] = (zo[it][j].astype(F32) + buf[j].astype(F32)).astype(zo[it].dtype)

    def stage_x1(it):
        x1_copy(it).wait_recv()
        rows = zo[it].shape[1]
        for j in range(n_z):
            at = pl.ds(j * rows, rows)
            zo[it][j] = (rc[it][quad, at].astype(F32) + r1[it][at].astype(F32)).astype(zo[it].dtype)
        stage_z(it, 0)

    def stage_z(it, s):
        for way, here in ((0, s), (1, n_z - 1 - s)):
            @pl.when(z == here)
            def _():
                for j in (range(n_z - 1, here, -1) if way == 0 else range(here)):
                    if s > 0:
                        z_add(it, way, j)
                    z_copy(it, way, j).start()

    def stage_end(it):
        a, c0, w = chunks[it][:3]
        col = pl.ds(c0, w)
        outs[a][:, col] = zo[it][z].astype(F32)
        for way, ok in ((0, z > 0), (1, z < n_z - 1)):
            @pl.when(ok)
            def _():
                buf = (zu if way == 0 else zd)[it].at[z]
                remote(buf, buf, z_send.at[it, way, z], z_recv.at[it, way, z], (dp, z)).wait_recv()
                outs[a][:, col] += buf[...].astype(F32)

    for it in range(n_it):
        core_start(it)
    loc = pltpu.make_async_copy(gx.at[z], gx_out.at[z], loc_sem.at[0])
    loc.start()
    stages = ((0, stage_core), (LAG, stage_x2), (2 * LAG, stage_x1), (2 * LAG + 1, functools.partial(stage_z, s=1)),
              (2 * LAG + 2, functools.partial(stage_z, s=2)), (2 * LAG + 3, stage_end))
    for t in range(n_it + 2 * LAG + 4):
        if t == 0:
            for s in range(1, n_z):
                tok_copy(s).start()
        for off, fn in stages:
            if 0 <= t - off < n_it:
                fn(t - off)
    for s in range(1, n_z ):
        frm = lax.rem(z + n_z - s, n_z)
        remote(gx_out.at[frm], gx_out.at[frm], t_send.at[s - 1], t_recv.at[s - 1], (dp, z)).wait_recv()
    loc.wait()
    for s in range(1, n_z ):
        tok_copy(s).wait_send()
    for it in range(n_it):
        for q in range(4):
            c_copy(it, q).wait_send()
        for f1 in (True, False):
            x2_copy(it, f1).wait_send()
        x1_copy(it).wait_send()
        for j in range(n_z):
            for way in (0, 1):
                @pl.when(j > z if way == 0 else j < z)
                def _():
                    z_copy(it, way, j).wait_send()

def scatter(gx, parts, chunks, collective_id=1):
    n_arr, n_it = len(parts), len(chunks)
    D = pltpu.SemaphoreType.DMA
    def V(c, *lead):
        p = parts[c[0]]
        return pltpu.VMEM((*lead, p.shape[1], c[2]), p.dtype)
    def zs(c):
        p = parts[c[0]]
        return pltpu.VMEM((4, p.shape[1] // 4, c[2]), p.dtype)
    vm = pl.BlockSpec(memory_space=pltpu.VMEM)
    scratch = [V(c, 4) for c in chunks] + [V(c, 2) for c in chunks] + [V(c) for c in chunks] + [zs(c) for c in chunks] * 3
    scratch += [D((1,)), D((3,)), D((3,)), D((n_it, 4)), D((n_it, 4)), D((n_it, 2)), D((n_it, 2)), D((n_it,)), D((n_it,)), D((n_it, 2, 4)), D((n_it, 2, 4))]
    return pl.pallas_call(
        functools.partial(scatter_kernel, chunks, n_arr),
        out_shape=[jax.ShapeDtypeStruct(gx.shape, gx.dtype)] + [jax.ShapeDtypeStruct((p.shape[1] // 4, p.shape[2]), F32) for p in parts],
        in_specs=[vm] * (1 + n_arr),
        out_specs=[pl.BlockSpec(memory_space=pltpu.HBM)] + [vm] * n_arr,
        scratch_shapes=scratch,
        compiler_params=pltpu.CompilerParams(collective_id=collective_id, has_side_effects=True, vmem_limit_bytes=56 << 20),
    )(gx, *parts)


def fits(mesh):
    return mesh.shape["dp"] == 8 and mesh.shape["seq"] == 4


ITEMS = ((0, 4, 2), (4, 2, 4), (1, 2, 4), (2, 4, 2), (3, 2, 4))
ROUTES = (
    (1, 0, 128, 2, 4),
    (2, 0, 384, 4, 2),
    (2, 384, 384, 2, 4),
    (3, 0, 1536, 4, 2),
    (3, 1536, 1536, 2, 4),
    (4, 0, 384, 4, 2),
    (4, 384, 384, 2, 4),
    (0, 0, 1152, 4, 2),
    (0, 1152, 1152, 2, 4),
)
LAG = 2


def fast_shards(
    tokens,
    segment_ids,
    valid_mask,
    cotangent,
    gain_one,
    gain_two,
    bias_table,
    qkv_weight,
    out_weight,
    in_weight,
    back_weight,
):
    n_z = lax.axis_size("seq")
    seq_count, block_len, width = tokens.shape
    seq_len = n_z * block_len
    n_dev = n_z * lax.axis_size("dp")
    g_rows, t_rows = gain_one.shape[0], bias_table.shape[0]
    small = jnp.concatenate([gain_one, gain_two, bias_table])
    small = jnp.pad(small[None], ((0, 7), (0, 128 - small.shape[0])))
    grad_local = cotangent * valid_mask[..., None].astype(BF)
    x4, seg4, qkv_full, out_full, in_full, back_full, small_full = gather(
        tokens,
        segment_ids.reshape(seq_count, 1, block_len),
        (qkv_weight, out_weight, in_weight, back_weight, small),
        ITEMS,
    )
    qkv_full = qkv_full.reshape(width, 3 * width)
    out_full = out_full.reshape(width, width)
    in_full = in_full.reshape(width, -1)
    back_full = back_full.reshape(-1, width)
    small_full = small_full[:, 0]
    gain_first = small_full[:, :g_rows].reshape(1, width).astype(F32)
    gain_second = small_full[:, g_rows : 2 * g_rows].reshape(1, width).astype(F32)
    table = small_full[:, 2 * g_rows : 2 * g_rows + t_rows].reshape(BUCKETS, HEADS)
    grad_local, x4 = lax.optimization_barrier((grad_local, x4))
    g_low = lax.all_to_all(grad_local, "seq", 0, 1, tiled=True).reshape(seq_len, width)
    x = x4.reshape(seq_len, width)
    flat_x = x.astype(F32)
    seg = seg4.reshape(seq_len)
    exq, exk, far_left, far_right = extras(seg)
    bias_rows = diagonals(table.astype(F32))
    far = jnp.stack([table[BUCKETS // 2 - 1], table[BUCKETS - 1]], axis=1).astype(F32)
    first_normed = (flat_x * rms_scale(flat_x) * gain_first).astype(BF)
    projected = jnp.dot(first_normed, qkv_full, preferred_element_type=F32).astype(BF)
    mixed, q_aug = attn_fwd(projected, (exq, exk, far_left, far_right), bias_rows, far)
    result, grad_middle, grad_mixed, grad_out, grad_in, grad_back, grad_gain_second = ffn(
        x, mixed, g_low, gain_second, out_full, in_full, back_full
    )
    output = lax.all_to_all(
        result.reshape(n_z, block_len, width), "seq", 0, 0, tiled=True
    )
    dq, dk, dv, diag = attn_bwd(q_aug, projected, grad_mixed, mixed, exk, bias_rows)
    grad_x, grad_qkv, grad_gain_first = tail(dq, dk, dv, x, grad_middle, gain_first, qkv_full)
    grad_table = table_sums(diag, BUCKETS)
    small_grad = jnp.concatenate(
        [
            grad_gain_first.reshape(n_dev, g_rows),
            grad_gain_second.reshape(n_dev, g_rows),
            grad_table.reshape(n_dev, t_rows),
        ],
        axis=1,
    )
    small_grad = jnp.pad(small_grad[:, None], ((0, 0), (0, 7), (0, 128 - small_grad.shape[1])))
    parts = (grad_qkv, small_grad.reshape(n_dev * 8, 128), grad_out, grad_in, grad_back)
    grad_tokens, own_qkv, own_small, own_out, own_in, own_back = scatter(
        grad_x.reshape(n_z, block_len, width),
        [p.reshape(8, -1, p.shape[1]) for p in parts],
        ROUTES,
    )
    own_small = own_small[0]
    return (
        output,
        grad_tokens,
        own_small[:g_rows],
        own_small[g_rows : 2 * g_rows],
        own_small[2 * g_rows : 2 * g_rows + t_rows],
        own_qkv,
        own_out,
        own_in,
        own_back,
    )


def solution(mesh):
    in_specs = (
        P("dp", "seq", None),
        P("dp", "seq"),
        P("dp", "seq"),
        P("dp", "seq", None),
        P(("dp", "seq")),
        P(("dp", "seq")),
        P(("dp", "seq")),
        P(("dp", "seq"), None),
        P(("dp", "seq"), None),
        P(("dp", "seq"), None),
        P(("dp", "seq"), None),
    )
    out_specs = (
        P("dp", "seq", None),
        P("dp", "seq", None),
        P(("dp", "seq")),
        P(("dp", "seq")),
        P(("dp", "seq")),
        P(("dp", "seq"), None),
        P(("dp", "seq"), None),
        P(("dp", "seq"), None),
        P(("dp", "seq"), None),
    )
    return jax.shard_map(fast_shards if fits(mesh) else general_shards, mesh=mesh, in_specs=in_specs, out_specs=out_specs, check_vma=False)
```

```python
import functools

import jax
import jax.numpy as jnp
from jax import lax
from jax.experimental import pallas as pl
from jax.experimental.pallas import tpu as pltpu
from jax.sharding import PartitionSpec as P

HEADS = 12
HD = 64
BUCKETS = 32


EPS = 1e-06
NEGATIVE = -1e30
bucket_limits = (12, 16, 23, 32, 46, 64, 91)


def bucket_of(relative):
    distance = jnp.abs(relative)
    counted = jnp.zeros_like(distance)
    for threshold in bucket_limits:
        counted = counted + (distance >= threshold).astype(jnp.int32)
    inside = jnp.where(distance < 8, distance, 8 + counted)
    return inside + 16 * (relative > 0).astype(jnp.int32)


def rms_scale(values):
    return lax.rsqrt(jnp.mean(values * values, axis=-1, keepdims=True) + EPS)


def smooth_gate(values):
    return jax.nn.gelu(values, approximate=True)


def norm_backward(values, scale_inv, gain_vec, grad_normed):
    weighted = grad_normed * gain_vec
    grad_gain = jnp.sum(grad_normed * values * scale_inv, axis=0)
    cubed = scale_inv * scale_inv * scale_inv
    grad_values = scale_inv * weighted - values * cubed * jnp.mean(
        weighted * values, axis=-1, keepdims=True
    )
    return (grad_values, grad_gain)


def group_scores(query_part, key_part, seg_query, seg_key, complete_bias):
    scores = (
        jnp.einsum("gqhd,gkhd->ghqk", query_part, key_part, preferred_element_type=jnp.float32)
        + complete_bias[None]
    )
    allowed = (seg_query[:, :, None] == seg_key[:, None, :])[:, None]
    return jnp.where(allowed, scores, NEGATIVE)


def query_backward(items, complete_bias):
    query_part, key_part, value_part, seg_query, seg_key, log_total, grad_part = items
    scores = group_scores(query_part, key_part, seg_query, seg_key, complete_bias)
    softmax_probabilities = jnp.exp(scores - log_total)
    grad_probs = jnp.einsum(
        "gqhd,gkhd->ghqk", grad_part, value_part, preferred_element_type=jnp.float32
    )
    row_inner = jnp.sum(softmax_probabilities * grad_probs, axis=-1, keepdims=True)
    grad_scores = (softmax_probabilities * (grad_probs - row_inner)).astype(jnp.bfloat16)
    grad_query = jnp.einsum(
        "ghqk,gkhd->gqhd", grad_scores, key_part, preferred_element_type=jnp.float32
    ).astype(jnp.bfloat16)
    return (softmax_probabilities, grad_scores, grad_query, row_inner)


def general_shards(
    tokens,
    segment_ids,
    valid_mask,
    cotangent,
    gain_one,
    gain_two,
    bias_table,
    qkv_weight,
    out_weight,
    in_weight,
    back_weight,
):
    gathered = (
        lax.all_gather(gain_one, ("dp", "seq"), axis=0, tiled=True),
        lax.all_gather(gain_two, ("dp", "seq"), axis=0, tiled=True),
        lax.all_gather(bias_table, ("dp", "seq"), axis=0, tiled=True),
        lax.all_gather(qkv_weight, ("dp", "seq"), axis=0, tiled=True),
        lax.all_gather(out_weight, ("dp", "seq"), axis=0, tiled=True),
        lax.all_gather(in_weight, ("dp", "seq"), axis=0, tiled=True),
        lax.all_gather(back_weight, ("dp", "seq"), axis=0, tiled=True),
    )
    gain_first, gain_second, table_flat, qkv_full, out_full, in_full, back_full = gathered
    seq_count, block_len, model_width = tokens.shape
    seq_len = block_len * lax.axis_size("seq")
    row_count = seq_count * block_len
    group_size = seq_count
    while group_size % 2 == 0 and group_size // 2 * block_len >= 512:
        group_size = group_size // 2
    group_count = seq_count // group_size
    flat_x = tokens.reshape(row_count, model_width).astype(jnp.float32)
    first_scale = rms_scale(flat_x)
    first_gain = gain_first.astype(jnp.float32)
    first_normed = (flat_x * first_scale * first_gain).astype(jnp.bfloat16)
    projected = jnp.dot(first_normed, qkv_full, preferred_element_type=jnp.float32).astype(
        jnp.bfloat16
    )
    queries = projected[:, :model_width].reshape(group_count, group_size, block_len, HEADS, HD)
    local_keys = projected[:, model_width : 2 * model_width].reshape(
        seq_count, block_len, model_width
    )
    local_values = projected[:, 2 * model_width :].reshape(seq_count, block_len, model_width)
    all_keys, all_values, all_segments = (
        lax.all_gather(local_keys, "seq", axis=1, tiled=True),
        lax.all_gather(local_values, "seq", axis=1, tiled=True),
        lax.all_gather(segment_ids, "seq", axis=1, tiled=True),
    )
    key_groups = all_keys.reshape(group_count, group_size, seq_len, HEADS, HD)
    value_groups = all_values.reshape(group_count, group_size, seq_len, HEADS, HD)
    segkey_groups = all_segments.reshape(group_count, group_size, seq_len)
    segquery_groups = segment_ids.reshape(group_count, group_size, block_len)
    offset = lax.axis_index("seq") * block_len
    query_places = offset + jnp.arange(block_len, dtype=jnp.int32)
    key_places = jnp.arange(seq_len, dtype=jnp.int32)
    buckets = bucket_of(key_places[None, :] - query_places[:, None])
    single_hot_vector = (
        buckets[None] == jnp.arange(BUCKETS, dtype=jnp.int32)[:, None, None]
    ).astype(jnp.bfloat16)
    bias_matrix = table_flat.reshape(BUCKETS, HEADS)
    complete_bias = jnp.einsum(
        "dto,dl->lto", single_hot_vector, bias_matrix, preferred_element_type=jnp.float32
    )

    def attend(group_items):
        query_part, key_part, value_part, seg_query, seg_key = group_items
        scores = group_scores(query_part, key_part, seg_query, seg_key, complete_bias)
        row_peak = jnp.max(scores, axis=-1, keepdims=True)
        shifted = jnp.exp(scores - row_peak)
        row_total = jnp.sum(shifted, axis=-1, keepdims=True)
        softmax_probabilities = (shifted / row_total).astype(jnp.bfloat16)
        attn_part = jnp.einsum(
            "ghqk,gkhd->gqhd", softmax_probabilities, value_part, preferred_element_type=jnp.float32
        )
        return (attn_part.astype(jnp.bfloat16), row_peak + jnp.log(row_total))

    attn_mixed, log_totals = lax.map(
        attend, (queries, key_groups, value_groups, segquery_groups, segkey_groups)
    )
    mixed_flat = attn_mixed.reshape(row_count, model_width)
    middle = flat_x + jnp.dot(mixed_flat, out_full, preferred_element_type=jnp.float32)
    second_scale = rms_scale(middle)
    second_gain = gain_second.astype(jnp.float32)
    second_normed = (middle * second_scale * second_gain).astype(jnp.bfloat16)
    hidden_pre = jnp.dot(second_normed, in_full, preferred_element_type=jnp.float32)
    hidden_float, gate_pullback = jax.vjp(smooth_gate, hidden_pre)
    hidden = hidden_float.astype(jnp.bfloat16)
    result = middle + jnp.dot(hidden, back_full, preferred_element_type=jnp.float32)
    output = result.astype(jnp.bfloat16).reshape(seq_count, block_len, model_width)
    grad_result = cotangent.reshape(row_count, model_width).astype(
        jnp.float32
    ) * valid_mask.reshape(row_count, 1).astype(jnp.float32)
    grad_branch = grad_result.astype(jnp.bfloat16)
    grad_back = jnp.einsum("tf,td->fd", hidden, grad_branch, preferred_element_type=jnp.float32)
    grad_hidden = jnp.einsum(
        "td,fd->tf", grad_branch, back_full, preferred_element_type=jnp.float32
    )
    grad_pre = gate_pullback(grad_hidden)[0].astype(jnp.bfloat16)
    grad_in = jnp.einsum("td,tf->df", second_normed, grad_pre, preferred_element_type=jnp.float32)
    grad_second_normed = jnp.einsum(
        "tf,df->td", grad_pre, in_full, preferred_element_type=jnp.float32
    )
    grad_middle_norm, grad_gain_second = norm_backward(
        middle, second_scale, second_gain, grad_second_normed
    )
    grad_middle = grad_result + grad_middle_norm
    grad_attn = grad_middle.astype(jnp.bfloat16)
    grad_out = jnp.einsum("td,te->de", mixed_flat, grad_attn, preferred_element_type=jnp.float32)
    grad_mixed = jnp.einsum(
        "te,de->td", grad_attn, out_full, preferred_element_type=jnp.float32
    ).astype(jnp.bfloat16)
    grad_mixed_groups = grad_mixed.reshape(group_count, group_size, block_len, HEADS, HD)
    backward_entries = (
        queries,
        key_groups,
        value_groups,
        segquery_groups,
        segkey_groups,
        log_totals,
        grad_mixed_groups,
    )
    bias_zero = jnp.zeros((HEADS, block_len, seq_len), jnp.float32)

    def full_backward(bias_total_sum, group_items):
        softmax_probabilities, grad_scores, grad_query, row_inner = query_backward(
            group_items, complete_bias
        )
        query_part = group_items[0]
        grad_part = group_items[6]
        key_gradient = jnp.einsum(
            "ghqk,gqhd->gkhd", grad_scores, query_part, preferred_element_type=jnp.float32
        )
        grad_value = jnp.einsum(
            "ghqk,gqhd->gkhd",
            softmax_probabilities.astype(jnp.bfloat16),
            grad_part,
            preferred_element_type=jnp.float32,
        )
        bias_total_sum = bias_total_sum + jnp.sum(grad_scores.astype(jnp.float32), axis=0)
        return (bias_total_sum, (grad_query, key_gradient, grad_value))

    bias_total_sum, (grad_queries, grad_keys, grad_values) = lax.scan(
        full_backward, bias_zero, backward_entries
    )
    key_terms = grad_keys.reshape(seq_count, seq_len, model_width)
    value_terms = grad_values.reshape(seq_count, seq_len, model_width)
    key_sum, value_sum = (
        lax.psum_scatter(
            key_terms.astype(jnp.bfloat16), "seq", scatter_dimension=1, tiled=True
        ).astype(jnp.float32),
        lax.psum_scatter(
            value_terms.astype(jnp.bfloat16), "seq", scatter_dimension=1, tiled=True
        ).astype(jnp.float32),
    )
    key_low = key_sum.astype(jnp.bfloat16)
    value_low = value_sum.astype(jnp.bfloat16)
    grad_projected = jnp.concatenate(
        [
            grad_queries.reshape(row_count, model_width),
            key_low.reshape(row_count, model_width),
            value_low.reshape(row_count, model_width),
        ],
        axis=1,
    )
    grad_qkv = jnp.einsum(
        "td,te->de", first_normed, grad_projected, preferred_element_type=jnp.float32
    )
    grad_first_normed = jnp.einsum(
        "te,de->td", grad_projected, qkv_full, preferred_element_type=jnp.float32
    )
    grad_x_norm, grad_gain_first = norm_backward(flat_x, first_scale, first_gain, grad_first_normed)
    grad_tokens = (
        (grad_middle + grad_x_norm).astype(jnp.bfloat16).reshape(seq_count, block_len, model_width)
    )
    grad_table = jnp.einsum(
        "fuy,suy->fs",
        single_hot_vector.astype(jnp.float32),
        bias_total_sum,
        precision=lax.Precision.HIGHEST,
    ).reshape(BUCKETS * HEADS)
    owned = (
        lax.psum_scatter(grad_gain_first, ("dp", "seq"), scatter_dimension=0, tiled=True),
        lax.psum_scatter(grad_gain_second, ("dp", "seq"), scatter_dimension=0, tiled=True),
        lax.psum_scatter(grad_table, ("dp", "seq"), scatter_dimension=0, tiled=True),
        lax.psum_scatter(grad_qkv, ("dp", "seq"), scatter_dimension=0, tiled=True),
        lax.psum_scatter(grad_out, ("dp", "seq"), scatter_dimension=0, tiled=True),
        lax.psum_scatter(grad_in, ("dp", "seq"), scatter_dimension=0, tiled=True),
        lax.psum_scatter(grad_back, ("dp", "seq"), scatter_dimension=0, tiled=True),
    )
    owned_gain_one, owned_gain_two, owned_table, owned_qkv, owned_out, owned_in, owned_back = owned
    return (
        output,
        grad_tokens,
        owned_gain_one,
        owned_gain_two,
        owned_table,
        owned_qkv,
        owned_out,
        owned_in,
        owned_back,
    )


MESH = pl.DeviceIdType.MESH

def flip(i, bit):
    return i + bit - 2 * bit * ((i // bit) % 2)

def gather_kernel(items, *refs):
    n_arr = 5
    tok, seg = refs[0], refs[1]
    shards = refs[2:2 + n_arr]
    xf, sf = refs[2 + n_arr], refs[3 + n_arr]
    full = refs[4 + n_arr:4 + 2 * n_arr]
    loc_sem, t_send, t_recv, s_send, s_recv, z_send, z_recv, h_send, h_recv = refs[4 + 2 * n_arr:]
    dp, z = lax.axis_index("dp"), lax.axis_index("seq")
    n_z = 4
    peers = [(dp, lax.rem(z + s, n_z)) for s in range(1, n_z)] + [(flip(dp, b), z) for b in (1, 2, 4)]
    barrier = pltpu.get_barrier_semaphore()
    for p in peers:
        pl.semaphore_signal(barrier, inc=1, device_id=p, device_id_type=MESH)
    pl.semaphore_wait(barrier, len(peers))

    def block(it, d, zz):
        return full[items[it][0]].at[d * n_z + zz]

    def own(it):
        return shards[items[it][0]]

    n_it = len(items)
    def z_copy(it, way, step):
        src_z = z - step if way == 0 else z + step
        src = own(it) if step == 0 else block(it, dp, src_z)
        return pltpu.make_async_remote_copy(
            src_ref=src, dst_ref=block(it, dp, src_z), send_sem=z_send.at[it, way, step],
            recv_sem=z_recv.at[it, way, step], device_id=(dp, z + 1 if way == 0 else z - 1), device_id_type=MESH)

    def z_wait(it, way, step):
        src_z = z - 1 - step if way == 0 else z + 1 + step
        blk = block(it, dp, src_z)
        pltpu.make_async_remote_copy(src_ref=blk, dst_ref=blk, send_sem=z_send.at[it, way, step],
            recv_sem=z_recv.at[it, way, step], device_id=(dp, z), device_id_type=MESH).wait_recv()

    def can_send(way, step):
        return (z >= step) & (z <= n_z - 2) if way == 0 else (z + step <= n_z - 1) & (z >= 1)

    def can_recv(way, step):
        return z >= step + 1 if way == 0 else z + 1 + step <= n_z - 1

    def z_start(it, step):
        for way in (0, 1):
            @pl.when(can_send(way, step))
            def _():
                z_copy(it, way, step).start()

    def z_recv_all(it, step):
        for way in (0, 1):
            @pl.when(can_recv(way, step))
            def _():
                z_wait(it, way, step)

    def hops(it):
        b1, b2 = items[it][1:]
        return [(0, b1), (0, b2), (b1, b2), (0, 1), (b1, 1), (b2, 1), (b1 + b2, 1)]

    def flips(d, mask):
        for b in (1, 2, 4):
            if mask & b:
                d = flip(d, b)
        return d

    def hop(it, slot, zz):
        mask, to = hops(it)[slot]
        blk = block(it, flips(dp, mask), zz)
        return pltpu.make_async_remote_copy(src_ref=blk, dst_ref=blk, send_sem=h_send.at[it, slot, zz],
            recv_sem=h_recv.at[it, slot, zz], device_id=(flip(dp, to), z), device_id_type=MESH)

    def hop_wait(it, slot, zz):
        mask, to = hops(it)[slot]
        blk = block(it, flips(dp, mask ^ to), zz)
        pltpu.make_async_remote_copy(src_ref=blk, dst_ref=blk, send_sem=h_send.at[it, slot, zz],
            recv_sem=h_recv.at[it, slot, zz], device_id=(dp, z), device_id_type=MESH).wait_recv()

    def own_hop(it, slot):
        to = hops(it)[slot][1]
        return pltpu.make_async_remote_copy(src_ref=own(it), dst_ref=block(it, dp, z), send_sem=h_send.at[it, slot, z],
            recv_sem=h_recv.at[it, slot, z], device_id=(flip(dp, to), z), device_id_type=MESH)

    def tok_copy(s):
        to = lax.rem(z + s, n_z)
        return [pltpu.make_async_remote_copy(src_ref=a.at[to], dst_ref=f.at[z], send_sem=ss.at[s - 1], recv_sem=rs.at[s - 1],
                device_id=(dp, to), device_id_type=MESH) for a, f, ss, rs in ((tok, xf, t_send, t_recv), (seg, sf, s_send, s_recv))]

    def tok_wait(s):
        frm = lax.rem(z + n_z - s, n_z)
        for f, ss, rs in ((xf, t_send, t_recv), (sf, s_send, s_recv)):
            pltpu.make_async_remote_copy(src_ref=f.at[frm], dst_ref=f.at[frm], send_sem=ss.at[s - 1], recv_sem=rs.at[s - 1],
                device_id=(dp, z), device_id_type=MESH).wait_recv()

    for it in range(n_it):
        z_start(it, 0)
        for slot in (0, 1, 3):
            own_hop(it, slot).start()
    locs = []
    for it in range(n_it):
        locs.append(pltpu.make_async_copy(own(it), block(it, dp, z), loc_sem.at[it]))
    locs.append(pltpu.make_async_copy(tok.at[z], xf.at[z], loc_sem.at[n_it]))
    locs.append(pltpu.make_async_copy(seg.at[z], sf.at[z], loc_sem.at[n_it + 1]))
    for c in locs:
        c.start()

    def forward(it, zz):
        hop_wait(it, 0, zz)
        hop(it, 2, zz).start()
        hop(it, 4, zz).start()
        hop_wait(it, 1, zz)
        hop(it, 5, zz).start()

    def arrivals(step):
        return [(can_recv(0, step), 0, z - 1 - step), (can_recv(1, step), 1, z + 1 + step)]

    for step in range(n_z):
        if step < n_z - 1:
            for it in range(n_it):
                for ok, way, zz in arrivals(step):
                    @pl.when(ok)
                    def _():
                        z_wait(it, way, step)
                        if step < n_z - 2:
                            @pl.when(can_send(way, step + 1))
                            def _():
                                z_copy(it, way, step + 1).start()
                        for slot in (0, 1, 3):
                            hop(it, slot, zz).start()
        if step == 1:
            for s in range(1, n_z):
                for c in tok_copy(s):
                    c.start()
        for it in range(n_it):
            if step == 0:
                forward(it, z)
            else:
                for ok, way, zz in arrivals(step - 1):
                    @pl.when(ok)
                    def _():
                        forward(it, zz)
    for zz in range(n_z):
        for it in range(n_it):
            hop_wait(it, 2, zz)
            hop(it, 6, zz).start()
    for s in range(1, n_z):
        tok_wait(s)
    for zz in range(n_z):
        for it in range(n_it):
            for slot in (3, 4, 5, 6):
                hop_wait(it, slot, zz)
    for c in locs:
        c.wait()
    for it in range(n_it):
        for step in range(n_z - 1):
            for way in (0, 1):
                @pl.when(can_send(way, step))
                def _():
                    z_copy(it, way, step).wait_send()
        for zz in range(n_z):
            for slot in range(7):
                hop(it, slot, zz).wait_send()
    for s in range(1, n_z):
        for c in tok_copy(s):
            c.wait_send()

def gather(tokens, seg, shards, items, collective_id=0):
    n_it = len(items)
    D = pltpu.SemaphoreType.DMA
    out_shape = [jax.ShapeDtypeStruct(tokens.shape, tokens.dtype), jax.ShapeDtypeStruct(seg.shape, seg.dtype)]
    out_shape += [jax.ShapeDtypeStruct((32, *s.shape), s.dtype) for s in shards]
    anyspec = pl.BlockSpec(memory_space=pltpu.HBM)
    return pl.pallas_call(
        functools.partial(gather_kernel, items),
        out_shape=out_shape,
        in_specs=[pl.BlockSpec(memory_space=pltpu.VMEM)] * (2 + len(shards)),
        out_specs=[anyspec] * len(out_shape),
        scratch_shapes=[D((n_it + 2,)), D((3,)), D((3,)), D((3,)), D((3,)), D((n_it, 2, 3)), D((n_it, 2, 3)), D((n_it, 7, 4)), D((n_it, 7, 4))],
        compiler_params=pltpu.CompilerParams(collective_id=collective_id, has_side_effects=True),
    )(tokens, seg, *shards)


LOG2E = 1.4426950408889634
BIG = -1e30
F32 = jnp.float32
BF = jnp.bfloat16

def extras(seg):
    L = seg.shape[0]
    nb = L.bit_length()
    nblk = L // 128
    lane = jnp.arange(128)[None, :] % 64
    row_blk = (jnp.arange(L) // 128)[:, None]
    b = lane - (nblk + 3)
    inb = (b >= 0) & (b < 2 * nb)
    bit = (seg[:, None] >> (jnp.clip(b, 0, 2 * nb - 1) // 2)) & 1
    flip = b % 2
    u = jnp.where(inb, (bit ^ flip), 0).astype(BF)
    w = jnp.where(inb & ((bit ^ flip) == 0), BIG, 0.0)
    onehot = (lane < nblk) & (lane == row_blk)
    ones = (lane >= nblk) & (lane < nblk + 3)
    exk = (w + (onehot | ones)).astype(BF)
    farl = ((lane < nblk) & (lane <= row_blk - 2)).astype(BF)
    farr = ((lane < nblk) & (lane >= row_blk + 2)).astype(BF)
    return u, exk, farl, farr

def diagonals(table):
    m = jnp.arange(512)
    rel = jnp.concatenate([(m + 127) % 512 - 255, 128 - m + 512 * (m >= 384)])
    hot = (bucket_of(rel)[:, None] == jnp.arange(table.shape[0])[None, :]).astype(BF)
    vec = jnp.dot(hot, table.astype(BF), preferred_element_type=F32)
    pair = vec.reshape(2, 512, -1, 2).transpose(2, 0, 3, 1).reshape(-1, 4, 512)
    back = jnp.pad(vec[512:].T[:, None], ((0, 0), (0, 7), (0, 0)))
    return jnp.pad(pair, ((0, 0), (0, 4), (0, 0))), back


def skewed(row):
    return pltpu.roll(jnp.broadcast_to(row, (128, 512)), 0, 1, stride=1, stride_axis=0)[:, :384]


def diagonal_sums(near):
    rows = 64
    x = jnp.concatenate([near, jnp.zeros((128, 128), F32)], axis=1)
    while rows >= 1:
        x = x[:rows] + pltpu.roll(x[rows:], 512 - rows, 1)
        rows //= 2
    return x


def fwd_kernel(nblk, bl_ref, q_ref, k_ref, v_ref, exq_ref, exk_ref, fl_ref, fr_ref, strip_ref, o_ref, qa_ref):
    L = q_ref.shape[0]
    hp = pl.program_id(0)
    lane = lax.broadcasted_iota(jnp.int32, (L, 128), 1)
    QB = 256
    outs = []
    for h in range(2):
        sel = (lane < 64) if h == 0 else (lane >= 64)
        strip = skewed(strip_ref[0, h:h + 1])
        bl = bl_ref[hp * 2 + h, 0].astype(BF); br = bl_ref[hp * 2 + h, 1].astype(BF)
        qa = jnp.where(sel, q_ref[...], exq_ref[...] + fl_ref[...] * bl + fr_ref[...] * br)
        ka = jnp.where(sel, k_ref[...], exk_ref[...])
        va = jnp.where(sel, v_ref[...], jnp.ones((L, 128), BF))
        lane_l = 64 * (1 - h)
        for blk in range(L // QB):
            r0 = blk * QB
            qb = qa[r0:r0 + QB]
            s = lax.dot_general(qb, ka, (((1,), (1,)), ((), ())), preferred_element_type=F32)
            rows = []
            for sub in range(QB // 128):
                I = blk * (QB // 128) + sub
                lo = max(I - 1, 0); hi = min(I + 1, nblk - 1)
                srow = s[sub * 128:(sub + 1) * 128]
                parts = []
                if lo > 0: parts.append(srow[:, :lo * 128])
                parts.append(srow[:, lo * 128:(hi + 1) * 128] + strip[:, (lo - I + 1) * 128:(hi - I + 2) * 128])
                if hi < nblk - 1: parts.append(srow[:, (hi + 1) * 128:])
                rows.append(jnp.concatenate(parts, axis=1))
            s = jnp.concatenate(rows, axis=0)
            m = jnp.max(s, axis=1, keepdims=True)
            p = jnp.exp2((s - m) * LOG2E).astype(BF)
            o = jnp.dot(p, va, preferred_element_type=F32)
            l = o[:, lane_l:lane_l + 1]
            outs.append(o / l)
            lse = m + jnp.log(l)
            hi_ = (-lse).astype(BF); rest = -lse - hi_.astype(F32)
            mid = rest.astype(BF); low = (rest - mid.astype(F32)).astype(BF)
            base = 64 * (1 - h) + nblk
            ln = lane[:QB]
            qx = jnp.where(ln == base, hi_, jnp.where(ln == base + 1, mid, jnp.where(ln == base + 2, low, qb)))
            qa_ref[h, r0:r0 + QB, :] = qx
    n = L // QB
    for blk in range(n):
        o_ref[blk * QB:(blk + 1) * QB, :] = jnp.where(lane[:QB] < 64, outs[blk], outs[n + blk]).astype(BF)

def attn_fwd(qkv, ex, strip, far, interpret=False):
    L, W = qkv.shape
    D = W // 3
    H = D // HD
    npair = H // 2
    nblk = L // 128
    exq, exk, fl, fr = ex
    full = lambda: pl.BlockSpec((L, 128), lambda i: (0, 0))
    return pl.pallas_call(
        functools.partial(fwd_kernel, nblk),
        grid=(npair,),
        in_specs=[pl.BlockSpec(memory_space=pltpu.SMEM),
                  pl.BlockSpec((L, 128), lambda i: (0, i)),
                  pl.BlockSpec((L, 128), lambda i: (0, npair + i)),
                  pl.BlockSpec((L, 128), lambda i: (0, 2 * npair + i)),
                  full(), full(), full(), full(),
                  pl.BlockSpec((1, 8, 512), lambda i: (i, 0, 0))],
        out_specs=[pl.BlockSpec((L, 128), lambda i: (0, i)), pl.BlockSpec((2, L, 128), lambda i: (i, 0, 0))],
        out_shape=[jax.ShapeDtypeStruct((L, D), BF), jax.ShapeDtypeStruct((H, L, 128), BF)],
        compiler_params=pltpu.CompilerParams(vmem_limit_bytes=48 << 20),
        cost_estimate=pl.CostEstimate(flops=4 * L * L * D * 4, bytes_accessed=L * W * 4, transcendentals=L * L * H),
    )(far, qkv, qkv, qkv, exq, exk, fl, fr, strip)


GELU_A = 0.7978845608028654
GELU_B = 0.044715


def mm(a, b, dims=((1,), (0,))):
    return lax.dot_general(a, b, (dims, ((), ())), preferred_element_type=F32)


def ffn_kernel(x_ref, mixed_ref, g_ref, gain_ref, wo_ref, wi_ref, wb_ref,
               out_ref, gm_ref, gmix_ref, dwo_ref, dwi_ref, dwb_ref, dgain_ref,
               mid_ref, h_ref, ht_ref, acc_ref, dh_ref):
    step = pl.program_id(0)
    rows = x_ref.shape[0]
    half = 256

    @pl.when(step == 0)
    def _():
        for r in range(0, rows, half):
            part = pl.ds(r, half)
            middle = x_ref[part].astype(F32) + mm(mixed_ref[part], wo_ref[...])
            mid_ref[part] = middle
            acc_ref[part] = middle
            scale = lax.rsqrt(jnp.mean(middle * middle, axis=-1, keepdims=True) + EPS)
            normed = (middle * scale * gain_ref[...]).astype(BF)
            h_ref[part] = normed
            ht_ref[:, part] = normed.T
            dh_ref[part] = jnp.zeros((half, x_ref.shape[1]), F32)

    gates = []
    hiddens = []
    for r in range(0, rows, half):
        part = pl.ds(r, half)
        pre = mm(h_ref[part], wi_ref[...])
        dhid = mm(g_ref[part], wb_ref[...], ((1,), (1,)))
        sq = pre * pre
        t = jnp.tanh(pre * (GELU_A + GELU_A * GELU_B * sq))
        half_t = 0.5 + 0.5 * t
        hidden = (pre * half_t).astype(BF)
        slope = half_t + pre * (0.5 - 0.5 * t * t) * (GELU_A + 3.0 * GELU_A * GELU_B * sq)
        dpre = (dhid * slope).astype(BF)
        acc_ref[part] += mm(hidden, wb_ref[...])
        dh_ref[part] += mm(dpre, wi_ref[...], ((1,), (1,)))
        hiddens.append(hidden)
        gates.append(dpre)
    dwi_ref[...] = mm(ht_ref[...], jnp.concatenate(gates, axis=0)).astype(BF)
    dwb_ref[...] = mm(jnp.concatenate(hiddens, axis=0), g_ref[...], ((0,), (0,))).astype(BF)

    @pl.when(step == pl.num_programs(0) - 1)
    def _():
        dgain = jnp.zeros((1, x_ref.shape[1]), F32)
        for r in range(0, rows, half):
            part = pl.ds(r, half)
            out_ref[part] = acc_ref[part].astype(BF)
            middle = mid_ref[part]
            dh = dh_ref[part]
            scale = lax.rsqrt(jnp.mean(middle * middle, axis=-1, keepdims=True) + EPS)
            dgain += jnp.sum(dh * (middle * scale), axis=0, keepdims=True)
            u = dh * gain_ref[...]
            inner = jnp.mean(u * middle, axis=-1, keepdims=True)
            gm = g_ref[part].astype(F32) + scale * u - middle * (scale * scale * scale * inner)
            gm_ref[part] = gm
            low = gm.astype(BF)
            h_ref[part] = low
            gmix_ref[part] = mm(low, wo_ref[...], ((1,), (1,))).astype(BF)
        dgain_ref[...] = dgain
        dwo_ref[...] = mm(mixed_ref[...], h_ref[...], ((0,), (0,))).astype(BF)


def ffn(x, mixed, g, gain, wo, wi, wb, chunk=512):
    rows, width = x.shape
    ff = wi.shape[1]
    whole = lambda s: pl.BlockSpec(s, lambda i: (0, 0), pipeline_mode=pl.Buffered(1))
    S = jax.ShapeDtypeStruct
    return pl.pallas_call(
        ffn_kernel,
        grid=(ff // chunk,),
        in_specs=[whole((rows, width))] * 3 + [whole((1, width)), whole((width, width)),
                  pl.BlockSpec((width, chunk), lambda i: (0, i)), pl.BlockSpec((chunk, width), lambda i: (i, 0))],
        out_specs=[whole((rows, width))] * 3 + [whole((width, width)), pl.BlockSpec((width, chunk), lambda i: (0, i)),
                   pl.BlockSpec((chunk, width), lambda i: (i, 0)), whole((1, width))],
        out_shape=[S((rows, width), BF), S((rows, width), F32), S((rows, width), BF), S((width, width), BF),
                   S((width, ff), BF), S((ff, width), BF), S((1, width), F32)],
        scratch_shapes=[pltpu.VMEM((rows, width), F32), pltpu.VMEM((rows, width), BF), pltpu.VMEM((width, rows), BF),
                        pltpu.VMEM((rows, width), F32), pltpu.VMEM((rows, width), F32)],
        compiler_params=pltpu.CompilerParams(vmem_limit_bytes=56 << 20),
        cost_estimate=pl.CostEstimate(flops=12 * rows * width * ff + 6 * rows * width * width, bytes_accessed=50 << 20, transcendentals=rows * ff),
    )(x, mixed, g, gain, wo, wi, wb)


def back_kernel(chunks, n_early, *refs):
    n_it, n_arr, n_z = len(chunks), 5, 4
    (qa_ref, qkv_ref, do_ref, o_ref, exk_ref, bias_ref, x_ref, gm_ref, gain_ref, gain2_ref, w_ref, y_ref) = refs[:12]
    p_out, p_in, p_back = refs[12:15]
    gx_out, y_out = refs[15:17]
    outs = refs[17:17 + n_arr]
    scr = refs[17 + n_arr:]
    k_ref, v_ref, p_qkv, p_small, gx, ht_ref, dqt_ref, dq_ref, dk_ref, dv_ref, diag_ref = scr[:11]
    scr = scr[11:]
    part = (p_qkv, p_small, p_out, p_in, p_back)
    rc, r2, r1, zo, zu, zd = (scr[k * n_it:(k + 1) * n_it] for k in range(6))
    stg = scr[6 * n_it:6 * n_it + n_early]
    (loc_sem, own_sem, t_send, t_recv, y_send, y_recv, c_send, c_recv, x2_send, x2_recv, x1_send, x1_recv,
     z_send, z_recv) = scr[6 * n_it + n_early:]
    dp, z = lax.axis_index("dp"), lax.axis_index("seq")
    core = lax.rem(dp, 2)
    quad = dp // 2
    peers = [(dp, lax.rem(z + s, n_z)) for s in range(1, n_z)] + [(flip(dp, b), z) for b in (1, 2, 4)]
    barrier = pltpu.get_barrier_semaphore()
    for p in peers:
        pl.semaphore_signal(barrier, inc=1, device_id=p, device_id_type=MESH)
    pl.semaphore_wait(barrier, len(peers))

    def remote(src, dst, ss, rs, to):
        return pltpu.make_async_remote_copy(src_ref=src, dst_ref=dst, send_sem=ss, recv_sem=rs, device_id=to, device_id_type=MESH)

    def piece(it, d):
        a, c0, w = chunks[it][:3]
        return part[a].at[d, :, pl.ds(c0, w)]

    def own_copy(it, q):
        return pltpu.make_async_copy(piece(it, 2 * q + core), stg[it].at[q], own_sem.at[it, q])

    def add_into(dst, src, chunk=16):
        rows = dst.shape[0]
        chunk = min(chunk, rows)
        @pl.loop(0, rows // chunk)
        def _(i):
            at = pl.ds(pl.multiple_of(i * chunk, chunk), chunk)
            dst[at] = dst[at] + src[at]

    def q_at(it, f1, f2):
        b1, b2 = chunks[it][3:]
        q = quad
        if f1: q = flip(q, b1 // 2)
        if f2: q = flip(q, b2 // 2)
        return q

    def c_copy(it, q):
        return remote(piece(it, 2 * q + 1 - core), rc[it].at[q], c_send.at[it, q], c_recv.at[it, q], (flip(dp, 1), z))

    def x2_copy(it, f1):
        q = q_at(it, f1, True)
        k = (q // (chunks[it][3] // 2)) % 2
        return remote(rc[it].at[q], r2[it].at[k], x2_send.at[it, k], x2_recv.at[it, k], (flip(dp, chunks[it][4]), z))

    def x1_copy(it):
        return remote(rc[it].at[q_at(it, True, False)], r1[it], x1_send.at[it], x1_recv.at[it], (flip(dp, chunks[it][3]), z))

    def rows_copy(src, dst, ss, rs, s):
        to = lax.rem(z + s, n_z)
        return remote(src.at[to], dst.at[z], ss.at[s - 1], rs.at[s - 1], (dp, to))

    def rows_wait(dst, ss, rs, s):
        frm = lax.rem(z + n_z - s, n_z)
        remote(dst.at[frm], dst.at[frm], ss.at[s - 1], rs.at[s - 1], (dp, z)).wait_recv()

    def core_start(it):
        for f1, f2 in ((True, True), (False, True), (True, False), (False, False)):
            c_copy(it, q_at(it, f1, f2)).start()

    def core_sum(it, f1, f2):
        q = q_at(it, f1, f2)
        c_copy(it, q).wait_recv()
        if it < n_early:
            own_copy(it, q).wait()
            add_into(rc[it].at[q], stg[it].at[q])
        else:
            add_into(rc[it].at[q], piece(it, 2 * q + core))

    def stage_core(it):
        for f1 in (True, False):
            core_sum(it, f1, True)
            x2_copy(it, f1).start()
        for f1 in (True, False):
            core_sum(it, f1, False)

    def stage_x2(it):
        for f1 in (True, False):
            q = q_at(it, f1, False)
            k = (q // (chunks[it][3] // 2)) % 2
            remote(rc[it].at[0], r2[it].at[k], x2_send.at[it, k], x2_recv.at[it, k], (dp, z)).wait_recv()
            add_into(rc[it].at[q], r2[it].at[k])
            if f1:
                x1_copy(it).start()

    def z_copy(it, way, j):
        src = zo[it].at[j]
        dst = (zu if way == 0 else zd)[it].at[j]
        return remote(src, dst, z_send.at[it, way, j], z_recv.at[it, way, j], (dp, z + 1 if way == 0 else z - 1))

    def z_add(it, way, j):
        buf = (zu if way == 0 else zd)[it]
        remote(buf.at[j], buf.at[j], z_send.at[it, way, j], z_recv.at[it, way, j], (dp, z)).wait_recv()
        zo[it][j] = (zo[it][j].astype(F32) + buf[j].astype(F32)).astype(zo[it].dtype)

    def stage_x1(it):
        x1_copy(it).wait_recv()
        rows = zo[it].shape[1]
        for j in range(n_z):
            at = pl.ds(j * rows, rows)
            zo[it][j] = (rc[it][quad, at].astype(F32) + r1[it][at].astype(F32)).astype(zo[it].dtype)
        stage_z(it, 0)

    def stage_z(it, s):
        for way, here in ((0, s), (1, n_z - 1 - s)):
            @pl.when(z == here)
            def _():
                for j in (range(n_z - 1, here, -1) if way == 0 else range(here)):
                    if s > 0:
                        z_add(it, way, j)
                    z_copy(it, way, j).start()

    def stage_end(it):
        a, c0, w = chunks[it][:3]
        col = pl.ds(c0, w)
        outs[a][:, col] = zo[it][z].astype(F32)
        for way, ok in ((0, z > 0), (1, z < n_z - 1)):
            @pl.when(ok)
            def _():
                buf = (zu if way == 0 else zd)[it].at[z]
                remote(buf, buf, z_send.at[it, way, z], z_recv.at[it, way, z], (dp, z)).wait_recv()
                outs[a][:, col] += buf[...].astype(F32)

    stage_z1, stage_z2 = functools.partial(stage_z, s=1), functools.partial(stage_z, s=2)
    rows, width = x_ref.shape
    nblk = rows // 128
    heads = qa_ref.shape[0]
    plan = {
        -1: [(stage_core, 0), (stage_core, 1)],
        0: [(stage_core, 4), (stage_core, 5)],
        2: [(stage_core, 2), (stage_core, 3)],
        4: [(stage_x2, 0), (stage_x2, 1)],
        5: [(stage_x2, 4), (stage_x2, 5)],
        8: [(stage_x2, 2), (stage_x2, 3)],
        10: [(stage_x1, 0), (stage_x1, 1)],
        11: [(stage_x1, 4), (stage_x1, 5), (stage_z1, 0), (stage_z1, 1)],
    }
    for it in range(n_early):
        core_start(it)
        for q in range(4):
            own_copy(it, q).start()
    kv = [pltpu.make_async_copy(qkv_ref.at[:, pl.ds((i + 1) * width, width)], ref, loc_sem.at[2 + i]) for i, ref in enumerate((k_ref, v_ref))]
    for c in kv:
        c.start()
    y_loc = pltpu.make_async_copy(y_ref.at[z], y_out.at[z], loc_sem.at[0])
    y_loc.start()
    for s in range(1, n_z):
        rows_copy(y_ref, y_out, y_send, y_recv, s).start()
    for fn, it in plan[-1]:
        fn(it)
    for c in kv:
        c.wait()

    diag_ref[...] = jnp.zeros_like(diag_ref)
    lane = lax.broadcasted_iota(jnp.int32, (rows, 128), 1)
    kb_rows = 256
    nsub = kb_rows // 128

    @pl.loop(0, heads)
    def _(h):
        par = lax.rem(h, 2)
        cols = pl.ds(pl.multiple_of((h // 2) * 128, 128), 128)
        sel = lane // 64 == par
        spare = lane % 64 - nblk
        strip = skewed(bias_ref[h, 0:1])
        qa = qa_ref[h]
        ka = jnp.where(sel, k_ref[:, cols], exk_ref[...])
        ones = jnp.where((spare >= 0) & (spare < 3), 1.0, 0.0).astype(BF)
        va = jnp.where(sel, v_ref[:, cols], ones)
        prod = do_ref[:, cols].astype(F32) * o_ref[:, cols].astype(F32)
        delta = -jnp.sum(jnp.where(sel, prod, 0.0), axis=1, keepdims=True)
        hi_ = delta.astype(BF)
        rest = delta - hi_.astype(F32)
        mid = rest.astype(BF)
        low = (rest - mid.astype(F32)).astype(BF)
        extra = jnp.where(spare == 0, hi_, jnp.where(spare == 1, mid, jnp.where(spare == 2, low, jnp.zeros((rows, 128), BF))))
        doa = jnp.where(sel, do_ref[:, cols], extra)
        near = jnp.zeros((128, 384), F32)
        for kb in range(rows // kb_rows):
            r0 = kb * kb_rows
            kab = ka[r0:r0 + kb_rows]
            s = mm(kab, qa, ((1,), (1,)))
            dp_ = mm(va[r0:r0 + kb_rows], doa, ((1,), (1,)))
            prow, dsrow = [], []
            for sub in range(nsub):
                J = kb * nsub + sub
                lo = max(J - 1, 0)
                hi = min(J + 1, nblk - 1)
                srow = s[sub * 128:(sub + 1) * 128]
                parts = []
                if lo > 0:
                    parts.append(srow[:, :lo * 128])
                parts.append(srow[:, lo * 128:(hi + 1) * 128] + strip[:, (lo - J + 1) * 128:(hi - J + 2) * 128])
                if hi < nblk - 1:
                    parts.append(srow[:, (hi + 1) * 128:])
                p = jnp.exp2(jnp.concatenate(parts, axis=1) * LOG2E)
                ds = p * dp_[sub * 128:(sub + 1) * 128]
                nr = ds[:, lo * 128:(hi + 1) * 128]
                if lo > J - 1:
                    nr = jnp.concatenate([jnp.zeros((128, 128), F32), nr], axis=1)
                if hi < J + 1:
                    nr = jnp.concatenate([nr, jnp.zeros((128, 128), F32)], axis=1)
                near = near + nr
                prow.append(p.astype(BF))
                dsrow.append(ds.astype(BF))
            pb = jnp.concatenate(prow, axis=0)
            dsb = jnp.concatenate(dsrow, axis=0)
            at = pl.ds(r0, kb_rows)
            dv_ref[at, cols] = jnp.where(sel[:kb_rows], mm(pb, doa).astype(BF), dv_ref[at, cols])
            dk_ref[at, cols] = jnp.where(sel[:kb_rows], mm(dsb, qa).astype(BF), dk_ref[at, cols])
            dqt = mm(kab, dsb, ((0,), (0,)))
            dqt_ref[...] = dqt if kb == 0 else dqt_ref[...] + dqt
        far = dqt_ref[pl.ds(pl.multiple_of(64 - 64 * par, 64), 8)]
        key_block = lax.broadcasted_iota(jnp.int32, far.shape, 0)
        query_block = lax.broadcasted_iota(jnp.int32, far.shape, 1) // 128
        left = jnp.sum(jnp.where(key_block <= query_block - 2, far, 0.0))
        right = jnp.sum(jnp.where(key_block >= query_block + 2, far, 0.0))
        column = lax.broadcasted_iota(jnp.int32, (1, 512), 1)
        diag_ref[pl.ds(h, 1)] = diagonal_sums(near) + jnp.where(column == 383, left, 0.0) + jnp.where(column == 385, right, 0.0)
        dq_ref[pl.ds(pl.multiple_of(h * 64, 64), 64)] = dqt_ref[pl.ds(pl.multiple_of(64 * par, 64), 64)].astype(BF)
        for k in range(heads):
            if k in plan:
                @pl.when(h == k)
                def _():
                    for fn, it in plan[k]:
                        fn(it)

    half = rows // n_z
    dgain = jnp.zeros((1, width), F32)

    def scaled(r):
        x = x_ref[pl.ds(r * half, half)].astype(F32)
        return x, lax.rsqrt(jnp.mean(x * x, axis=-1, keepdims=True) + EPS)

    for r in range(n_z):
        x, scale = scaled(r)
        ht_ref[:, r * half:(r + 1) * half] = (x * scale * gain_ref[...]).astype(BF).T
    for i in range(3):
        w0 = i * width
        if i == 0:
            dw = mm(ht_ref[...], dq_ref[...], ((1,), (1,)))
        else:
            dw = mm(ht_ref[...], (dk_ref, dv_ref)[i - 1][...])
        dw = dw.astype(BF)
        for d in range(8):
            p_qkv[d, :, w0:w0 + width] = dw[d * 96:(d + 1) * 96]
        if i == 1:
            for it in (0, 1):
                stage_z2(it)
            for it in (4, 5):
                stage_z1(it)
    for it in (6, 7):
        core_start(it)
    gx_loc = pltpu.make_async_copy(gx.at[z], gx_out.at[z], loc_sem.at[1])
    for r in range(n_z):
        at = pl.ds(r * half, half)
        x, scale = scaled(r)
        dh = mm(dq_ref[:, at], w_ref[:, :width], ((0,), (1,)))
        dh += mm(dk_ref[at], w_ref[:, width:2 * width], ((1,), (1,)))
        dh += mm(dv_ref[at], w_ref[:, 2 * width:], ((1,), (1,)))
        dgain += jnp.sum(dh * (x * scale), axis=0, keepdims=True)
        u = dh * gain_ref[...]
        inner = jnp.mean(u * x, axis=-1, keepdims=True)
        gx[r] = (gm_ref[at] + scale * u - x * (scale * scale * scale * inner)).astype(BF)
        if r == 1:
            for it in (6, 7):
                stage_core(it)
    gx_loc.start()
    for s in range(1, n_z):
        rows_copy(gx, gx_out, t_send, t_recv, s).start()
    n_dev = 32
    own = width // n_dev
    place = lax.broadcasted_iota(jnp.int32, (n_dev, width), 1)
    mine = place // own == lax.broadcasted_iota(jnp.int32, (n_dev, width), 0)
    col = lax.broadcasted_iota(jnp.int32, (width, 128), 1)
    row = lax.broadcasted_iota(jnp.int32, (width, 128), 0) % own
    small = jnp.zeros((n_dev, 128), F32)
    for i, g in enumerate((dgain, gain2_ref[...])):
        small += exact(jnp.where(mine, g, 0.0), (col == row + i * own).astype(F32), ((1,), (0,)))
    m = lax.broadcasted_iota(jnp.int32, (n_dev, 512), 1)
    hot = bucket_of(128 - m + jnp.where(m >= 384, 512, 0)) == lax.broadcasted_iota(jnp.int32, (n_dev, 512), 0)
    sums = exact(hot.astype(F32), diag_ref[...], ((1,), (1,)))
    col = lax.broadcasted_iota(jnp.int32, (16, 128), 1)
    row = lax.broadcasted_iota(jnp.int32, (16, 128), 0)
    small += exact(sums, ((col == row + 2 * own) & (row < heads)).astype(F32), ((1,), (0,)))
    for d in range(8):
        p_small[d] = small[d * n_z:(d + 1) * n_z]
    core_start(8)
    stage_core(8)
    for fn, its in (
        (stage_x1, (2, 3)),
        (stage_z1, (2, 3)),
        (stage_x2, (6, 7, 8)),
        (stage_z2, (4, 5, 2, 3)),
        (stage_x1, (6, 7, 8)),
        (stage_z1, (6, 7, 8)),
        (stage_z2, (6, 7, 8)),
        (stage_end, range(n_it)),
    ):
        for it in its:
            fn(it)
    for s in range(1, n_z):
        rows_wait(y_out, y_send, y_recv, s)
        rows_wait(gx_out, t_send, t_recv, s)
    y_loc.wait()
    gx_loc.wait()
    for s in range(1, n_z):
        rows_copy(y_ref, y_out, y_send, y_recv, s).wait_send()
        rows_copy(gx, gx_out, t_send, t_recv, s).wait_send()
    for it in range(n_it):
        for q in range(4):
            c_copy(it, q).wait_send()
        for f1 in (True, False):
            x2_copy(it, f1).wait_send()
        x1_copy(it).wait_send()
        for j in range(n_z):
            for way in (0, 1):
                @pl.when(j > z if way == 0 else j < z)
                def _():
                    z_copy(it, way, j).wait_send()


def exact(a, b, dims):
    return lax.dot_general(a, b, (dims, ((), ())), preferred_element_type=F32, precision=lax.Precision.HIGHEST)


def backward(qa, qkv, do, o, exk, bias, x, gm, gain, dgain2, w, y, g_out, g_in, g_back, chunks, n_early, collective_id=1):
    rows, width = x.shape
    n_it = len(chunks)
    D = pltpu.SemaphoreType.DMA
    S = jax.ShapeDtypeStruct
    parts = (S((8, 96, 3 * width), BF), S((8, 4, 128), F32), g_out, g_in, g_back)

    def V(c, *lead):
        p = parts[c[0]]
        return pltpu.VMEM((*lead, p.shape[1], c[2]), p.dtype)

    def zs(c):
        p = parts[c[0]]
        return pltpu.VMEM((4, p.shape[1] // 4, c[2]), p.dtype)

    vm = pl.BlockSpec(memory_space=pltpu.VMEM)
    hbm = pl.BlockSpec(memory_space=pltpu.HBM)
    scratch = [pltpu.VMEM((rows, width), BF), pltpu.VMEM((rows, width), BF), pltpu.VMEM(parts[0].shape, BF), pltpu.VMEM((8, 4, 128), F32), pltpu.VMEM((4, rows // 4, width), BF),
               pltpu.VMEM((width, rows), BF), pltpu.VMEM((128, rows), F32), pltpu.VMEM((width, rows), BF),
               pltpu.VMEM((rows, width), BF), pltpu.VMEM((rows, width), BF), pltpu.VMEM((16, 512), F32)]
    scratch += [V(c, 4) for c in chunks] + [V(c, 2) for c in chunks] + [V(c) for c in chunks] + [zs(c) for c in chunks] * 3
    scratch += [V(c, 4) for c in chunks[:n_early]]
    scratch += [D((4,)), D((n_early, 4)), D((3,)), D((3,)), D((3,)), D((3,)), D((n_it, 4)), D((n_it, 4)), D((n_it, 2)), D((n_it, 2)),
                D((n_it,)), D((n_it,)), D((n_it, 2, 4)), D((n_it, 2, 4))]
    return pl.pallas_call(
        functools.partial(back_kernel, chunks, n_early),
        out_shape=[S((4, rows // 4, width), BF)] * 2 + [S((p.shape[1] // 4, p.shape[2]), F32) for p in parts],
        in_specs=[vm, hbm] + [vm] * 9 + [hbm] * 4,
        out_specs=[hbm] * 2 + [vm] * 5,
        scratch_shapes=scratch,
        compiler_params=pltpu.CompilerParams(collective_id=collective_id, has_side_effects=True, vmem_limit_bytes=62 << 20),
    )(qa, qkv, do, o, exk, bias, x, gm, gain, dgain2, w, y, g_out, g_in, g_back)


def fits(mesh):
    return mesh.shape["dp"] == 8 and mesh.shape["seq"] == 4


ITEMS = ((0, 4, 2), (4, 2, 4), (1, 2, 4), (2, 4, 2), (3, 2, 4))
ROUTES = (
    (3, 0, 1536, 4, 2),
    (3, 1536, 1536, 2, 4),
    (4, 0, 384, 4, 2),
    (4, 384, 384, 2, 4),
    (2, 0, 384, 4, 2),
    (2, 384, 384, 2, 4),
    (0, 0, 1152, 4, 2),
    (0, 1152, 1152, 2, 4),
    (1, 0, 128, 2, 4),
)
EARLY = 6


def fast_shards(
    tokens,
    segment_ids,
    valid_mask,
    cotangent,
    gain_one,
    gain_two,
    bias_table,
    qkv_weight,
    out_weight,
    in_weight,
    back_weight,
):
    n_z = lax.axis_size("seq")
    seq_count, block_len, width = tokens.shape
    seq_len = n_z * block_len
    n_dev = n_z * lax.axis_size("dp")
    g_rows, t_rows = gain_one.shape[0], bias_table.shape[0]
    small = jnp.concatenate([gain_one, gain_two, bias_table])
    small = jnp.pad(small[None], ((0, 7), (0, 128 - small.shape[0])))
    grad_local = cotangent * valid_mask[..., None].astype(BF)
    x4, seg4, qkv_full, out_full, in_full, back_full, small_full = gather(
        tokens,
        segment_ids.reshape(seq_count, 1, block_len),
        (qkv_weight, out_weight, in_weight, back_weight, small),
        ITEMS,
    )
    qkv_full = qkv_full.reshape(width, 3 * width)
    out_full = out_full.reshape(width, width)
    in_full = in_full.reshape(width, -1)
    back_full = back_full.reshape(-1, width)
    small_full = small_full[:, 0]
    gain_first = small_full[:, :g_rows].reshape(1, width).astype(F32)
    gain_second = small_full[:, g_rows : 2 * g_rows].reshape(1, width).astype(F32)
    table = small_full[:, 2 * g_rows : 2 * g_rows + t_rows].reshape(BUCKETS, HEADS)
    grad_local, x4 = lax.optimization_barrier((grad_local, x4))
    g_low = lax.all_to_all(grad_local, "seq", 0, 1, tiled=True).reshape(seq_len, width)
    x = x4.reshape(seq_len, width)
    flat_x = x.astype(F32)
    seg = seg4.reshape(seq_len)
    exq, exk, far_left, far_right = extras(seg)
    bias_rows, bias_back = diagonals(table.astype(F32))
    far = jnp.stack([table[BUCKETS // 2 - 1], table[BUCKETS - 1]], axis=1).astype(F32)
    first_normed = (flat_x * rms_scale(flat_x) * gain_first).astype(BF)
    projected = jnp.dot(first_normed, qkv_full, preferred_element_type=F32).astype(BF)
    mixed, q_aug = attn_fwd(projected, (exq, exk, far_left, far_right), bias_rows, far)
    result, grad_middle, grad_mixed, grad_out, grad_in, grad_back, grad_gain_second = ffn(
        x, mixed, g_low, gain_second, out_full, in_full, back_full
    )
    grad_tokens, output, own_qkv, own_small, own_out, own_in, own_back = backward(
        q_aug,
        projected,
        grad_mixed,
        mixed,
        exk,
        bias_back,
        x,
        grad_middle,
        gain_first,
        grad_gain_second,
        qkv_full,
        result.reshape(n_z, block_len, width),
        grad_out.reshape(8, -1, width),
        grad_in.reshape(8, -1, in_full.shape[1]),
        grad_back.reshape(8, -1, width),
        ROUTES,
        EARLY,
    )
    own_small = own_small[0]
    return (
        output,
        grad_tokens,
        own_small[:g_rows],
        own_small[g_rows : 2 * g_rows],
        own_small[2 * g_rows : 2 * g_rows + t_rows],
        own_qkv,
        own_out,
        own_in,
        own_back,
    )


def solution(mesh):
    in_specs = (
        P("dp", "seq", None),
        P("dp", "seq"),
        P("dp", "seq"),
        P("dp", "seq", None),
        P(("dp", "seq")),
        P(("dp", "seq")),
        P(("dp", "seq")),
        P(("dp", "seq"), None),
        P(("dp", "seq"), None),
        P(("dp", "seq"), None),
        P(("dp", "seq"), None),
    )
    out_specs = (
        P("dp", "seq", None),
        P("dp", "seq", None),
        P(("dp", "seq")),
        P(("dp", "seq")),
        P(("dp", "seq")),
        P(("dp", "seq"), None),
        P(("dp", "seq"), None),
        P(("dp", "seq"), None),
        P(("dp", "seq"), None),
    )
    return jax.shard_map(fast_shards if fits(mesh) else general_shards, mesh=mesh, in_specs=in_specs, out_specs=out_specs, check_vma=False)
```

```python
import functools

import jax
import jax.numpy as jnp
from jax import lax
from jax.experimental import pallas as pl
from jax.experimental.pallas import tpu as pltpu
from jax.sharding import PartitionSpec as P

HEADS = 12
HD = 64
BUCKETS = 32


EPS = 1e-06
NEGATIVE = -1e30
bucket_limits = (12, 16, 23, 32, 46, 64, 91)


def bucket_of(relative):
    distance = jnp.abs(relative)
    counted = jnp.zeros_like(distance)
    for threshold in bucket_limits:
        counted = counted + (distance >= threshold).astype(jnp.int32)
    inside = jnp.where(distance < 8, distance, 8 + counted)
    return inside + 16 * (relative > 0).astype(jnp.int32)


def rms_scale(values):
    return lax.rsqrt(jnp.mean(values * values, axis=-1, keepdims=True) + EPS)


def smooth_gate(values):
    return jax.nn.gelu(values, approximate=True)


def norm_backward(values, scale_inv, gain_vec, grad_normed):
    weighted = grad_normed * gain_vec
    grad_gain = jnp.sum(grad_normed * values * scale_inv, axis=0)
    cubed = scale_inv * scale_inv * scale_inv
    grad_values = scale_inv * weighted - values * cubed * jnp.mean(
        weighted * values, axis=-1, keepdims=True
    )
    return (grad_values, grad_gain)


def group_scores(query_part, key_part, seg_query, seg_key, complete_bias):
    scores = (
        jnp.einsum("gqhd,gkhd->ghqk", query_part, key_part, preferred_element_type=jnp.float32)
        + complete_bias[None]
    )
    allowed = (seg_query[:, :, None] == seg_key[:, None, :])[:, None]
    return jnp.where(allowed, scores, NEGATIVE)


def query_backward(items, complete_bias):
    query_part, key_part, value_part, seg_query, seg_key, log_total, grad_part = items
    scores = group_scores(query_part, key_part, seg_query, seg_key, complete_bias)
    softmax_probabilities = jnp.exp(scores - log_total)
    grad_probs = jnp.einsum(
        "gqhd,gkhd->ghqk", grad_part, value_part, preferred_element_type=jnp.float32
    )
    row_inner = jnp.sum(softmax_probabilities * grad_probs, axis=-1, keepdims=True)
    grad_scores = (softmax_probabilities * (grad_probs - row_inner)).astype(jnp.bfloat16)
    grad_query = jnp.einsum(
        "ghqk,gkhd->gqhd", grad_scores, key_part, preferred_element_type=jnp.float32
    ).astype(jnp.bfloat16)
    return (softmax_probabilities, grad_scores, grad_query, row_inner)


def general_shards(
    tokens,
    segment_ids,
    valid_mask,
    cotangent,
    gain_one,
    gain_two,
    bias_table,
    qkv_weight,
    out_weight,
    in_weight,
    back_weight,
):
    gathered = (
        lax.all_gather(gain_one, ("dp", "seq"), axis=0, tiled=True),
        lax.all_gather(gain_two, ("dp", "seq"), axis=0, tiled=True),
        lax.all_gather(bias_table, ("dp", "seq"), axis=0, tiled=True),
        lax.all_gather(qkv_weight, ("dp", "seq"), axis=0, tiled=True),
        lax.all_gather(out_weight, ("dp", "seq"), axis=0, tiled=True),
        lax.all_gather(in_weight, ("dp", "seq"), axis=0, tiled=True),
        lax.all_gather(back_weight, ("dp", "seq"), axis=0, tiled=True),
    )
    gain_first, gain_second, table_flat, qkv_full, out_full, in_full, back_full = gathered
    seq_count, block_len, model_width = tokens.shape
    seq_len = block_len * lax.axis_size("seq")
    row_count = seq_count * block_len
    group_size = seq_count
    while group_size % 2 == 0 and group_size // 2 * block_len >= 512:
        group_size = group_size // 2
    group_count = seq_count // group_size
    flat_x = tokens.reshape(row_count, model_width).astype(jnp.float32)
    first_scale = rms_scale(flat_x)
    first_gain = gain_first.astype(jnp.float32)
    first_normed = (flat_x * first_scale * first_gain).astype(jnp.bfloat16)
    projected = jnp.dot(first_normed, qkv_full, preferred_element_type=jnp.float32).astype(
        jnp.bfloat16
    )
    queries = projected[:, :model_width].reshape(group_count, group_size, block_len, HEADS, HD)
    local_keys = projected[:, model_width : 2 * model_width].reshape(
        seq_count, block_len, model_width
    )
    local_values = projected[:, 2 * model_width :].reshape(seq_count, block_len, model_width)
    all_keys, all_values, all_segments = (
        lax.all_gather(local_keys, "seq", axis=1, tiled=True),
        lax.all_gather(local_values, "seq", axis=1, tiled=True),
        lax.all_gather(segment_ids, "seq", axis=1, tiled=True),
    )
    key_groups = all_keys.reshape(group_count, group_size, seq_len, HEADS, HD)
    value_groups = all_values.reshape(group_count, group_size, seq_len, HEADS, HD)
    segkey_groups = all_segments.reshape(group_count, group_size, seq_len)
    segquery_groups = segment_ids.reshape(group_count, group_size, block_len)
    offset = lax.axis_index("seq") * block_len
    query_places = offset + jnp.arange(block_len, dtype=jnp.int32)
    key_places = jnp.arange(seq_len, dtype=jnp.int32)
    buckets = bucket_of(key_places[None, :] - query_places[:, None])
    single_hot_vector = (
        buckets[None] == jnp.arange(BUCKETS, dtype=jnp.int32)[:, None, None]
    ).astype(jnp.bfloat16)
    bias_matrix = table_flat.reshape(BUCKETS, HEADS)
    complete_bias = jnp.einsum(
        "dto,dl->lto", single_hot_vector, bias_matrix, preferred_element_type=jnp.float32
    )

    def attend(group_items):
        query_part, key_part, value_part, seg_query, seg_key = group_items
        scores = group_scores(query_part, key_part, seg_query, seg_key, complete_bias)
        row_peak = jnp.max(scores, axis=-1, keepdims=True)
        shifted = jnp.exp(scores - row_peak)
        row_total = jnp.sum(shifted, axis=-1, keepdims=True)
        softmax_probabilities = (shifted / row_total).astype(jnp.bfloat16)
        attn_part = jnp.einsum(
            "ghqk,gkhd->gqhd", softmax_probabilities, value_part, preferred_element_type=jnp.float32
        )
        return (attn_part.astype(jnp.bfloat16), row_peak + jnp.log(row_total))

    attn_mixed, log_totals = lax.map(
        attend, (queries, key_groups, value_groups, segquery_groups, segkey_groups)
    )
    mixed_flat = attn_mixed.reshape(row_count, model_width)
    middle = flat_x + jnp.dot(mixed_flat, out_full, preferred_element_type=jnp.float32)
    second_scale = rms_scale(middle)
    second_gain = gain_second.astype(jnp.float32)
    second_normed = (middle * second_scale * second_gain).astype(jnp.bfloat16)
    hidden_pre = jnp.dot(second_normed, in_full, preferred_element_type=jnp.float32)
    hidden_float, gate_pullback = jax.vjp(smooth_gate, hidden_pre)
    hidden = hidden_float.astype(jnp.bfloat16)
    result = middle + jnp.dot(hidden, back_full, preferred_element_type=jnp.float32)
    output = result.astype(jnp.bfloat16).reshape(seq_count, block_len, model_width)
    grad_result = cotangent.reshape(row_count, model_width).astype(
        jnp.float32
    ) * valid_mask.reshape(row_count, 1).astype(jnp.float32)
    grad_branch = grad_result.astype(jnp.bfloat16)
    grad_back = jnp.einsum("tf,td->fd", hidden, grad_branch, preferred_element_type=jnp.float32)
    grad_hidden = jnp.einsum(
        "td,fd->tf", grad_branch, back_full, preferred_element_type=jnp.float32
    )
    grad_pre = gate_pullback(grad_hidden)[0].astype(jnp.bfloat16)
    grad_in = jnp.einsum("td,tf->df", second_normed, grad_pre, preferred_element_type=jnp.float32)
    grad_second_normed = jnp.einsum(
        "tf,df->td", grad_pre, in_full, preferred_element_type=jnp.float32
    )
    grad_middle_norm, grad_gain_second = norm_backward(
        middle, second_scale, second_gain, grad_second_normed
    )
    grad_middle = grad_result + grad_middle_norm
    grad_attn = grad_middle.astype(jnp.bfloat16)
    grad_out = jnp.einsum("td,te->de", mixed_flat, grad_attn, preferred_element_type=jnp.float32)
    grad_mixed = jnp.einsum(
        "te,de->td", grad_attn, out_full, preferred_element_type=jnp.float32
    ).astype(jnp.bfloat16)
    grad_mixed_groups = grad_mixed.reshape(group_count, group_size, block_len, HEADS, HD)
    backward_entries = (
        queries,
        key_groups,
        value_groups,
        segquery_groups,
        segkey_groups,
        log_totals,
        grad_mixed_groups,
    )
    bias_zero = jnp.zeros((HEADS, block_len, seq_len), jnp.float32)

    def full_backward(bias_total_sum, group_items):
        softmax_probabilities, grad_scores, grad_query, row_inner = query_backward(
            group_items, complete_bias
        )
        query_part = group_items[0]
        grad_part = group_items[6]
        key_gradient = jnp.einsum(
            "ghqk,gqhd->gkhd", grad_scores, query_part, preferred_element_type=jnp.float32
        )
        grad_value = jnp.einsum(
            "ghqk,gqhd->gkhd",
            softmax_probabilities.astype(jnp.bfloat16),
            grad_part,
            preferred_element_type=jnp.float32,
        )
        bias_total_sum = bias_total_sum + jnp.sum(grad_scores.astype(jnp.float32), axis=0)
        return (bias_total_sum, (grad_query, key_gradient, grad_value))

    bias_total_sum, (grad_queries, grad_keys, grad_values) = lax.scan(
        full_backward, bias_zero, backward_entries
    )
    key_terms = grad_keys.reshape(seq_count, seq_len, model_width)
    value_terms = grad_values.reshape(seq_count, seq_len, model_width)
    key_sum, value_sum = (
        lax.psum_scatter(
            key_terms.astype(jnp.bfloat16), "seq", scatter_dimension=1, tiled=True
        ).astype(jnp.float32),
        lax.psum_scatter(
            value_terms.astype(jnp.bfloat16), "seq", scatter_dimension=1, tiled=True
        ).astype(jnp.float32),
    )
    key_low = key_sum.astype(jnp.bfloat16)
    value_low = value_sum.astype(jnp.bfloat16)
    grad_projected = jnp.concatenate(
        [
            grad_queries.reshape(row_count, model_width),
            key_low.reshape(row_count, model_width),
            value_low.reshape(row_count, model_width),
        ],
        axis=1,
    )
    grad_qkv = jnp.einsum(
        "td,te->de", first_normed, grad_projected, preferred_element_type=jnp.float32
    )
    grad_first_normed = jnp.einsum(
        "te,de->td", grad_projected, qkv_full, preferred_element_type=jnp.float32
    )
    grad_x_norm, grad_gain_first = norm_backward(flat_x, first_scale, first_gain, grad_first_normed)
    grad_tokens = (
        (grad_middle + grad_x_norm).astype(jnp.bfloat16).reshape(seq_count, block_len, model_width)
    )
    grad_table = jnp.einsum(
        "fuy,suy->fs",
        single_hot_vector.astype(jnp.float32),
        bias_total_sum,
        precision=lax.Precision.HIGHEST,
    ).reshape(BUCKETS * HEADS)
    owned = (
        lax.psum_scatter(grad_gain_first, ("dp", "seq"), scatter_dimension=0, tiled=True),
        lax.psum_scatter(grad_gain_second, ("dp", "seq"), scatter_dimension=0, tiled=True),
        lax.psum_scatter(grad_table, ("dp", "seq"), scatter_dimension=0, tiled=True),
        lax.psum_scatter(grad_qkv, ("dp", "seq"), scatter_dimension=0, tiled=True),
        lax.psum_scatter(grad_out, ("dp", "seq"), scatter_dimension=0, tiled=True),
        lax.psum_scatter(grad_in, ("dp", "seq"), scatter_dimension=0, tiled=True),
        lax.psum_scatter(grad_back, ("dp", "seq"), scatter_dimension=0, tiled=True),
    )
    owned_gain_one, owned_gain_two, owned_table, owned_qkv, owned_out, owned_in, owned_back = owned
    return (
        output,
        grad_tokens,
        owned_gain_one,
        owned_gain_two,
        owned_table,
        owned_qkv,
        owned_out,
        owned_in,
        owned_back,
    )


MESH = pl.DeviceIdType.MESH

def flip(i, bit):
    return i + bit - 2 * bit * ((i // bit) % 2)

def forward_kernel(items, *refs):
    tok, cot, seg = refs[:3]
    shards = refs[3:8]
    xf, gf, out_full, in_full, back_full, w_ref, qkv_ref, o_ref, qa_ref, exk_ref, gains_ref, biasb_ref = refs[8:20]
    wv, sv, sf, exq_ref, fl_ref, fr_ref, bias_ref = refs[20:27]
    full = (wv, out_full, in_full, back_full, sv)
    loc_sem, t_send, t_recv, s_send, s_recv, g_send, g_recv, z_send, z_recv, h_send, h_recv = refs[27:]
    dp, z = lax.axis_index("dp"), lax.axis_index("seq")
    n_z = 4
    peers = [(dp, lax.rem(z + s, n_z)) for s in range(1, n_z)] + [(flip(dp, b), z) for b in (1, 2, 4)]
    barrier = pltpu.get_barrier_semaphore()
    for p in peers:
        pl.semaphore_signal(barrier, inc=1, device_id=p, device_id_type=MESH)
    pl.semaphore_wait(barrier, len(peers))

    def block(it, d, zz):
        return full[items[it][0]].at[d * n_z + zz]

    def own(it):
        return shards[items[it][0]]

    n_it = len(items)
    def z_copy(it, way, step):
        src_z = z - step if way == 0 else z + step
        src = own(it) if step == 0 else block(it, dp, src_z)
        return pltpu.make_async_remote_copy(
            src_ref=src, dst_ref=block(it, dp, src_z), send_sem=z_send.at[it, way, step],
            recv_sem=z_recv.at[it, way, step], device_id=(dp, z + 1 if way == 0 else z - 1), device_id_type=MESH)

    def z_wait(it, way, step):
        src_z = z - 1 - step if way == 0 else z + 1 + step
        blk = block(it, dp, src_z)
        pltpu.make_async_remote_copy(src_ref=blk, dst_ref=blk, send_sem=z_send.at[it, way, step],
            recv_sem=z_recv.at[it, way, step], device_id=(dp, z), device_id_type=MESH).wait_recv()

    def can_send(way, step):
        return (z >= step) & (z <= n_z - 2) if way == 0 else (z + step <= n_z - 1) & (z >= 1)

    def can_recv(way, step):
        return z >= step + 1 if way == 0 else z + 1 + step <= n_z - 1

    def z_start(it, step):
        for way in (0, 1):
            @pl.when(can_send(way, step))
            def _():
                z_copy(it, way, step).start()

    def z_recv_all(it, step):
        for way in (0, 1):
            @pl.when(can_recv(way, step))
            def _():
                z_wait(it, way, step)

    def hops(it):
        b1, b2 = items[it][1:]
        return [(0, b1), (0, b2), (b1, b2), (0, 1), (b1, 1), (b2, 1), (b1 + b2, 1)]

    def flips(d, mask):
        for b in (1, 2, 4):
            if mask & b:
                d = flip(d, b)
        return d

    def hop(it, slot, zz):
        mask, to = hops(it)[slot]
        blk = block(it, flips(dp, mask), zz)
        return pltpu.make_async_remote_copy(src_ref=blk, dst_ref=blk, send_sem=h_send.at[it, slot, zz],
            recv_sem=h_recv.at[it, slot, zz], device_id=(flip(dp, to), z), device_id_type=MESH)

    def hop_wait(it, slot, zz):
        mask, to = hops(it)[slot]
        blk = block(it, flips(dp, mask ^ to), zz)
        pltpu.make_async_remote_copy(src_ref=blk, dst_ref=blk, send_sem=h_send.at[it, slot, zz],
            recv_sem=h_recv.at[it, slot, zz], device_id=(dp, z), device_id_type=MESH).wait_recv()

    def own_hop(it, slot):
        to = hops(it)[slot][1]
        return pltpu.make_async_remote_copy(src_ref=own(it), dst_ref=block(it, dp, z), send_sem=h_send.at[it, slot, z],
            recv_sem=h_recv.at[it, slot, z], device_id=(flip(dp, to), z), device_id_type=MESH)

    def tok_copy(s, first, last):
        to = lax.rem(z + s, n_z)
        return [pltpu.make_async_remote_copy(src_ref=a.at[to], dst_ref=f.at[z], send_sem=ss.at[s - 1], recv_sem=rs.at[s - 1],
                device_id=(dp, to), device_id_type=MESH) for a, f, ss, rs in ((tok, xf, t_send, t_recv), (seg, sf, s_send, s_recv), (cot, gf, g_send, g_recv))[first:last]]

    def tok_wait(s, first, last):
        frm = lax.rem(z + n_z - s, n_z)
        for f, ss, rs in ((xf, t_send, t_recv), (sf, s_send, s_recv), (gf, g_send, g_recv))[first:last]:
            pltpu.make_async_remote_copy(src_ref=f.at[frm], dst_ref=f.at[frm], send_sem=ss.at[s - 1], recv_sem=rs.at[s - 1],
                device_id=(dp, z), device_id_type=MESH).wait_recv()

    for it in range(n_it):
        z_start(it, 0)
        for slot in (0, 1, 3):
            own_hop(it, slot).start()
    locs = []
    for it in range(n_it):
        locs.append(pltpu.make_async_copy(own(it), block(it, dp, z), loc_sem.at[it]))
    locs.append(pltpu.make_async_copy(tok.at[z], xf.at[z], loc_sem.at[n_it]))
    locs.append(pltpu.make_async_copy(seg.at[z], sf.at[z], loc_sem.at[n_it + 1]))
    locs.append(pltpu.make_async_copy(cot.at[z], gf.at[z], loc_sem.at[n_it + 2]))
    for c in locs:
        c.start()

    def forward(it, zz):
        hop_wait(it, 0, zz)
        hop(it, 2, zz).start()
        hop(it, 4, zz).start()
        hop_wait(it, 1, zz)
        hop(it, 5, zz).start()

    def arrivals(step):
        return [(can_recv(0, step), 0, z - 1 - step), (can_recv(1, step), 1, z + 1 + step)]

    def chain(it, step):
        for ok, way, zz in arrivals(step):
            @pl.when(ok)
            def _():
                z_wait(it, way, step)
                if step < n_z - 2:
                    @pl.when(can_send(way, step + 1))
                    def _():
                        z_copy(it, way, step + 1).start()
                for slot in (0, 1, 3):
                    hop(it, slot, zz).start()

    def pass_on(it, step):
        if step < 0:
            forward(it, z)
        else:
            for ok, way, zz in arrivals(step):
                @pl.when(ok)
                def _():
                    forward(it, zz)

    first, rest = (0, 1), tuple(range(2, n_it))
    for step in range(n_z - 1):
        for it in first:
            chain(it, step)
    for it in rest:
        chain(it, 0)
    for it in rest:
        chain(it, 1)
    for s in range(1, n_z):
        for c in tok_copy(s, 0, 2):
            c.start()
    for step in range(-1, n_z - 1):
        for it in first:
            pass_on(it, step)
    for it in rest:
        chain(it, 2)
    for it in rest:
        pass_on(it, -1)
    def last_hop(it):
        for zz in range(n_z):
            hop_wait(it, 2, zz)
            hop(it, 6, zz).start()

    def arrived(it):
        for zz in range(n_z):
            for slot in (3, 4, 5, 6):
                hop_wait(it, slot, zz)

    for it in first:
        last_hop(it)
    for it in rest:
        pass_on(it, 0)
    for it in first:
        arrived(it)
    for c in locs:
        c.wait()

    width = xf.shape[2]
    block_len = xf.shape[1]
    rows = n_z * block_len
    nblk = rows // 128
    n_dev = sv.shape[0]
    own_len = width // n_dev
    heads = qa_ref.shape[0]

    @pl.loop(0, n_dev // 2)
    def _(i):
        pair = [wv[2 * i].astype(F32), wv[2 * i + 1].astype(F32)]
        w_ref[pl.ds(pl.multiple_of(i * 48, 48), 48)] = jnp.concatenate(pair, axis=0).astype(BF)

    flat = sv[...].reshape(n_dev * 8, 128)
    pick = lax.broadcasted_iota(jnp.int32, (n_dev, n_dev * 8), 1) == 8 * lax.broadcasted_iota(jnp.int32, (n_dev, n_dev * 8), 0)
    small = exact(pick.astype(F32), flat, ((1,), (0,)))
    place = lax.broadcasted_iota(jnp.int32, (n_dev, width), 1)
    mine = place // own_len == lax.broadcasted_iota(jnp.int32, (n_dev, width), 0)
    from_lane = lax.broadcasted_iota(jnp.int32, (128, width), 0)
    to_lane = lax.broadcasted_iota(jnp.int32, (128, width), 1) % own_len
    for i in range(2):
        spread = exact(small, (from_lane == to_lane + i * own_len).astype(F32), ((1,), (0,)))
        gains_ref[i:i + 1] = jnp.sum(jnp.where(mine, spread, 0.0), axis=0, keepdims=True)
    bucket = lax.broadcasted_iota(jnp.int32, (n_dev, 512), 0)
    m = lax.broadcasted_iota(jnp.int32, (n_dev, 512), 1)
    bias_ref[...] = exact(small, (bucket_of((m + 127) % 512 - 255) == bucket).astype(F32), ((0,), (0,)))
    biasb_ref[...] = exact(small, (bucket_of(128 - m + jnp.where(m >= 384, 512, 0)) == bucket).astype(F32), ((0,), (0,)))

    for s in range(1, n_z):
        tok_wait(s, 0, 2)
    for s in range(1, n_z):
        for c in tok_copy(s, 2, 3):
            c.start()
    nb = rows.bit_length()
    lane = lax.broadcasted_iota(jnp.int32, (block_len, 128), 1) % 64
    rel = lane - (nblk + 3)
    inside = (rel >= 0) & (rel < 2 * nb)
    bit_of = lax.broadcasted_iota(jnp.int32, (16, 128), 0)
    rel16 = lax.broadcasted_iota(jnp.int32, (16, 128), 1) % 64 - (nblk + 3)
    to_bits = jnp.where(rel16 == 2 * bit_of, 1.0, jnp.where(rel16 == 2 * bit_of + 1, -1.0, 0.0)).astype(BF)
    for r in range(n_z):
        at = pl.ds(r * block_len, block_len)
        ids = jnp.broadcast_to(sf[r], (16, block_len))
        bits = (jnp.right_shift(ids, lax.broadcasted_iota(jnp.int32, ids.shape, 0)) & 1).astype(F32).astype(BF)
        u = mm(bits, to_bits, ((0,), (0,))) + jnp.where(inside & (rel % 2 == 1), 1.0, 0.0)
        exq_ref[at] = u.astype(BF)
        row_blk = r * (block_len // 128) + lax.broadcasted_iota(jnp.int32, (block_len, 128), 0) // 128
        unit = ((lane < nblk) & (lane == row_blk)) | ((lane >= nblk) & (lane < nblk + 3))
        exk_ref[at] = jnp.where(inside, jnp.where(u == 0.0, BIG, 0.0), jnp.where(unit, 1.0, 0.0)).astype(BF)
        fl_ref[at] = jnp.where((lane < nblk) & (lane <= row_blk - 2), 1.0, 0.0).astype(BF)
        fr_ref[at] = jnp.where((lane < nblk) & (lane >= row_blk + 2), 1.0, 0.0).astype(BF)
        x = xf[r].astype(F32)
        scale = lax.rsqrt(jnp.mean(x * x, axis=-1, keepdims=True) + EPS)
        normed = (x * scale * gains_ref[0:1]).astype(BF)
        qkv_ref[at] = mm(normed, w_ref[...]).astype(BF)
        if r == 2:
            for it in rest:
                pass_on(it, 1)

    plan = {0: [(pass_on, 2, 2), (pass_on, 3, 2), (pass_on, 4, 2)], 2: [(last_hop, 2), (last_hop, 3)], 3: [(last_hop, 4)]}

    @pl.loop(0, heads // 2)
    def _(hp):
        cols = [pl.ds(pl.multiple_of(i * width + hp * 128, 128), 128) for i in range(3)]
        lane = lax.broadcasted_iota(jnp.int32, (rows, 128), 1)
        lane1 = lax.broadcasted_iota(jnp.int32, (1, 128), 1)
        QB = 256
        outs = []
        for h in range(2):
            head = hp * 2 + h
            sel = (lane < 64) if h == 0 else (lane >= 64)
            strip = skewed(bias_ref[pl.ds(2 * own_len + head, 1)])
            side = [jnp.sum(jnp.where(lane1 == 2 * own_len + head, sv[d, 0:1], 0.0), axis=1, keepdims=True).astype(BF)
                    for d in (n_dev // 2 - 1, n_dev - 1)]
            qa = jnp.where(sel, qkv_ref[:, cols[0]], exq_ref[...] + fl_ref[...] * side[0] + fr_ref[...] * side[1])
            ka = jnp.where(sel, qkv_ref[:, cols[1]], exk_ref[...])
            va = jnp.where(sel, qkv_ref[:, cols[2]], jnp.ones((rows, 128), BF))
            lane_l = 64 * (1 - h)
            for blk in range(rows // QB):
                r0 = blk * QB
                qb = qa[r0:r0 + QB]
                s = mm(qb, ka, ((1,), (1,)))
                srows = []
                for sub in range(QB // 128):
                    I = blk * (QB // 128) + sub
                    lo = max(I - 1, 0)
                    hi = min(I + 1, nblk - 1)
                    srow = s[sub * 128:(sub + 1) * 128]
                    parts = []
                    if lo > 0:
                        parts.append(srow[:, :lo * 128])
                    parts.append(srow[:, lo * 128:(hi + 1) * 128] + strip[:, (lo - I + 1) * 128:(hi - I + 2) * 128])
                    if hi < nblk - 1:
                        parts.append(srow[:, (hi + 1) * 128:])
                    srows.append(jnp.concatenate(parts, axis=1))
                s = jnp.concatenate(srows, axis=0)
                top = jnp.max(s, axis=1, keepdims=True)
                p = jnp.exp2((s - top) * LOG2E).astype(BF)
                o = mm(p, va)
                l = o[:, lane_l:lane_l + 1]
                outs.append(o / l)
                lse = -top - jnp.log(l)
                hi_ = lse.astype(BF)
                rest = lse - hi_.astype(F32)
                mid = rest.astype(BF)
                low = (rest - mid.astype(F32)).astype(BF)
                base = 64 * (1 - h) + nblk
                ln = lane[:QB]
                qa_ref[head, r0:r0 + QB] = jnp.where(ln == base, hi_, jnp.where(ln == base + 1, mid, jnp.where(ln == base + 2, low, qb)))
        n = rows // QB
        for blk in range(n):
            o_ref[blk * QB:(blk + 1) * QB, cols[0]] = jnp.where(lane[:QB] < 64, outs[blk], outs[n + blk]).astype(BF)
        for k, calls in plan.items():
            @pl.when(hp == k)
            def _():
                for fn, *which in calls:
                    fn(*which)

    for it in range(2, n_it):
        arrived(it)
    for s in range(1, n_z):
        tok_wait(s, 2, 3)
    for it in range(n_it):
        for step in range(n_z - 1):
            for way in (0, 1):
                @pl.when(can_send(way, step))
                def _():
                    z_copy(it, way, step).wait_send()
        for zz in range(n_z):
            for slot in range(7):
                hop(it, slot, zz).wait_send()
    for s in range(1, n_z):
        for c in tok_copy(s, 0, 3):
            c.wait_send()

def forward(tokens, cot, seg, shards, items, collective_id=0):
    n_it = len(items)
    n_dev = 32
    n_z, block_len, width = tokens.shape
    rows = n_z * block_len
    heads = width // HD
    D = pltpu.SemaphoreType.DMA
    S = jax.ShapeDtypeStruct
    vm = pl.BlockSpec(memory_space=pltpu.VMEM)
    hbm = pl.BlockSpec(memory_space=pltpu.HBM)
    qkv, out, in_, back, small = shards
    return pl.pallas_call(
        functools.partial(forward_kernel, items),
        out_shape=[S(tokens.shape, BF), S(tokens.shape, BF)] + [S((n_dev, *a.shape), BF) for a in (out, in_, back)]
        + [S((width, 3 * width), BF), S((rows, 3 * width), BF), S((rows, width), BF), S((heads, rows, 128), BF), S((rows, 128), BF),
           S((8, width), F32), S((128, 512), F32)],
        in_specs=[vm] * (3 + len(shards)),
        out_specs=[vm, hbm, hbm, hbm, hbm] + [vm] * 7,
        scratch_shapes=[pltpu.VMEM((n_dev, *qkv.shape), BF), pltpu.VMEM((n_dev, *small.shape), F32), pltpu.VMEM(seg.shape, seg.dtype),
                        pltpu.VMEM((rows, 128), BF), pltpu.VMEM((rows, 128), BF), pltpu.VMEM((rows, 128), BF), pltpu.VMEM((128, 512), F32),
                        D((n_it + 3,)), D((3,)), D((3,)), D((3,)), D((3,)), D((3,)), D((3,)), D((n_it, 2, 3)), D((n_it, 2, 3)),
                        D((n_it, 7, 4)), D((n_it, 7, 4))],
        compiler_params=pltpu.CompilerParams(collective_id=collective_id, has_side_effects=True, vmem_limit_bytes=60 << 20),
    )(tokens, cot, seg, *shards)


LOG2E = 1.4426950408889634
BIG = -1e30
F32 = jnp.float32
BF = jnp.bfloat16

def skewed(row):
    return pltpu.roll(jnp.broadcast_to(row, (128, 512)), 0, 1, stride=1, stride_axis=0)[:, :384]


def diagonal_sums(near):
    rows = 64
    x = jnp.concatenate([near, jnp.zeros((128, 128), F32)], axis=1)
    while rows >= 1:
        x = x[:rows] + pltpu.roll(x[rows:], 512 - rows, 1)
        rows //= 2
    return x


GELU_A = 0.7978845608028654
GELU_B = 0.044715


def mm(a, b, dims=((1,), (0,))):
    return lax.dot_general(a, b, (dims, ((), ())), preferred_element_type=F32)


def ffn_kernel(x_ref, mixed_ref, g_ref, gain_ref, wo_ref, wi_ref, wb_ref,
               out_ref, gm_ref, gmix_ref, dwo_ref, dwi_ref, dwb_ref, dgain_ref,
               mid_ref, h_ref, ht_ref, acc_ref, dh_ref):
    step = pl.program_id(0)
    rows = x_ref.shape[0]
    half = 256

    @pl.when(step == 0)
    def _():
        for r in range(0, rows, half):
            part = pl.ds(r, half)
            middle = x_ref[part].astype(F32) + mm(mixed_ref[part], wo_ref[...])
            mid_ref[part] = middle
            acc_ref[part] = middle
            scale = lax.rsqrt(jnp.mean(middle * middle, axis=-1, keepdims=True) + EPS)
            normed = (middle * scale * gain_ref[...]).astype(BF)
            h_ref[part] = normed
            ht_ref[:, part] = normed.T
            dh_ref[part] = jnp.zeros((half, x_ref.shape[1]), F32)

    gates = []
    hiddens = []
    for r in range(0, rows, half):
        part = pl.ds(r, half)
        pre = mm(h_ref[part], wi_ref[...])
        dhid = mm(g_ref[part], wb_ref[...], ((1,), (1,)))
        sq = pre * pre
        t = jnp.tanh(pre * (GELU_A + GELU_A * GELU_B * sq))
        half_t = 0.5 + 0.5 * t
        hidden = (pre * half_t).astype(BF)
        slope = half_t + pre * (0.5 - 0.5 * t * t) * (GELU_A + 3.0 * GELU_A * GELU_B * sq)
        dpre = (dhid * slope).astype(BF)
        acc_ref[part] += mm(hidden, wb_ref[...])
        dh_ref[part] += mm(dpre, wi_ref[...], ((1,), (1,)))
        hiddens.append(hidden)
        gates.append(dpre)
    dwi_ref[...] = mm(ht_ref[...], jnp.concatenate(gates, axis=0)).astype(BF)
    dwb_ref[...] = mm(jnp.concatenate(hiddens, axis=0), g_ref[...], ((0,), (0,))).astype(BF)

    @pl.when(step == pl.num_programs(0) - 1)
    def _():
        dgain = jnp.zeros((1, x_ref.shape[1]), F32)
        for r in range(0, rows, half):
            part = pl.ds(r, half)
            out_ref[part] = acc_ref[part].astype(BF)
            middle = mid_ref[part]
            dh = dh_ref[part]
            scale = lax.rsqrt(jnp.mean(middle * middle, axis=-1, keepdims=True) + EPS)
            dgain += jnp.sum(dh * (middle * scale), axis=0, keepdims=True)
            u = dh * gain_ref[...]
            inner = jnp.mean(u * middle, axis=-1, keepdims=True)
            gm = g_ref[part].astype(F32) + scale * u - middle * (scale * scale * scale * inner)
            gm_ref[part] = gm
            low = gm.astype(BF)
            h_ref[part] = low
            gmix_ref[part] = mm(low, wo_ref[...], ((1,), (1,))).astype(BF)
        dgain_ref[...] = dgain
        dwo_ref[...] = mm(mixed_ref[...], h_ref[...], ((0,), (0,))).astype(BF)


def ffn(x, mixed, g, gain, wo, wi, wb, chunk=512):
    rows, width = x.shape
    ff = wi.shape[1]
    whole = lambda s: pl.BlockSpec(s, lambda i: (0, 0), pipeline_mode=pl.Buffered(1))
    S = jax.ShapeDtypeStruct
    return pl.pallas_call(
        ffn_kernel,
        grid=(ff // chunk,),
        in_specs=[whole((rows, width))] * 3 + [whole((1, width)), whole((width, width)),
                  pl.BlockSpec((width, chunk), lambda i: (0, i)), pl.BlockSpec((chunk, width), lambda i: (i, 0))],
        out_specs=[whole((rows, width))] * 3 + [whole((width, width)), pl.BlockSpec((width, chunk), lambda i: (0, i)),
                   pl.BlockSpec((chunk, width), lambda i: (i, 0)), whole((1, width))],
        out_shape=[S((rows, width), BF), S((rows, width), F32), S((rows, width), BF), S((width, width), BF),
                   S((width, ff), BF), S((ff, width), BF), S((1, width), F32)],
        scratch_shapes=[pltpu.VMEM((rows, width), F32), pltpu.VMEM((rows, width), BF), pltpu.VMEM((width, rows), BF),
                        pltpu.VMEM((rows, width), F32), pltpu.VMEM((rows, width), F32)],
        compiler_params=pltpu.CompilerParams(vmem_limit_bytes=56 << 20),
        cost_estimate=pl.CostEstimate(flops=12 * rows * width * ff + 6 * rows * width * width, bytes_accessed=50 << 20, transcendentals=rows * ff),
    )(x, mixed, g, gain, wo, wi, wb)


def back_kernel(chunks, n_early, *refs):
    n_it, n_arr, n_z = len(chunks), 5, 4
    (qa_ref, qkv_ref, do_ref, o_ref, exk_ref, bias_ref, x_ref, gm_ref, gain_ref, gain2_ref, w_ref, y_ref) = refs[:12]
    p_out, p_in, p_back = refs[12:15]
    gx_out, y_out = refs[15:17]
    outs = refs[17:17 + n_arr]
    scr = refs[17 + n_arr:]
    k_ref, v_ref, p_qkv, p_small, gx, ht_ref, dqt_ref, dq_ref, dk_ref, dv_ref, diag_ref = scr[:11]
    scr = scr[11:]
    part = (p_qkv, p_small, p_out, p_in, p_back)
    rc, r2, r1, zo, zu, zd = (scr[k * n_it:(k + 1) * n_it] for k in range(6))
    stg = scr[6 * n_it:6 * n_it + n_early]
    (loc_sem, own_sem, t_send, t_recv, y_send, y_recv, c_send, c_recv, x2_send, x2_recv, x1_send, x1_recv,
     z_send, z_recv) = scr[6 * n_it + n_early:]
    dp, z = lax.axis_index("dp"), lax.axis_index("seq")
    core = lax.rem(dp, 2)
    quad = dp // 2
    peers = [(dp, lax.rem(z + s, n_z)) for s in range(1, n_z)] + [(flip(dp, b), z) for b in (1, 2, 4)]
    barrier = pltpu.get_barrier_semaphore()
    for p in peers:
        pl.semaphore_signal(barrier, inc=1, device_id=p, device_id_type=MESH)
    pl.semaphore_wait(barrier, len(peers))

    def remote(src, dst, ss, rs, to):
        return pltpu.make_async_remote_copy(src_ref=src, dst_ref=dst, send_sem=ss, recv_sem=rs, device_id=to, device_id_type=MESH)

    def piece(it, d):
        a, c0, w = chunks[it][:3]
        return part[a].at[d, :, pl.ds(c0, w)]

    def own_copy(it, q):
        return pltpu.make_async_copy(piece(it, 2 * q + core), stg[it].at[q], own_sem.at[it, q])

    def add_into(dst, src, chunk=16):
        rows = dst.shape[0]
        chunk = min(chunk, rows)
        @pl.loop(0, rows // chunk)
        def _(i):
            at = pl.ds(pl.multiple_of(i * chunk, chunk), chunk)
            dst[at] = dst[at] + src[at]

    def q_at(it, f1, f2):
        b1, b2 = chunks[it][3:]
        q = quad
        if f1: q = flip(q, b1 // 2)
        if f2: q = flip(q, b2 // 2)
        return q

    def c_copy(it, q):
        return remote(piece(it, 2 * q + 1 - core), rc[it].at[q], c_send.at[it, q], c_recv.at[it, q], (flip(dp, 1), z))

    def x2_copy(it, f1):
        q = q_at(it, f1, True)
        k = (q // (chunks[it][3] // 2)) % 2
        return remote(rc[it].at[q], r2[it].at[k], x2_send.at[it, k], x2_recv.at[it, k], (flip(dp, chunks[it][4]), z))

    def x1_copy(it):
        return remote(rc[it].at[q_at(it, True, False)], r1[it], x1_send.at[it], x1_recv.at[it], (flip(dp, chunks[it][3]), z))

    def rows_copy(src, dst, ss, rs, s):
        to = lax.rem(z + s, n_z)
        return remote(src.at[to], dst.at[z], ss.at[s - 1], rs.at[s - 1], (dp, to))

    def rows_wait(dst, ss, rs, s):
        frm = lax.rem(z + n_z - s, n_z)
        remote(dst.at[frm], dst.at[frm], ss.at[s - 1], rs.at[s - 1], (dp, z)).wait_recv()

    def core_start(it):
        for f1, f2 in ((True, True), (False, True), (True, False), (False, False)):
            c_copy(it, q_at(it, f1, f2)).start()

    def core_sum(it, f1, f2):
        q = q_at(it, f1, f2)
        c_copy(it, q).wait_recv()
        if it < n_early:
            own_copy(it, q).wait()
            add_into(rc[it].at[q], stg[it].at[q])
        else:
            add_into(rc[it].at[q], piece(it, 2 * q + core))

    def stage_core(it):
        for f1 in (True, False):
            core_sum(it, f1, True)
            x2_copy(it, f1).start()
        for f1 in (True, False):
            core_sum(it, f1, False)

    def stage_x2(it):
        for f1 in (True, False):
            q = q_at(it, f1, False)
            k = (q // (chunks[it][3] // 2)) % 2
            remote(rc[it].at[0], r2[it].at[k], x2_send.at[it, k], x2_recv.at[it, k], (dp, z)).wait_recv()
            add_into(rc[it].at[q], r2[it].at[k])
            if f1:
                x1_copy(it).start()

    def z_copy(it, way, j):
        src = zo[it].at[j]
        dst = (zu if way == 0 else zd)[it].at[j]
        return remote(src, dst, z_send.at[it, way, j], z_recv.at[it, way, j], (dp, z + 1 if way == 0 else z - 1))

    def z_add(it, way, j):
        buf = (zu if way == 0 else zd)[it]
        remote(buf.at[j], buf.at[j], z_send.at[it, way, j], z_recv.at[it, way, j], (dp, z)).wait_recv()
        zo[it][j] = (zo[it][j].astype(F32) + buf[j].astype(F32)).astype(zo[it].dtype)

    def stage_x1(it):
        x1_copy(it).wait_recv()
        rows = zo[it].shape[1]
        for j in range(n_z):
            at = pl.ds(j * rows, rows)
            zo[it][j] = (rc[it][quad, at].astype(F32) + r1[it][at].astype(F32)).astype(zo[it].dtype)
        stage_z(it, 0)

    def stage_z(it, s):
        for way, here in ((0, s), (1, n_z - 1 - s)):
            @pl.when(z == here)
            def _():
                for j in (range(n_z - 1, here, -1) if way == 0 else range(here)):
                    if s > 0:
                        z_add(it, way, j)
                    z_copy(it, way, j).start()

    def stage_end(it):
        a, c0, w = chunks[it][:3]
        col = pl.ds(c0, w)
        outs[a][:, col] = zo[it][z].astype(F32)
        for way, ok in ((0, z > 0), (1, z < n_z - 1)):
            @pl.when(ok)
            def _():
                buf = (zu if way == 0 else zd)[it].at[z]
                remote(buf, buf, z_send.at[it, way, z], z_recv.at[it, way, z], (dp, z)).wait_recv()
                outs[a][:, col] += buf[...].astype(F32)

    stage_z1, stage_z2 = functools.partial(stage_z, s=1), functools.partial(stage_z, s=2)
    width = x_ref.shape[2]
    rows = n_z * x_ref.shape[1]
    nblk = rows // 128
    heads = qa_ref.shape[0]
    plan = {
        -1: [(stage_core, 0), (stage_core, 1)],
        0: [(stage_core, 4), (stage_core, 5)],
        4: [(stage_x2, 0), (stage_x2, 1), (stage_core, 2), (stage_core, 3)],
        5: [(stage_x2, 4), (stage_x2, 5)],
        7: [(stage_x1, 0), (stage_x1, 1)],
        8: [(stage_z1, 0), (stage_z1, 1)],
        9: [(stage_z2, 0), (stage_z2, 1)],
        11: [(stage_x2, 2), (stage_x2, 3)],
    }
    for it in range(n_early):
        core_start(it)
        for q in range(4):
            own_copy(it, q).start()
    kv = [pltpu.make_async_copy(qkv_ref.at[:, pl.ds((i + 1) * width, width)], ref, loc_sem.at[2 + i]) for i, ref in enumerate((k_ref, v_ref))]
    for c in kv:
        c.start()
    y_loc = pltpu.make_async_copy(y_ref.at[z], y_out.at[z], loc_sem.at[0])
    y_loc.start()
    for s in range(1, n_z):
        rows_copy(y_ref, y_out, y_send, y_recv, s).start()
    for fn, it in plan[-1]:
        fn(it)
    for c in kv:
        c.wait()

    diag_ref[...] = jnp.zeros_like(diag_ref)
    lane = lax.broadcasted_iota(jnp.int32, (rows, 128), 1)
    kb_rows = 256
    nsub = kb_rows // 128

    @pl.loop(0, heads)
    def _(h):
        par = lax.rem(h, 2)
        cols = pl.ds(pl.multiple_of((h // 2) * 128, 128), 128)
        sel = lane // 64 == par
        spare = lane % 64 - nblk
        strip = skewed(bias_ref[pl.ds(2 * (width // 32) + h, 1)])
        qa = qa_ref[h]
        ka = jnp.where(sel, k_ref[:, cols], exk_ref[...])
        ones = jnp.where((spare >= 0) & (spare < 3), 1.0, 0.0).astype(BF)
        va = jnp.where(sel, v_ref[:, cols], ones)
        prod = do_ref[:, cols].astype(F32) * o_ref[:, cols].astype(F32)
        delta = -jnp.sum(jnp.where(sel, prod, 0.0), axis=1, keepdims=True)
        hi_ = delta.astype(BF)
        rest = delta - hi_.astype(F32)
        mid = rest.astype(BF)
        low = (rest - mid.astype(F32)).astype(BF)
        extra = jnp.where(spare == 0, hi_, jnp.where(spare == 1, mid, jnp.where(spare == 2, low, jnp.zeros((rows, 128), BF))))
        doa = jnp.where(sel, do_ref[:, cols], extra)
        near = jnp.zeros((128, 384), F32)
        for kb in range(rows // kb_rows):
            r0 = kb * kb_rows
            kab = ka[r0:r0 + kb_rows]
            s = mm(kab, qa, ((1,), (1,)))
            dp_ = mm(va[r0:r0 + kb_rows], doa, ((1,), (1,)))
            prow, dsrow = [], []
            for sub in range(nsub):
                J = kb * nsub + sub
                lo = max(J - 1, 0)
                hi = min(J + 1, nblk - 1)
                srow = s[sub * 128:(sub + 1) * 128]
                parts = []
                if lo > 0:
                    parts.append(srow[:, :lo * 128])
                parts.append(srow[:, lo * 128:(hi + 1) * 128] + strip[:, (lo - J + 1) * 128:(hi - J + 2) * 128])
                if hi < nblk - 1:
                    parts.append(srow[:, (hi + 1) * 128:])
                p = jnp.exp2(jnp.concatenate(parts, axis=1) * LOG2E)
                ds = p * dp_[sub * 128:(sub + 1) * 128]
                nr = ds[:, lo * 128:(hi + 1) * 128]
                if lo > J - 1:
                    nr = jnp.concatenate([jnp.zeros((128, 128), F32), nr], axis=1)
                if hi < J + 1:
                    nr = jnp.concatenate([nr, jnp.zeros((128, 128), F32)], axis=1)
                near = near + nr
                prow.append(p.astype(BF))
                dsrow.append(ds.astype(BF))
            pb = jnp.concatenate(prow, axis=0)
            dsb = jnp.concatenate(dsrow, axis=0)
            at = pl.ds(r0, kb_rows)
            dv_ref[at, cols] = jnp.where(sel[:kb_rows], mm(pb, doa).astype(BF), dv_ref[at, cols])
            dk_ref[at, cols] = jnp.where(sel[:kb_rows], mm(dsb, qa).astype(BF), dk_ref[at, cols])
            dqt = mm(kab, dsb, ((0,), (0,)))
            dqt_ref[...] = dqt if kb == 0 else dqt_ref[...] + dqt
        far = dqt_ref[pl.ds(pl.multiple_of(64 - 64 * par, 64), 8)]
        key_block = lax.broadcasted_iota(jnp.int32, far.shape, 0)
        query_block = lax.broadcasted_iota(jnp.int32, far.shape, 1) // 128
        left = jnp.sum(jnp.where(key_block <= query_block - 2, far, 0.0))
        right = jnp.sum(jnp.where(key_block >= query_block + 2, far, 0.0))
        column = lax.broadcasted_iota(jnp.int32, (1, 512), 1)
        diag_ref[pl.ds(h, 1)] = diagonal_sums(near) + jnp.where(column == 383, left, 0.0) + jnp.where(column == 385, right, 0.0)
        dq_ref[pl.ds(pl.multiple_of(h * 64, 64), 64)] = dqt_ref[pl.ds(pl.multiple_of(64 * par, 64), 64)].astype(BF)
        for k in range(heads):
            if k in plan:
                @pl.when(h == k)
                def _():
                    for fn, it in plan[k]:
                        fn(it)

    half = rows // n_z
    dgain = jnp.zeros((1, width), F32)

    def scaled(r):
        x = x_ref[r].astype(F32)
        return x, lax.rsqrt(jnp.mean(x * x, axis=-1, keepdims=True) + EPS)

    gx_loc = pltpu.make_async_copy(gx.at[z], gx_out.at[z], loc_sem.at[1])
    for r in range(n_z):
        at = pl.ds(r * half, half)
        x, scale = scaled(r)
        ht_ref[:, at] = (x * scale * gain_ref[0:1]).astype(BF).T
        dh = mm(dq_ref[:, at], w_ref[:, :width], ((0,), (1,)))
        dh += mm(dk_ref[at], w_ref[:, width:2 * width], ((1,), (1,)))
        dh += mm(dv_ref[at], w_ref[:, 2 * width:], ((1,), (1,)))
        dgain += jnp.sum(dh * (x * scale), axis=0, keepdims=True)
        u = dh * gain_ref[0:1]
        inner = jnp.mean(u * x, axis=-1, keepdims=True)
        gx[r] = (gm_ref[at] + scale * u - x * (scale * scale * scale * inner)).astype(BF)
    for it in X1_BEFORE:
        stage_x1(it)
    for s in range(1, n_z):
        rows_copy(gx, gx_out, t_send, t_recv, s).start()
    for it in X1_AFTER:
        stage_x1(it)
    gx_loc.start()
    for i in range(3):
        w0 = i * width
        if i == 0:
            dw = mm(ht_ref[...], dq_ref[...], ((1,), (1,)))
        else:
            dw = mm(ht_ref[...], (dk_ref, dv_ref)[i - 1][...])
        dw = dw.astype(BF)
        for d in range(8):
            p_qkv[d, :, w0:w0 + width] = dw[d * 96:(d + 1) * 96]
        if i == 1:
            core_start(6)
            for it in X1_BEFORE:
                stage_z1(it)
    core_start(7)
    stage_core(6)
    stage_core(7)
    n_dev = 32
    own = width // n_dev
    place = lax.broadcasted_iota(jnp.int32, (n_dev, width), 1)
    mine = place // own == lax.broadcasted_iota(jnp.int32, (n_dev, width), 0)
    col = lax.broadcasted_iota(jnp.int32, (width, 128), 1)
    row = lax.broadcasted_iota(jnp.int32, (width, 128), 0) % own
    small = jnp.zeros((n_dev, 128), F32)
    for i, g in enumerate((dgain, gain2_ref[...])):
        small += exact(jnp.where(mine, g, 0.0), (col == row + i * own).astype(F32), ((1,), (0,)))
    m = lax.broadcasted_iota(jnp.int32, (n_dev, 512), 1)
    hot = bucket_of(128 - m + jnp.where(m >= 384, 512, 0)) == lax.broadcasted_iota(jnp.int32, (n_dev, 512), 0)
    sums = exact(hot.astype(F32), diag_ref[...], ((1,), (1,)))
    col = lax.broadcasted_iota(jnp.int32, (16, 128), 1)
    row = lax.broadcasted_iota(jnp.int32, (16, 128), 0)
    small += exact(sums, ((col == row + 2 * own) & (row < heads)).astype(F32), ((1,), (0,)))
    for d in range(8):
        p_small[d] = small[d * n_z:(d + 1) * n_z]
    core_start(8)
    stage_core(8)
    for fn, its in (
        (stage_z1, X1_AFTER),
        (stage_z2, X1_BEFORE),
        (stage_x2, (6, 7, 8)),
        (stage_z2, X1_AFTER),
        (stage_x1, (6, 7, 8)),
        (stage_z1, (6, 7, 8)),
        (stage_z2, (6, 7, 8)),
        (stage_end, range(n_it)),
    ):
        for it in its:
            fn(it)
    for s in range(1, n_z):
        rows_wait(y_out, y_send, y_recv, s)
        rows_wait(gx_out, t_send, t_recv, s)
    y_loc.wait()
    gx_loc.wait()
    for s in range(1, n_z):
        rows_copy(y_ref, y_out, y_send, y_recv, s).wait_send()
        rows_copy(gx, gx_out, t_send, t_recv, s).wait_send()
    for it in range(n_it):
        for q in range(4):
            c_copy(it, q).wait_send()
        for f1 in (True, False):
            x2_copy(it, f1).wait_send()
        x1_copy(it).wait_send()
        for j in range(n_z):
            for way in (0, 1):
                @pl.when(j > z if way == 0 else j < z)
                def _():
                    z_copy(it, way, j).wait_send()


X1_BEFORE = ()
X1_AFTER = (4, 5, 2, 3)


def exact(a, b, dims):
    return lax.dot_general(a, b, (dims, ((), ())), preferred_element_type=F32, precision=lax.Precision.HIGHEST)


def backward(qa, qkv, do, o, exk, bias, x, gm, gain, dgain2, w, y, g_out, g_in, g_back, chunks, n_early, collective_id=1):
    width = x.shape[2]
    rows = x.shape[0] * x.shape[1]
    n_it = len(chunks)
    D = pltpu.SemaphoreType.DMA
    S = jax.ShapeDtypeStruct
    parts = (S((8, 96, 3 * width), BF), S((8, 4, 128), F32), g_out, g_in, g_back)

    def V(c, *lead):
        p = parts[c[0]]
        return pltpu.VMEM((*lead, p.shape[1], c[2]), p.dtype)

    def zs(c):
        p = parts[c[0]]
        return pltpu.VMEM((4, p.shape[1] // 4, c[2]), p.dtype)

    vm = pl.BlockSpec(memory_space=pltpu.VMEM)
    hbm = pl.BlockSpec(memory_space=pltpu.HBM)
    scratch = [pltpu.VMEM((rows, width), BF), pltpu.VMEM((rows, width), BF), pltpu.VMEM(parts[0].shape, BF), pltpu.VMEM((8, 4, 128), F32), pltpu.VMEM((4, rows // 4, width), BF),
               pltpu.VMEM((width, rows), BF), pltpu.VMEM((128, rows), F32), pltpu.VMEM((width, rows), BF),
               pltpu.VMEM((rows, width), BF), pltpu.VMEM((rows, width), BF), pltpu.VMEM((16, 512), F32)]
    scratch += [V(c, 4) for c in chunks] + [V(c, 2) for c in chunks] + [V(c) for c in chunks] + [zs(c) for c in chunks] * 3
    scratch += [V(c, 4) for c in chunks[:n_early]]
    scratch += [D((4,)), D((n_early, 4)), D((3,)), D((3,)), D((3,)), D((3,)), D((n_it, 4)), D((n_it, 4)), D((n_it, 2)), D((n_it, 2)),
                D((n_it,)), D((n_it,)), D((n_it, 2, 4)), D((n_it, 2, 4))]
    return pl.pallas_call(
        functools.partial(back_kernel, chunks, n_early),
        out_shape=[S((4, rows // 4, width), BF)] * 2 + [S((p.shape[1] // 4, p.shape[2]), F32) for p in parts],
        in_specs=[vm, hbm] + [vm] * 9 + [hbm] * 4,
        out_specs=[hbm] * 2 + [vm] * 5,
        scratch_shapes=scratch,
        compiler_params=pltpu.CompilerParams(collective_id=collective_id, has_side_effects=True, vmem_limit_bytes=63 << 20),
    )(qa, qkv, do, o, exk, bias, x, gm, gain, dgain2, w, y, g_out, g_in, g_back)


def fits(mesh):
    return mesh.shape["dp"] == 8 and mesh.shape["seq"] == 4


ITEMS = ((0, 4, 2), (4, 2, 4), (1, 2, 4), (2, 4, 2), (3, 2, 4))
ROUTES = (
    (3, 0, 1536, 4, 2),
    (3, 1536, 1536, 2, 4),
    (4, 0, 384, 4, 2),
    (4, 384, 384, 2, 4),
    (2, 0, 384, 4, 2),
    (2, 384, 384, 2, 4),
    (0, 0, 1152, 4, 2),
    (0, 1152, 1152, 2, 4),
    (1, 0, 128, 2, 4),
)
EARLY = 6


def fast_shards(
    tokens,
    segment_ids,
    valid_mask,
    cotangent,
    gain_one,
    gain_two,
    bias_table,
    qkv_weight,
    out_weight,
    in_weight,
    back_weight,
):
    n_z = lax.axis_size("seq")
    seq_count, block_len, width = tokens.shape
    seq_len = n_z * block_len
    g_rows, t_rows = gain_one.shape[0], bias_table.shape[0]
    small = jnp.concatenate([gain_one, gain_two, bias_table]).astype(F32)
    small = jnp.pad(small[None], ((0, 7), (0, 128 - small.shape[0])))
    x4, g4, out_full, in_full, back_full, qkv_full, projected, mixed, q_aug, exk, gains, bias_back = forward(
        tokens,
        cotangent * valid_mask[..., None].astype(BF),
        segment_ids.reshape(seq_count, 1, block_len),
        (qkv_weight, out_weight, in_weight, back_weight, small),
        ITEMS,
    )
    x = x4.reshape(seq_len, width)
    g_low = g4.reshape(seq_len, width)
    out_full = out_full.reshape(width, width)
    in_full = in_full.reshape(width, -1)
    back_full = back_full.reshape(-1, width)
    result, grad_middle, grad_mixed, grad_out, grad_in, grad_back, grad_gain_second = ffn(
        x, mixed, g_low, gains[1:2], out_full, in_full, back_full
    )
    grad_tokens, output, own_qkv, own_small, own_out, own_in, own_back = backward(
        q_aug,
        projected,
        grad_mixed,
        mixed,
        exk,
        bias_back,
        x4,
        grad_middle,
        gains,
        grad_gain_second,
        qkv_full,
        result.reshape(n_z, block_len, width),
        grad_out.reshape(8, -1, width),
        grad_in.reshape(8, -1, in_full.shape[1]),
        grad_back.reshape(8, -1, width),
        ROUTES,
        EARLY,
    )
    own_small = own_small[0]
    return (
        output,
        grad_tokens,
        own_small[:g_rows],
        own_small[g_rows : 2 * g_rows],
        own_small[2 * g_rows : 2 * g_rows + t_rows],
        own_qkv,
        own_out,
        own_in,
        own_back,
    )


def solution(mesh):
    in_specs = (
        P("dp", "seq", None),
        P("dp", "seq"),
        P("dp", "seq"),
        P("dp", "seq", None),
        P(("dp", "seq")),
        P(("dp", "seq")),
        P(("dp", "seq")),
        P(("dp", "seq"), None),
        P(("dp", "seq"), None),
        P(("dp", "seq"), None),
        P(("dp", "seq"), None),
    )
    out_specs = (
        P("dp", "seq", None),
        P("dp", "seq", None),
        P(("dp", "seq")),
        P(("dp", "seq")),
        P(("dp", "seq")),
        P(("dp", "seq"), None),
        P(("dp", "seq"), None),
        P(("dp", "seq"), None),
        P(("dp", "seq"), None),
    )
    return jax.shard_map(fast_shards if fits(mesh) else general_shards, mesh=mesh, in_specs=in_specs, out_specs=out_specs, check_vma=False)
```

```python
import functools

import jax
import jax.numpy as jnp
from jax import lax
from jax.experimental import pallas as pl
from jax.experimental.pallas import tpu as pltpu
from jax.sharding import PartitionSpec as P

HEADS = 12
HD = 64
BUCKETS = 32


EPS = 1e-06
NEGATIVE = -1e30
bucket_limits = (12, 16, 23, 32, 46, 64, 91)


def bucket_of(relative):
    distance = jnp.abs(relative)
    counted = jnp.zeros_like(distance)
    for threshold in bucket_limits:
        counted = counted + (distance >= threshold).astype(jnp.int32)
    inside = jnp.where(distance < 8, distance, 8 + counted)
    return inside + 16 * (relative > 0).astype(jnp.int32)


def rms_scale(values):
    return lax.rsqrt(jnp.mean(values * values, axis=-1, keepdims=True) + EPS)


def smooth_gate(values):
    return jax.nn.gelu(values, approximate=True)


def norm_backward(values, scale_inv, gain_vec, grad_normed):
    weighted = grad_normed * gain_vec
    grad_gain = jnp.sum(grad_normed * values * scale_inv, axis=0)
    cubed = scale_inv * scale_inv * scale_inv
    grad_values = scale_inv * weighted - values * cubed * jnp.mean(
        weighted * values, axis=-1, keepdims=True
    )
    return (grad_values, grad_gain)


def group_scores(query_part, key_part, seg_query, seg_key, complete_bias):
    scores = (
        jnp.einsum("gqhd,gkhd->ghqk", query_part, key_part, preferred_element_type=jnp.float32)
        + complete_bias[None]
    )
    allowed = (seg_query[:, :, None] == seg_key[:, None, :])[:, None]
    return jnp.where(allowed, scores, NEGATIVE)


def query_backward(items, complete_bias):
    query_part, key_part, value_part, seg_query, seg_key, log_total, grad_part = items
    scores = group_scores(query_part, key_part, seg_query, seg_key, complete_bias)
    softmax_probabilities = jnp.exp(scores - log_total)
    grad_probs = jnp.einsum(
        "gqhd,gkhd->ghqk", grad_part, value_part, preferred_element_type=jnp.float32
    )
    row_inner = jnp.sum(softmax_probabilities * grad_probs, axis=-1, keepdims=True)
    grad_scores = (softmax_probabilities * (grad_probs - row_inner)).astype(jnp.bfloat16)
    grad_query = jnp.einsum(
        "ghqk,gkhd->gqhd", grad_scores, key_part, preferred_element_type=jnp.float32
    ).astype(jnp.bfloat16)
    return (softmax_probabilities, grad_scores, grad_query, row_inner)


def general_shards(
    tokens,
    segment_ids,
    valid_mask,
    cotangent,
    gain_one,
    gain_two,
    bias_table,
    qkv_weight,
    out_weight,
    in_weight,
    back_weight,
):
    gathered = (
        lax.all_gather(gain_one, ("dp", "seq"), axis=0, tiled=True),
        lax.all_gather(gain_two, ("dp", "seq"), axis=0, tiled=True),
        lax.all_gather(bias_table, ("dp", "seq"), axis=0, tiled=True),
        lax.all_gather(qkv_weight, ("dp", "seq"), axis=0, tiled=True),
        lax.all_gather(out_weight, ("dp", "seq"), axis=0, tiled=True),
        lax.all_gather(in_weight, ("dp", "seq"), axis=0, tiled=True),
        lax.all_gather(back_weight, ("dp", "seq"), axis=0, tiled=True),
    )
    gain_first, gain_second, table_flat, qkv_full, out_full, in_full, back_full = gathered
    seq_count, block_len, model_width = tokens.shape
    seq_len = block_len * lax.axis_size("seq")
    row_count = seq_count * block_len
    group_size = seq_count
    while group_size % 2 == 0 and group_size // 2 * block_len >= 512:
        group_size = group_size // 2
    group_count = seq_count // group_size
    flat_x = tokens.reshape(row_count, model_width).astype(jnp.float32)
    first_scale = rms_scale(flat_x)
    first_gain = gain_first.astype(jnp.float32)
    first_normed = (flat_x * first_scale * first_gain).astype(jnp.bfloat16)
    projected = jnp.dot(first_normed, qkv_full, preferred_element_type=jnp.float32).astype(
        jnp.bfloat16
    )
    queries = projected[:, :model_width].reshape(group_count, group_size, block_len, HEADS, HD)
    local_keys = projected[:, model_width : 2 * model_width].reshape(
        seq_count, block_len, model_width
    )
    local_values = projected[:, 2 * model_width :].reshape(seq_count, block_len, model_width)
    all_keys, all_values, all_segments = (
        lax.all_gather(local_keys, "seq", axis=1, tiled=True),
        lax.all_gather(local_values, "seq", axis=1, tiled=True),
        lax.all_gather(segment_ids, "seq", axis=1, tiled=True),
    )
    key_groups = all_keys.reshape(group_count, group_size, seq_len, HEADS, HD)
    value_groups = all_values.reshape(group_count, group_size, seq_len, HEADS, HD)
    segkey_groups = all_segments.reshape(group_count, group_size, seq_len)
    segquery_groups = segment_ids.reshape(group_count, group_size, block_len)
    offset = lax.axis_index("seq") * block_len
    query_places = offset + jnp.arange(block_len, dtype=jnp.int32)
    key_places = jnp.arange(seq_len, dtype=jnp.int32)
    buckets = bucket_of(key_places[None, :] - query_places[:, None])
    single_hot_vector = (
        buckets[None] == jnp.arange(BUCKETS, dtype=jnp.int32)[:, None, None]
    ).astype(jnp.bfloat16)
    bias_matrix = table_flat.reshape(BUCKETS, HEADS)
    complete_bias = jnp.einsum(
        "dto,dl->lto", single_hot_vector, bias_matrix, preferred_element_type=jnp.float32
    )

    def attend(group_items):
        query_part, key_part, value_part, seg_query, seg_key = group_items
        scores = group_scores(query_part, key_part, seg_query, seg_key, complete_bias)
        row_peak = jnp.max(scores, axis=-1, keepdims=True)
        shifted = jnp.exp(scores - row_peak)
        row_total = jnp.sum(shifted, axis=-1, keepdims=True)
        softmax_probabilities = (shifted / row_total).astype(jnp.bfloat16)
        attn_part = jnp.einsum(
            "ghqk,gkhd->gqhd", softmax_probabilities, value_part, preferred_element_type=jnp.float32
        )
        return (attn_part.astype(jnp.bfloat16), row_peak + jnp.log(row_total))

    attn_mixed, log_totals = lax.map(
        attend, (queries, key_groups, value_groups, segquery_groups, segkey_groups)
    )
    mixed_flat = attn_mixed.reshape(row_count, model_width)
    middle = flat_x + jnp.dot(mixed_flat, out_full, preferred_element_type=jnp.float32)
    second_scale = rms_scale(middle)
    second_gain = gain_second.astype(jnp.float32)
    second_normed = (middle * second_scale * second_gain).astype(jnp.bfloat16)
    hidden_pre = jnp.dot(second_normed, in_full, preferred_element_type=jnp.float32)
    hidden_float, gate_pullback = jax.vjp(smooth_gate, hidden_pre)
    hidden = hidden_float.astype(jnp.bfloat16)
    result = middle + jnp.dot(hidden, back_full, preferred_element_type=jnp.float32)
    output = result.astype(jnp.bfloat16).reshape(seq_count, block_len, model_width)
    grad_result = cotangent.reshape(row_count, model_width).astype(
        jnp.float32
    ) * valid_mask.reshape(row_count, 1).astype(jnp.float32)
    grad_branch = grad_result.astype(jnp.bfloat16)
    grad_back = jnp.einsum("tf,td->fd", hidden, grad_branch, preferred_element_type=jnp.float32)
    grad_hidden = jnp.einsum(
        "td,fd->tf", grad_branch, back_full, preferred_element_type=jnp.float32
    )
    grad_pre = gate_pullback(grad_hidden)[0].astype(jnp.bfloat16)
    grad_in = jnp.einsum("td,tf->df", second_normed, grad_pre, preferred_element_type=jnp.float32)
    grad_second_normed = jnp.einsum(
        "tf,df->td", grad_pre, in_full, preferred_element_type=jnp.float32
    )
    grad_middle_norm, grad_gain_second = norm_backward(
        middle, second_scale, second_gain, grad_second_normed
    )
    grad_middle = grad_result + grad_middle_norm
    grad_attn = grad_middle.astype(jnp.bfloat16)
    grad_out = jnp.einsum("td,te->de", mixed_flat, grad_attn, preferred_element_type=jnp.float32)
    grad_mixed = jnp.einsum(
        "te,de->td", grad_attn, out_full, preferred_element_type=jnp.float32
    ).astype(jnp.bfloat16)
    grad_mixed_groups = grad_mixed.reshape(group_count, group_size, block_len, HEADS, HD)
    backward_entries = (
        queries,
        key_groups,
        value_groups,
        segquery_groups,
        segkey_groups,
        log_totals,
        grad_mixed_groups,
    )
    bias_zero = jnp.zeros((HEADS, block_len, seq_len), jnp.float32)

    def full_backward(bias_total_sum, group_items):
        softmax_probabilities, grad_scores, grad_query, row_inner = query_backward(
            group_items, complete_bias
        )
        query_part = group_items[0]
        grad_part = group_items[6]
        key_gradient = jnp.einsum(
            "ghqk,gqhd->gkhd", grad_scores, query_part, preferred_element_type=jnp.float32
        )
        grad_value = jnp.einsum(
            "ghqk,gqhd->gkhd",
            softmax_probabilities.astype(jnp.bfloat16),
            grad_part,
            preferred_element_type=jnp.float32,
        )
        bias_total_sum = bias_total_sum + jnp.sum(grad_scores.astype(jnp.float32), axis=0)
        return (bias_total_sum, (grad_query, key_gradient, grad_value))

    bias_total_sum, (grad_queries, grad_keys, grad_values) = lax.scan(
        full_backward, bias_zero, backward_entries
    )
    key_terms = grad_keys.reshape(seq_count, seq_len, model_width)
    value_terms = grad_values.reshape(seq_count, seq_len, model_width)
    key_sum, value_sum = (
        lax.psum_scatter(
            key_terms.astype(jnp.bfloat16), "seq", scatter_dimension=1, tiled=True
        ).astype(jnp.float32),
        lax.psum_scatter(
            value_terms.astype(jnp.bfloat16), "seq", scatter_dimension=1, tiled=True
        ).astype(jnp.float32),
    )
    key_low = key_sum.astype(jnp.bfloat16)
    value_low = value_sum.astype(jnp.bfloat16)
    grad_projected = jnp.concatenate(
        [
            grad_queries.reshape(row_count, model_width),
            key_low.reshape(row_count, model_width),
            value_low.reshape(row_count, model_width),
        ],
        axis=1,
    )
    grad_qkv = jnp.einsum(
        "td,te->de", first_normed, grad_projected, preferred_element_type=jnp.float32
    )
    grad_first_normed = jnp.einsum(
        "te,de->td", grad_projected, qkv_full, preferred_element_type=jnp.float32
    )
    grad_x_norm, grad_gain_first = norm_backward(flat_x, first_scale, first_gain, grad_first_normed)
    grad_tokens = (
        (grad_middle + grad_x_norm).astype(jnp.bfloat16).reshape(seq_count, block_len, model_width)
    )
    grad_table = jnp.einsum(
        "fuy,suy->fs",
        single_hot_vector.astype(jnp.float32),
        bias_total_sum,
        precision=lax.Precision.HIGHEST,
    ).reshape(BUCKETS * HEADS)
    owned = (
        lax.psum_scatter(grad_gain_first, ("dp", "seq"), scatter_dimension=0, tiled=True),
        lax.psum_scatter(grad_gain_second, ("dp", "seq"), scatter_dimension=0, tiled=True),
        lax.psum_scatter(grad_table, ("dp", "seq"), scatter_dimension=0, tiled=True),
        lax.psum_scatter(grad_qkv, ("dp", "seq"), scatter_dimension=0, tiled=True),
        lax.psum_scatter(grad_out, ("dp", "seq"), scatter_dimension=0, tiled=True),
        lax.psum_scatter(grad_in, ("dp", "seq"), scatter_dimension=0, tiled=True),
        lax.psum_scatter(grad_back, ("dp", "seq"), scatter_dimension=0, tiled=True),
    )
    owned_gain_one, owned_gain_two, owned_table, owned_qkv, owned_out, owned_in, owned_back = owned
    return (
        output,
        grad_tokens,
        owned_gain_one,
        owned_gain_two,
        owned_table,
        owned_qkv,
        owned_out,
        owned_in,
        owned_back,
    )


MESH = pl.DeviceIdType.MESH

def flip(i, bit):
    return i + bit - 2 * bit * ((i // bit) % 2)

def forward_kernel(items, *refs):
    tok, cot, seg = refs[:3]
    shards = refs[3:8]
    xf, gf, out_full, in_full, back_full, w_ref, qkv_ref, o_ref, qa_ref, exk_ref, gains_ref, biasb_ref = refs[8:20]
    wv, sv, sf, exq_ref, fl_ref, fr_ref, bias_ref = refs[20:27]
    full = (wv, out_full, in_full, back_full, sv)
    loc_sem, t_send, t_recv, s_send, s_recv, g_send, g_recv, z_send, z_recv, h_send, h_recv = refs[27:]
    dp, z = lax.axis_index("dp"), lax.axis_index("seq")
    n_z = 4
    peers = [(dp, lax.rem(z + s, n_z)) for s in range(1, n_z)] + [(flip(dp, b), z) for b in (1, 2, 4)]
    barrier = pltpu.get_barrier_semaphore()
    for p in peers:
        pl.semaphore_signal(barrier, inc=1, device_id=p, device_id_type=MESH)
    pl.semaphore_wait(barrier, len(peers))

    def block(it, d, zz):
        return full[items[it][0]].at[d * n_z + zz]

    def own(it):
        return shards[items[it][0]]

    n_it = len(items)
    def z_copy(it, way, step):
        src_z = z - step if way == 0 else z + step
        src = own(it) if step == 0 else block(it, dp, src_z)
        return pltpu.make_async_remote_copy(
            src_ref=src, dst_ref=block(it, dp, src_z), send_sem=z_send.at[it, way, step],
            recv_sem=z_recv.at[it, way, step], device_id=(dp, z + 1 if way == 0 else z - 1), device_id_type=MESH)

    def z_wait(it, way, step):
        src_z = z - 1 - step if way == 0 else z + 1 + step
        blk = block(it, dp, src_z)
        pltpu.make_async_remote_copy(src_ref=blk, dst_ref=blk, send_sem=z_send.at[it, way, step],
            recv_sem=z_recv.at[it, way, step], device_id=(dp, z), device_id_type=MESH).wait_recv()

    def can_send(way, step):
        return (z >= step) & (z <= n_z - 2) if way == 0 else (z + step <= n_z - 1) & (z >= 1)

    def can_recv(way, step):
        return z >= step + 1 if way == 0 else z + 1 + step <= n_z - 1

    def z_start(it, step):
        for way in (0, 1):
            @pl.when(can_send(way, step))
            def _():
                z_copy(it, way, step).start()

    def z_recv_all(it, step):
        for way in (0, 1):
            @pl.when(can_recv(way, step))
            def _():
                z_wait(it, way, step)

    def hops(it):
        b1, b2 = items[it][1:]
        return [(0, b1), (0, b2), (b1, b2), (0, 1), (b1, 1), (b2, 1), (b1 + b2, 1)]

    def flips(d, mask):
        for b in (1, 2, 4):
            if mask & b:
                d = flip(d, b)
        return d

    def hop(it, slot, zz):
        mask, to = hops(it)[slot]
        blk = block(it, flips(dp, mask), zz)
        return pltpu.make_async_remote_copy(src_ref=blk, dst_ref=blk, send_sem=h_send.at[it, slot, zz],
            recv_sem=h_recv.at[it, slot, zz], device_id=(flip(dp, to), z), device_id_type=MESH)

    def hop_wait(it, slot, zz):
        mask, to = hops(it)[slot]
        blk = block(it, flips(dp, mask ^ to), zz)
        pltpu.make_async_remote_copy(src_ref=blk, dst_ref=blk, send_sem=h_send.at[it, slot, zz],
            recv_sem=h_recv.at[it, slot, zz], device_id=(dp, z), device_id_type=MESH).wait_recv()

    def own_hop(it, slot):
        to = hops(it)[slot][1]
        return pltpu.make_async_remote_copy(src_ref=own(it), dst_ref=block(it, dp, z), send_sem=h_send.at[it, slot, z],
            recv_sem=h_recv.at[it, slot, z], device_id=(flip(dp, to), z), device_id_type=MESH)

    def tok_copy(s, first, last):
        to = lax.rem(z + s, n_z)
        return [pltpu.make_async_remote_copy(src_ref=a.at[to], dst_ref=f.at[z], send_sem=ss.at[s - 1], recv_sem=rs.at[s - 1],
                device_id=(dp, to), device_id_type=MESH) for a, f, ss, rs in ((tok, xf, t_send, t_recv), (seg, sf, s_send, s_recv), (cot, gf, g_send, g_recv))[first:last]]

    def tok_wait(s, first, last):
        frm = lax.rem(z + n_z - s, n_z)
        for f, ss, rs in ((xf, t_send, t_recv), (sf, s_send, s_recv), (gf, g_send, g_recv))[first:last]:
            pltpu.make_async_remote_copy(src_ref=f.at[frm], dst_ref=f.at[frm], send_sem=ss.at[s - 1], recv_sem=rs.at[s - 1],
                device_id=(dp, z), device_id_type=MESH).wait_recv()

    for it in range(n_it):
        z_start(it, 0)
        for slot in (0, 1, 3):
            own_hop(it, slot).start()
    locs = []
    for it in range(n_it):
        locs.append(pltpu.make_async_copy(own(it), block(it, dp, z), loc_sem.at[it]))
    locs.append(pltpu.make_async_copy(tok.at[z], xf.at[z], loc_sem.at[n_it]))
    locs.append(pltpu.make_async_copy(seg.at[z], sf.at[z], loc_sem.at[n_it + 1]))
    locs.append(pltpu.make_async_copy(cot.at[z], gf.at[z], loc_sem.at[n_it + 2]))
    for c in locs:
        c.start()

    def forward(it, zz):
        hop_wait(it, 0, zz)
        hop(it, 2, zz).start()
        hop(it, 4, zz).start()
        hop_wait(it, 1, zz)
        hop(it, 5, zz).start()

    def arrivals(step):
        return [(can_recv(0, step), 0, z - 1 - step), (can_recv(1, step), 1, z + 1 + step)]

    def chain(it, step):
        for ok, way, zz in arrivals(step):
            @pl.when(ok)
            def _():
                z_wait(it, way, step)
                if step < n_z - 2:
                    @pl.when(can_send(way, step + 1))
                    def _():
                        z_copy(it, way, step + 1).start()
                for slot in (0, 1, 3):
                    hop(it, slot, zz).start()

    def pass_on(it, step):
        if step < 0:
            forward(it, z)
        else:
            for ok, way, zz in arrivals(step):
                @pl.when(ok)
                def _():
                    forward(it, zz)

    first, rest = (0, 1), tuple(range(2, n_it))
    for step in range(n_z - 1):
        for it in first:
            chain(it, step)
    for it in rest:
        chain(it, 0)
    for it in rest:
        chain(it, 1)
    for s in range(1, n_z):
        for c in tok_copy(s, 0, 2):
            c.start()
    for step in range(-1, n_z - 1):
        for it in first:
            pass_on(it, step)
    for it in rest:
        chain(it, 2)
    for it in rest:
        pass_on(it, -1)
    def last_hop(it):
        for zz in range(n_z):
            hop_wait(it, 2, zz)
            hop(it, 6, zz).start()

    def arrived(it):
        for zz in range(n_z):
            for slot in (3, 4, 5, 6):
                hop_wait(it, slot, zz)

    for it in first:
        last_hop(it)
    for it in rest:
        pass_on(it, 0)
    for it in first:
        arrived(it)
    for c in locs:
        c.wait()

    width = xf.shape[2]
    block_len = xf.shape[1]
    rows = n_z * block_len
    nblk = rows // 128
    n_dev = sv.shape[0]
    own_len = width // n_dev
    heads = qa_ref.shape[0]

    @pl.loop(0, n_dev // 2)
    def _(i):
        pair = [wv[2 * i].astype(F32), wv[2 * i + 1].astype(F32)]
        w_ref[pl.ds(pl.multiple_of(i * 48, 48), 48)] = jnp.concatenate(pair, axis=0).astype(BF)

    flat = sv[...].reshape(n_dev * 8, 128)
    pick = lax.broadcasted_iota(jnp.int32, (n_dev, n_dev * 8), 1) == 8 * lax.broadcasted_iota(jnp.int32, (n_dev, n_dev * 8), 0)
    small = exact(pick.astype(F32), flat, ((1,), (0,)))
    place = lax.broadcasted_iota(jnp.int32, (n_dev, width), 1)
    mine = place // own_len == lax.broadcasted_iota(jnp.int32, (n_dev, width), 0)
    from_lane = lax.broadcasted_iota(jnp.int32, (128, width), 0)
    to_lane = lax.broadcasted_iota(jnp.int32, (128, width), 1) % own_len
    for i in range(2):
        spread = exact(small, (from_lane == to_lane + i * own_len).astype(F32), ((1,), (0,)))
        gains_ref[i:i + 1] = jnp.sum(jnp.where(mine, spread, 0.0), axis=0, keepdims=True)
    bucket = lax.broadcasted_iota(jnp.int32, (n_dev, 512), 0)
    m = lax.broadcasted_iota(jnp.int32, (n_dev, 512), 1)
    bias_ref[...] = exact(small, (bucket_of((m + 127) % 512 - 255) == bucket).astype(F32), ((0,), (0,)))
    biasb_ref[...] = exact(small, (bucket_of(128 - m + jnp.where(m >= 384, 512, 0)) == bucket).astype(F32), ((0,), (0,)))

    for s in range(1, n_z):
        tok_wait(s, 0, 2)
    for s in range(1, n_z):
        for c in tok_copy(s, 2, 3):
            c.start()
    nb = rows.bit_length()
    lane = lax.broadcasted_iota(jnp.int32, (block_len, 128), 1) % 64
    rel = lane - (nblk + 3)
    inside = (rel >= 0) & (rel < 2 * nb)
    bit_of = lax.broadcasted_iota(jnp.int32, (16, 128), 0)
    rel16 = lax.broadcasted_iota(jnp.int32, (16, 128), 1) % 64 - (nblk + 3)
    to_bits = jnp.where(rel16 == 2 * bit_of, 1.0, jnp.where(rel16 == 2 * bit_of + 1, -1.0, 0.0)).astype(BF)
    for r in range(n_z):
        at = pl.ds(r * block_len, block_len)
        ids = jnp.broadcast_to(sf[r], (16, block_len))
        bits = (jnp.right_shift(ids, lax.broadcasted_iota(jnp.int32, ids.shape, 0)) & 1).astype(F32).astype(BF)
        u = mm(bits, to_bits, ((0,), (0,))) + jnp.where(inside & (rel % 2 == 1), 1.0, 0.0)
        exq_ref[at] = u.astype(BF)
        row_blk = r * (block_len // 128) + lax.broadcasted_iota(jnp.int32, (block_len, 128), 0) // 128
        unit = ((lane < nblk) & (lane == row_blk)) | ((lane >= nblk) & (lane < nblk + 3))
        exk_ref[at] = jnp.where(inside, jnp.where(u == 0.0, BIG, 0.0), jnp.where(unit, 1.0, 0.0)).astype(BF)
        fl_ref[at] = jnp.where((lane < nblk) & (lane <= row_blk - 2), 1.0, 0.0).astype(BF)
        fr_ref[at] = jnp.where((lane < nblk) & (lane >= row_blk + 2), 1.0, 0.0).astype(BF)
        x = xf[r].astype(F32)
        scale = lax.rsqrt(jnp.mean(x * x, axis=-1, keepdims=True) + EPS)
        normed = (x * scale * gains_ref[0:1]).astype(BF)
        qkv_ref[at] = mm(normed, w_ref[...]).astype(BF)
        if r == 2:
            for it in rest:
                pass_on(it, 1)

    plan = {0: [(pass_on, 2, 2), (pass_on, 3, 2), (pass_on, 4, 2)], 2: [(last_hop, 2), (last_hop, 3)], 3: [(last_hop, 4)]}

    @pl.loop(0, heads // 2)
    def _(hp):
        cols = [pl.ds(pl.multiple_of(i * width + hp * 128, 128), 128) for i in range(3)]
        lane = lax.broadcasted_iota(jnp.int32, (rows, 128), 1)
        lane1 = lax.broadcasted_iota(jnp.int32, (1, 128), 1)
        QB = 256
        outs = []
        for h in range(2):
            head = hp * 2 + h
            sel = (lane < 64) if h == 0 else (lane >= 64)
            strip = skewed(bias_ref[pl.ds(2 * own_len + head, 1)])
            side = [jnp.sum(jnp.where(lane1 == 2 * own_len + head, sv[d, 0:1], 0.0), axis=1, keepdims=True).astype(BF)
                    for d in (n_dev // 2 - 1, n_dev - 1)]
            qa = jnp.where(sel, qkv_ref[:, cols[0]], exq_ref[...] + fl_ref[...] * side[0] + fr_ref[...] * side[1])
            ka = jnp.where(sel, qkv_ref[:, cols[1]], exk_ref[...])
            va = jnp.where(sel, qkv_ref[:, cols[2]], jnp.ones((rows, 128), BF))
            lane_l = 64 * (1 - h)
            for blk in range(rows // QB):
                r0 = blk * QB
                qb = qa[r0:r0 + QB]
                s = mm(qb, ka, ((1,), (1,)))
                srows = []
                for sub in range(QB // 128):
                    I = blk * (QB // 128) + sub
                    lo = max(I - 1, 0)
                    hi = min(I + 1, nblk - 1)
                    srow = s[sub * 128:(sub + 1) * 128]
                    parts = []
                    if lo > 0:
                        parts.append(srow[:, :lo * 128])
                    parts.append(srow[:, lo * 128:(hi + 1) * 128] + strip[:, (lo - I + 1) * 128:(hi - I + 2) * 128])
                    if hi < nblk - 1:
                        parts.append(srow[:, (hi + 1) * 128:])
                    srows.append(jnp.concatenate(parts, axis=1))
                s = jnp.concatenate(srows, axis=0)
                top = jnp.max(s, axis=1, keepdims=True)
                p = jnp.exp2((s - top) * LOG2E).astype(BF)
                o = mm(p, va)
                l = o[:, lane_l:lane_l + 1]
                outs.append(o / l)
                lse = -top - jnp.log(l)
                hi_ = lse.astype(BF)
                rest = lse - hi_.astype(F32)
                mid = rest.astype(BF)
                low = (rest - mid.astype(F32)).astype(BF)
                base = 64 * (1 - h) + nblk
                ln = lane[:QB]
                qa_ref[head, r0:r0 + QB] = jnp.where(ln == base, hi_, jnp.where(ln == base + 1, mid, jnp.where(ln == base + 2, low, qb)))
        n = rows // QB
        for blk in range(n):
            o_ref[blk * QB:(blk + 1) * QB, cols[0]] = jnp.where(lane[:QB] < 64, outs[blk], outs[n + blk]).astype(BF)
        for k, calls in plan.items():
            @pl.when(hp == k)
            def _():
                for fn, *which in calls:
                    fn(*which)

    for it in range(2, n_it):
        arrived(it)
    for s in range(1, n_z):
        tok_wait(s, 2, 3)
    for it in range(n_it):
        for step in range(n_z - 1):
            for way in (0, 1):
                @pl.when(can_send(way, step))
                def _():
                    z_copy(it, way, step).wait_send()
        for zz in range(n_z):
            for slot in range(7):
                hop(it, slot, zz).wait_send()
    for s in range(1, n_z):
        for c in tok_copy(s, 0, 3):
            c.wait_send()

def forward(tokens, cot, seg, shards, items, collective_id=0):
    n_it = len(items)
    n_dev = 32
    n_z, block_len, width = tokens.shape
    rows = n_z * block_len
    heads = width // HD
    D = pltpu.SemaphoreType.DMA
    S = jax.ShapeDtypeStruct
    vm = pl.BlockSpec(memory_space=pltpu.VMEM)
    hbm = pl.BlockSpec(memory_space=pltpu.HBM)
    qkv, out, in_, back, small = shards
    return pl.pallas_call(
        functools.partial(forward_kernel, items),
        out_shape=[S(tokens.shape, BF), S(tokens.shape, BF)] + [S((n_dev, *a.shape), BF) for a in (out, in_, back)]
        + [S((width, 3 * width), BF), S((rows, 3 * width), BF), S((rows, width), BF), S((heads, rows, 128), BF), S((rows, 128), BF),
           S((8, width), F32), S((128, 512), F32)],
        in_specs=[vm] * (3 + len(shards)),
        out_specs=[vm, hbm, hbm, hbm, hbm] + [vm] * 7,
        scratch_shapes=[pltpu.VMEM((n_dev, *qkv.shape), BF), pltpu.VMEM((n_dev, *small.shape), F32), pltpu.VMEM(seg.shape, seg.dtype),
                        pltpu.VMEM((rows, 128), BF), pltpu.VMEM((rows, 128), BF), pltpu.VMEM((rows, 128), BF), pltpu.VMEM((128, 512), F32),
                        D((n_it + 3,)), D((3,)), D((3,)), D((3,)), D((3,)), D((3,)), D((3,)), D((n_it, 2, 3)), D((n_it, 2, 3)),
                        D((n_it, 7, 4)), D((n_it, 7, 4))],
        compiler_params=pltpu.CompilerParams(collective_id=collective_id, has_side_effects=True, vmem_limit_bytes=60 << 20),
    )(tokens, cot, seg, *shards)


LOG2E = 1.4426950408889634
BIG = -1e30
F32 = jnp.float32
BF = jnp.bfloat16

def skewed(row):
    return pltpu.roll(jnp.broadcast_to(row, (128, 512)), 0, 1, stride=1, stride_axis=0)[:, :384]


def diagonal_sums(near):
    rows = 64
    x = jnp.concatenate([near, jnp.zeros((128, 128), F32)], axis=1)
    while rows >= 1:
        x = x[:rows] + pltpu.roll(x[rows:], 512 - rows, 1)
        rows //= 2
    return x


GELU_A = 0.7978845608028654
GELU_B = 0.044715


def mm(a, b, dims=((1,), (0,))):
    return lax.dot_general(a, b, (dims, ((), ())), preferred_element_type=F32)


def ffn_kernel(x_ref, mixed_ref, g_ref, gain_ref, wo_ref, wi_ref, wb_ref,
               out_ref, gm_ref, gmix_ref, dwo_ref, dwi_ref, dwb_ref, dgain_ref,
               mid_ref, h_ref, ht_ref, acc_ref, dh_ref):
    step = pl.program_id(0)
    rows = x_ref.shape[0]
    half = 256

    @pl.when(step == 0)
    def _():
        for r in range(0, rows, half):
            part = pl.ds(r, half)
            middle = x_ref[part].astype(F32) + mm(mixed_ref[part], wo_ref[...])
            mid_ref[part] = middle
            acc_ref[part] = middle
            scale = lax.rsqrt(jnp.mean(middle * middle, axis=-1, keepdims=True) + EPS)
            normed = (middle * scale * gain_ref[1:2]).astype(BF)
            h_ref[part] = normed
            ht_ref[:, part] = normed.T
            dh_ref[part] = jnp.zeros((half, x_ref.shape[1]), F32)

    gates = []
    hiddens = []
    for r in range(0, rows, half):
        part = pl.ds(r, half)
        pre = mm(h_ref[part], wi_ref[...])
        dhid = mm(g_ref[part], wb_ref[...], ((1,), (1,)))
        sq = pre * pre
        t = jnp.tanh(pre * (GELU_A + GELU_A * GELU_B * sq))
        half_t = 0.5 + 0.5 * t
        hidden = (pre * half_t).astype(BF)
        slope = half_t + pre * (0.5 - 0.5 * t * t) * (GELU_A + 3.0 * GELU_A * GELU_B * sq)
        dpre = (dhid * slope).astype(BF)
        acc_ref[part] += mm(hidden, wb_ref[...])
        dh_ref[part] += mm(dpre, wi_ref[...], ((1,), (1,)))
        hiddens.append(hidden)
        gates.append(dpre)
    dwi_ref[...] = mm(ht_ref[...], jnp.concatenate(gates, axis=0)).astype(BF)
    dwb_ref[...] = mm(jnp.concatenate(hiddens, axis=0), g_ref[...], ((0,), (0,))).astype(BF)

    @pl.when(step == pl.num_programs(0) - 1)
    def _():
        dgain = jnp.zeros((1, x_ref.shape[1]), F32)
        for r in range(0, rows, half):
            part = pl.ds(r, half)
            out_ref[part] = acc_ref[part].astype(BF)
            middle = mid_ref[part]
            dh = dh_ref[part]
            scale = lax.rsqrt(jnp.mean(middle * middle, axis=-1, keepdims=True) + EPS)
            dgain += jnp.sum(dh * (middle * scale), axis=0, keepdims=True)
            u = dh * gain_ref[1:2]
            inner = jnp.mean(u * middle, axis=-1, keepdims=True)
            gm = g_ref[part].astype(F32) + scale * u - middle * (scale * scale * scale * inner)
            gm_ref[part] = gm
            low = gm.astype(BF)
            h_ref[part] = low
            gmix_ref[part] = mm(low, wo_ref[...], ((1,), (1,))).astype(BF)
        dgain_ref[...] = dgain
        dwo_ref[...] = mm(mixed_ref[...], h_ref[...], ((0,), (0,))).astype(BF)


def ffn(x, mixed, g, gain, wo, wi, wb, chunk=512):
    rows, width = x.shape
    ff = wi.shape[1]
    whole = lambda s: pl.BlockSpec(s, lambda i: (0, 0), pipeline_mode=pl.Buffered(1))
    S = jax.ShapeDtypeStruct
    return pl.pallas_call(
        ffn_kernel,
        grid=(ff // chunk,),
        in_specs=[whole((rows, width))] * 3 + [whole((8, width)), whole((width, width)),
                  pl.BlockSpec((width, chunk), lambda i: (0, i)), pl.BlockSpec((chunk, width), lambda i: (i, 0))],
        out_specs=[whole((rows, width))] * 3 + [whole((width, width)), pl.BlockSpec((width, chunk), lambda i: (0, i)),
                   pl.BlockSpec((chunk, width), lambda i: (i, 0)), whole((1, width))],
        out_shape=[S((rows, width), BF), S((rows, width), F32), S((rows, width), BF), S((width, width), BF),
                   S((width, ff), BF), S((ff, width), BF), S((1, width), F32)],
        scratch_shapes=[pltpu.VMEM((rows, width), F32), pltpu.VMEM((rows, width), BF), pltpu.VMEM((width, rows), BF),
                        pltpu.VMEM((rows, width), F32), pltpu.VMEM((rows, width), F32)],
        compiler_params=pltpu.CompilerParams(vmem_limit_bytes=56 << 20),
        cost_estimate=pl.CostEstimate(flops=12 * rows * width * ff + 6 * rows * width * width, bytes_accessed=50 << 20, transcendentals=rows * ff),
    )(x, mixed, g, gain, wo, wi, wb)


def back_kernel(chunks, n_early, *refs):
    n_it, n_arr, n_z = len(chunks), 5, 4
    (qa_ref, qkv_ref, do_ref, o_ref, exk_ref, bias_ref, x_ref, gm_ref, gain_ref, gain2_ref, w_ref, y_ref) = refs[:12]
    p_out, p_in, p_back = refs[12:15]
    gx_out, y_out = refs[15:17]
    outs = refs[17:17 + n_arr]
    scr = refs[17 + n_arr:]
    k_ref, v_ref, p_qkv, p_small, gx, ht_ref, dqt_ref, dq_ref, dk_ref, dv_ref, diag_ref = scr[:11]
    scr = scr[11:]
    part = (p_qkv, p_small, p_out, p_in, p_back)
    rc, r2, r1, zo, zu, zd = (scr[k * n_it:(k + 1) * n_it] for k in range(6))
    stg = scr[6 * n_it:6 * n_it + n_early]
    (loc_sem, own_sem, t_send, t_recv, y_send, y_recv, c_send, c_recv, x2_send, x2_recv, x1_send, x1_recv,
     z_send, z_recv) = scr[6 * n_it + n_early:]
    dp, z = lax.axis_index("dp"), lax.axis_index("seq")
    core = lax.rem(dp, 2)
    quad = dp // 2
    peers = [(dp, lax.rem(z + s, n_z)) for s in range(1, n_z)] + [(flip(dp, b), z) for b in (1, 2, 4)]
    barrier = pltpu.get_barrier_semaphore()
    for p in peers:
        pl.semaphore_signal(barrier, inc=1, device_id=p, device_id_type=MESH)
    pl.semaphore_wait(barrier, len(peers))

    def remote(src, dst, ss, rs, to):
        return pltpu.make_async_remote_copy(src_ref=src, dst_ref=dst, send_sem=ss, recv_sem=rs, device_id=to, device_id_type=MESH)

    def piece(it, d):
        a, c0, w = chunks[it][:3]
        return part[a].at[d, :, pl.ds(c0, w)]

    def own_copy(it, q):
        return pltpu.make_async_copy(piece(it, 2 * q + core), stg[it].at[q], own_sem.at[it, q])

    def add_into(dst, src, chunk=16):
        rows = dst.shape[0]
        chunk = min(chunk, rows)
        @pl.loop(0, rows // chunk)
        def _(i):
            at = pl.ds(pl.multiple_of(i * chunk, chunk), chunk)
            dst[at] = dst[at] + src[at]

    def q_at(it, f1, f2):
        b1, b2 = chunks[it][3:]
        q = quad
        if f1: q = flip(q, b1 // 2)
        if f2: q = flip(q, b2 // 2)
        return q

    def c_copy(it, q):
        return remote(piece(it, 2 * q + 1 - core), rc[it].at[q], c_send.at[it, q], c_recv.at[it, q], (flip(dp, 1), z))

    def x2_copy(it, f1):
        q = q_at(it, f1, True)
        k = (q // (chunks[it][3] // 2)) % 2
        return remote(rc[it].at[q], r2[it].at[k], x2_send.at[it, k], x2_recv.at[it, k], (flip(dp, chunks[it][4]), z))

    def x1_copy(it):
        return remote(rc[it].at[q_at(it, True, False)], r1[it], x1_send.at[it], x1_recv.at[it], (flip(dp, chunks[it][3]), z))

    def rows_copy(src, dst, ss, rs, s):
        to = lax.rem(z + s, n_z)
        return remote(src.at[to], dst.at[z], ss.at[s - 1], rs.at[s - 1], (dp, to))

    def rows_wait(dst, ss, rs, s):
        frm = lax.rem(z + n_z - s, n_z)
        remote(dst.at[frm], dst.at[frm], ss.at[s - 1], rs.at[s - 1], (dp, z)).wait_recv()

    def core_start(it):
        for f1, f2 in ((True, True), (False, True), (True, False), (False, False)):
            c_copy(it, q_at(it, f1, f2)).start()

    def core_sum(it, f1, f2):
        q = q_at(it, f1, f2)
        c_copy(it, q).wait_recv()
        if it < n_early:
            own_copy(it, q).wait()
            add_into(rc[it].at[q], stg[it].at[q])
        else:
            add_into(rc[it].at[q], piece(it, 2 * q + core))

    def stage_core(it):
        for f1 in (True, False):
            core_sum(it, f1, True)
            x2_copy(it, f1).start()
        for f1 in (True, False):
            core_sum(it, f1, False)

    def stage_x2(it):
        for f1 in (True, False):
            q = q_at(it, f1, False)
            k = (q // (chunks[it][3] // 2)) % 2
            remote(rc[it].at[0], r2[it].at[k], x2_send.at[it, k], x2_recv.at[it, k], (dp, z)).wait_recv()
            add_into(rc[it].at[q], r2[it].at[k])
            if f1:
                x1_copy(it).start()

    def z_copy(it, way, j):
        src = zo[it].at[j]
        dst = (zu if way == 0 else zd)[it].at[j]
        return remote(src, dst, z_send.at[it, way, j], z_recv.at[it, way, j], (dp, z + 1 if way == 0 else z - 1))

    def z_add(it, way, j):
        buf = (zu if way == 0 else zd)[it]
        remote(buf.at[j], buf.at[j], z_send.at[it, way, j], z_recv.at[it, way, j], (dp, z)).wait_recv()
        zo[it][j] = (zo[it][j].astype(F32) + buf[j].astype(F32)).astype(zo[it].dtype)

    def stage_x1(it):
        x1_copy(it).wait_recv()
        rows = zo[it].shape[1]
        for j in range(n_z):
            at = pl.ds(j * rows, rows)
            zo[it][j] = (rc[it][quad, at].astype(F32) + r1[it][at].astype(F32)).astype(zo[it].dtype)
        stage_z(it, 0)

    def stage_z(it, s):
        for way, here in ((0, s), (1, n_z - 1 - s)):
            @pl.when(z == here)
            def _():
                for j in (range(n_z - 1, here, -1) if way == 0 else range(here)):
                    if s > 0:
                        z_add(it, way, j)
                    z_copy(it, way, j).start()

    def stage_end(it):
        a, c0, w = chunks[it][:3]
        col = pl.ds(c0, w)
        outs[a][:, col] = zo[it][z].astype(F32)
        for way, ok in ((0, z > 0), (1, z < n_z - 1)):
            @pl.when(ok)
            def _():
                buf = (zu if way == 0 else zd)[it].at[z]
                remote(buf, buf, z_send.at[it, way, z], z_recv.at[it, way, z], (dp, z)).wait_recv()
                outs[a][:, col] += buf[...].astype(F32)

    stage_z1, stage_z2 = functools.partial(stage_z, s=1), functools.partial(stage_z, s=2)
    width = x_ref.shape[2]
    rows = n_z * x_ref.shape[1]
    nblk = rows // 128
    heads = qa_ref.shape[0]
    plan = {
        -1: [(stage_core, 0), (stage_core, 1)],
        3: [(stage_x2, 0), (stage_x2, 1), (stage_core, 4), (stage_core, 5)],
        5: [(stage_core, 2), (stage_core, 3)],
        6: [(stage_x1, 0), (stage_x1, 1), (stage_x2, 4), (stage_x2, 5)],
        7: [(stage_z1, 0), (stage_z1, 1)],
        8: [(stage_z2, 0), (stage_z2, 1)],
        11: [(stage_x2, 2), (stage_x2, 3)],
    }
    for it in range(n_early):
        core_start(it)
        for q in range(4):
            own_copy(it, q).start()
    kv = [pltpu.make_async_copy(qkv_ref.at[:, pl.ds((i + 1) * width, width)], ref, loc_sem.at[2 + i]) for i, ref in enumerate((k_ref, v_ref))]
    for c in kv:
        c.start()
    y_loc = pltpu.make_async_copy(y_ref.at[z], y_out.at[z], loc_sem.at[0])
    y_loc.start()
    for s in range(1, n_z):
        rows_copy(y_ref, y_out, y_send, y_recv, s).start()
    for fn, it in plan[-1]:
        fn(it)
    for c in kv:
        c.wait()

    diag_ref[...] = jnp.zeros_like(diag_ref)
    lane = lax.broadcasted_iota(jnp.int32, (rows, 128), 1)
    kb_rows = 256
    nsub = kb_rows // 128

    @pl.loop(0, heads)
    def _(h):
        par = lax.rem(h, 2)
        cols = pl.ds(pl.multiple_of((h // 2) * 128, 128), 128)
        sel = lane // 64 == par
        spare = lane % 64 - nblk
        strip = skewed(bias_ref[pl.ds(2 * (width // 32) + h, 1)])
        qa = qa_ref[h]
        ka = jnp.where(sel, k_ref[:, cols], exk_ref[...])
        ones = jnp.where((spare >= 0) & (spare < 3), 1.0, 0.0).astype(BF)
        va = jnp.where(sel, v_ref[:, cols], ones)
        prod = do_ref[:, cols].astype(F32) * o_ref[:, cols].astype(F32)
        delta = -jnp.sum(jnp.where(sel, prod, 0.0), axis=1, keepdims=True)
        hi_ = delta.astype(BF)
        rest = delta - hi_.astype(F32)
        mid = rest.astype(BF)
        low = (rest - mid.astype(F32)).astype(BF)
        extra = jnp.where(spare == 0, hi_, jnp.where(spare == 1, mid, jnp.where(spare == 2, low, jnp.zeros((rows, 128), BF))))
        doa = jnp.where(sel, do_ref[:, cols], extra)
        near = jnp.zeros((128, 384), F32)
        for kb in range(rows // kb_rows):
            r0 = kb * kb_rows
            kab = ka[r0:r0 + kb_rows]
            s = mm(kab, qa, ((1,), (1,)))
            dp_ = mm(va[r0:r0 + kb_rows], doa, ((1,), (1,)))
            prow, dsrow = [], []
            for sub in range(nsub):
                J = kb * nsub + sub
                lo = max(J - 1, 0)
                hi = min(J + 1, nblk - 1)
                srow = s[sub * 128:(sub + 1) * 128]
                parts = []
                if lo > 0:
                    parts.append(srow[:, :lo * 128])
                parts.append(srow[:, lo * 128:(hi + 1) * 128] + strip[:, (lo - J + 1) * 128:(hi - J + 2) * 128])
                if hi < nblk - 1:
                    parts.append(srow[:, (hi + 1) * 128:])
                p = jnp.exp2(jnp.concatenate(parts, axis=1) * LOG2E)
                ds = p * dp_[sub * 128:(sub + 1) * 128]
                nr = ds[:, lo * 128:(hi + 1) * 128]
                if lo > J - 1:
                    nr = jnp.concatenate([jnp.zeros((128, 128), F32), nr], axis=1)
                if hi < J + 1:
                    nr = jnp.concatenate([nr, jnp.zeros((128, 128), F32)], axis=1)
                near = near + nr
                prow.append(p.astype(BF))
                dsrow.append(ds.astype(BF))
            pb = jnp.concatenate(prow, axis=0)
            dsb = jnp.concatenate(dsrow, axis=0)
            at = pl.ds(r0, kb_rows)
            dv_ref[at, cols] = jnp.where(sel[:kb_rows], mm(pb, doa).astype(BF), dv_ref[at, cols])
            dk_ref[at, cols] = jnp.where(sel[:kb_rows], mm(dsb, qa).astype(BF), dk_ref[at, cols])
            dqt = mm(kab, dsb, ((0,), (0,)))
            dqt_ref[...] = dqt if kb == 0 else dqt_ref[...] + dqt
        far = dqt_ref[pl.ds(pl.multiple_of(64 - 64 * par, 64), 8)]
        key_block = lax.broadcasted_iota(jnp.int32, far.shape, 0)
        query_block = lax.broadcasted_iota(jnp.int32, far.shape, 1) // 128
        left = jnp.sum(jnp.where(key_block <= query_block - 2, far, 0.0))
        right = jnp.sum(jnp.where(key_block >= query_block + 2, far, 0.0))
        column = lax.broadcasted_iota(jnp.int32, (1, 512), 1)
        diag_ref[pl.ds(h, 1)] = diagonal_sums(near) + jnp.where(column == 383, left, 0.0) + jnp.where(column == 385, right, 0.0)
        dq_ref[pl.ds(pl.multiple_of(h * 64, 64), 64)] = dqt_ref[pl.ds(pl.multiple_of(64 * par, 64), 64)].astype(BF)
        for k in range(heads):
            if k in plan:
                @pl.when(h == k)
                def _():
                    for fn, it in plan[k]:
                        fn(it)

    half = rows // n_z
    dgain = jnp.zeros((1, width), F32)

    def scaled(r):
        x = x_ref[r].astype(F32)
        return x, lax.rsqrt(jnp.mean(x * x, axis=-1, keepdims=True) + EPS)

    gx_loc = pltpu.make_async_copy(gx.at[z], gx_out.at[z], loc_sem.at[1])
    for r in range(n_z):
        at = pl.ds(r * half, half)
        x, scale = scaled(r)
        ht_ref[:, at] = (x * scale * gain_ref[0:1]).astype(BF).T
        dh = mm(dq_ref[:, at], w_ref[:, :width], ((0,), (1,)))
        dh += mm(dk_ref[at], w_ref[:, width:2 * width], ((1,), (1,)))
        dh += mm(dv_ref[at], w_ref[:, 2 * width:], ((1,), (1,)))
        dgain += jnp.sum(dh * (x * scale), axis=0, keepdims=True)
        u = dh * gain_ref[0:1]
        inner = jnp.mean(u * x, axis=-1, keepdims=True)
        gx[r] = (gm_ref[at] + scale * u - x * (scale * scale * scale * inner)).astype(BF)
    for it in X1_BEFORE:
        stage_x1(it)
    for s in range(1, n_z):
        rows_copy(gx, gx_out, t_send, t_recv, s).start()
    for it in X1_AFTER:
        stage_x1(it)
    gx_loc.start()
    for i in range(3):
        w0 = i * width
        if i == 0:
            dw = mm(ht_ref[...], dq_ref[...], ((1,), (1,)))
        else:
            dw = mm(ht_ref[...], (dk_ref, dv_ref)[i - 1][...])
        dw = dw.astype(BF)
        for d in range(8):
            p_qkv[d, :, w0:w0 + width] = dw[d * 96:(d + 1) * 96]
        if i == 1:
            core_start(6)
            for it in X1_BEFORE:
                stage_z1(it)
    core_start(7)
    stage_core(6)
    stage_core(7)
    n_dev = 32
    own = width // n_dev
    place = lax.broadcasted_iota(jnp.int32, (n_dev, width), 1)
    mine = place // own == lax.broadcasted_iota(jnp.int32, (n_dev, width), 0)
    col = lax.broadcasted_iota(jnp.int32, (width, 128), 1)
    row = lax.broadcasted_iota(jnp.int32, (width, 128), 0) % own
    small = jnp.zeros((n_dev, 128), F32)
    for i, g in enumerate((dgain, gain2_ref[...])):
        small += exact(jnp.where(mine, g, 0.0), (col == row + i * own).astype(F32), ((1,), (0,)))
    m = lax.broadcasted_iota(jnp.int32, (n_dev, 512), 1)
    hot = bucket_of(128 - m + jnp.where(m >= 384, 512, 0)) == lax.broadcasted_iota(jnp.int32, (n_dev, 512), 0)
    sums = exact(hot.astype(F32), diag_ref[...], ((1,), (1,)))
    col = lax.broadcasted_iota(jnp.int32, (16, 128), 1)
    row = lax.broadcasted_iota(jnp.int32, (16, 128), 0)
    small += exact(sums, ((col == row + 2 * own) & (row < heads)).astype(F32), ((1,), (0,)))
    for d in range(8):
        p_small[d] = small[d * n_z:(d + 1) * n_z]
    core_start(8)
    stage_core(8)
    for fn, its in (
        (stage_z1, X1_AFTER),
        (stage_z2, X1_BEFORE),
        (stage_x2, (6, 7, 8)),
        (stage_z2, X1_AFTER),
        (stage_x1, (6, 7, 8)),
        (stage_z1, (6, 7, 8)),
        (stage_z2, (6, 7, 8)),
        (stage_end, range(n_it)),
    ):
        for it in its:
            fn(it)
    for s in range(1, n_z):
        rows_wait(y_out, y_send, y_recv, s)
        rows_wait(gx_out, t_send, t_recv, s)
    y_loc.wait()
    gx_loc.wait()
    for s in range(1, n_z):
        rows_copy(y_ref, y_out, y_send, y_recv, s).wait_send()
        rows_copy(gx, gx_out, t_send, t_recv, s).wait_send()
    for it in range(n_it):
        for q in range(4):
            c_copy(it, q).wait_send()
        for f1 in (True, False):
            x2_copy(it, f1).wait_send()
        x1_copy(it).wait_send()
        for j in range(n_z):
            for way in (0, 1):
                @pl.when(j > z if way == 0 else j < z)
                def _():
                    z_copy(it, way, j).wait_send()


X1_BEFORE = ()
X1_AFTER = (4, 5, 2, 3)


def exact(a, b, dims):
    return lax.dot_general(a, b, (dims, ((), ())), preferred_element_type=F32, precision=lax.Precision.HIGHEST)


def backward(qa, qkv, do, o, exk, bias, x, gm, gain, dgain2, w, y, g_out, g_in, g_back, chunks, n_early, collective_id=1):
    width = x.shape[2]
    rows = x.shape[0] * x.shape[1]
    n_it = len(chunks)
    D = pltpu.SemaphoreType.DMA
    S = jax.ShapeDtypeStruct
    parts = (S((8, 96, 3 * width), BF), S((8, 4, 128), F32), g_out, g_in, g_back)

    def V(c, *lead):
        p = parts[c[0]]
        return pltpu.VMEM((*lead, p.shape[1], c[2]), p.dtype)

    def zs(c):
        p = parts[c[0]]
        return pltpu.VMEM((4, p.shape[1] // 4, c[2]), p.dtype)

    vm = pl.BlockSpec(memory_space=pltpu.VMEM)
    hbm = pl.BlockSpec(memory_space=pltpu.HBM)
    scratch = [pltpu.VMEM((rows, width), BF), pltpu.VMEM((rows, width), BF), pltpu.VMEM(parts[0].shape, BF), pltpu.VMEM((8, 4, 128), F32), pltpu.VMEM((4, rows // 4, width), BF),
               pltpu.VMEM((width, rows), BF), pltpu.VMEM((128, rows), F32), pltpu.VMEM((width, rows), BF),
               pltpu.VMEM((rows, width), BF), pltpu.VMEM((rows, width), BF), pltpu.VMEM((16, 512), F32)]
    scratch += [V(c, 4) for c in chunks] + [V(c, 2) for c in chunks] + [V(c) for c in chunks] + [zs(c) for c in chunks] * 3
    scratch += [V(c, 4) for c in chunks[:n_early]]
    scratch += [D((4,)), D((n_early, 4)), D((3,)), D((3,)), D((3,)), D((3,)), D((n_it, 4)), D((n_it, 4)), D((n_it, 2)), D((n_it, 2)),
                D((n_it,)), D((n_it,)), D((n_it, 2, 4)), D((n_it, 2, 4))]
    return pl.pallas_call(
        functools.partial(back_kernel, chunks, n_early),
        out_shape=[S((4, rows // 4, width), BF)] * 2 + [S((p.shape[1] // 4, p.shape[2]), F32) for p in parts],
        in_specs=[vm, hbm] + [vm] * 9 + [hbm] * 4,
        out_specs=[hbm] * 2 + [vm] * 5,
        scratch_shapes=scratch,
        compiler_params=pltpu.CompilerParams(collective_id=collective_id, has_side_effects=True, vmem_limit_bytes=63 << 20),
    )(qa, qkv, do, o, exk, bias, x, gm, gain, dgain2, w, y, g_out, g_in, g_back)


def fits(mesh):
    return mesh.shape["dp"] == 8 and mesh.shape["seq"] == 4


ITEMS = ((0, 4, 2), (4, 2, 4), (1, 2, 4), (2, 4, 2), (3, 2, 4))
ROUTES = (
    (3, 0, 1536, 4, 2),
    (3, 1536, 1536, 2, 4),
    (4, 0, 384, 4, 2),
    (4, 384, 384, 2, 4),
    (2, 0, 384, 4, 2),
    (2, 384, 384, 2, 4),
    (0, 0, 1152, 4, 2),
    (0, 1152, 1152, 2, 4),
    (1, 0, 128, 2, 4),
)
EARLY = 6


def fast_shards(
    tokens,
    segment_ids,
    valid_mask,
    cotangent,
    gain_one,
    gain_two,
    bias_table,
    qkv_weight,
    out_weight,
    in_weight,
    back_weight,
):
    n_z = lax.axis_size("seq")
    seq_count, block_len, width = tokens.shape
    seq_len = n_z * block_len
    g_rows, t_rows = gain_one.shape[0], bias_table.shape[0]
    small = jnp.concatenate([gain_one, gain_two, bias_table]).astype(F32)
    small = jnp.pad(small[None], ((0, 7), (0, 128 - small.shape[0])))
    x4, g4, out_full, in_full, back_full, qkv_full, projected, mixed, q_aug, exk, gains, bias_back = forward(
        tokens,
        cotangent * valid_mask[..., None].astype(BF),
        segment_ids.reshape(seq_count, 1, block_len),
        (qkv_weight, out_weight, in_weight, back_weight, small),
        ITEMS,
    )
    x = x4.reshape(seq_len, width)
    g_low = g4.reshape(seq_len, width)
    out_full = out_full.reshape(width, width)
    in_full = in_full.reshape(width, -1)
    back_full = back_full.reshape(-1, width)
    result, grad_middle, grad_mixed, grad_out, grad_in, grad_back, grad_gain_second = ffn(
        x, mixed, g_low, gains, out_full, in_full, back_full
    )
    grad_tokens, output, own_qkv, own_small, own_out, own_in, own_back = backward(
        q_aug,
        projected,
        grad_mixed,
        mixed,
        exk,
        bias_back,
        x4,
        grad_middle,
        gains,
        grad_gain_second,
        qkv_full,
        result.reshape(n_z, block_len, width),
        grad_out.reshape(8, -1, width),
        grad_in.reshape(8, -1, in_full.shape[1]),
        grad_back.reshape(8, -1, width),
        ROUTES,
        EARLY,
    )
    own_small = own_small[0]
    return (
        output,
        grad_tokens,
        own_small[:g_rows],
        own_small[g_rows : 2 * g_rows],
        own_small[2 * g_rows : 2 * g_rows + t_rows],
        own_qkv,
        own_out,
        own_in,
        own_back,
    )


def solution(mesh):
    in_specs = (
        P("dp", "seq", None),
        P("dp", "seq"),
        P("dp", "seq"),
        P("dp", "seq", None),
        P(("dp", "seq")),
        P(("dp", "seq")),
        P(("dp", "seq")),
        P(("dp", "seq"), None),
        P(("dp", "seq"), None),
        P(("dp", "seq"), None),
        P(("dp", "seq"), None),
    )
    out_specs = (
        P("dp", "seq", None),
        P("dp", "seq", None),
        P(("dp", "seq")),
        P(("dp", "seq")),
        P(("dp", "seq")),
        P(("dp", "seq"), None),
        P(("dp", "seq"), None),
        P(("dp", "seq"), None),
        P(("dp", "seq"), None),
    )
    return jax.shard_map(fast_shards if fits(mesh) else general_shards, mesh=mesh, in_specs=in_specs, out_specs=out_specs, check_vma=False)
```
